32 devices in a mesh: grp: 16 (over z, x, core), ep: 2 (over y).
Axes of the slice: x: 2, y: 2, z: 4, core: 2. Of those that a mesh axis runs over, the one named last changes fastest.
Arguments:
- inputs: bfloat16 [8192, 1024], P(('grp', 'ep')), may hold values from -8 to 8
- attn_gain: bfloat16 [1024], P(('grp', 'ep')), may hold values from 0.099609375 to 1.8984375
- w_query: bfloat16 [1024, 1024], P(('grp', 'ep')), may hold values from -0.1875 to 0.1875
- w_key: bfloat16 [1024, 1024], P(('grp', 'ep')), may hold values from -0.1875 to 0.1875
- w_value: bfloat16 [1024, 1024], P(('grp', 'ep')), may hold values from -0.25 to 0.25
- w_output: bfloat16 [1024, 1024], P(('grp', 'ep')), may hold values from -3 to 3
- centroids: bfloat16 [1024, 2], P(('grp', 'ep')), may hold values from -0.09375 to 0.09375
- norm1_gain: bfloat16 [2, 1024], P('ep'), may hold values from 0.099609375 to 1.8984375
- norm2_gain: bfloat16 [2, 1024], P('ep'), may hold values from 0.099609375 to 1.8984375
- up_first: bfloat16 [2, 1024, 4096], P('ep'), may hold values from -0.1875 to 0.1875
- down_first: bfloat16 [2, 4096, 1024], P('ep'), may hold values from -0.09375 to 0.09375
- up_second: bfloat16 [2, 1024, 4096], P('ep'), may hold values from -0.1875 to 0.1875
- down_second: bfloat16 [2, 4096, 1024], P('ep'), may hold values from -0.09375 to 0.09375
- routes: int32 [8192, 1], P(('grp', 'ep')), may hold values from 0 to 1; in each aligned block of 256 rows (0 to 255, 256 to 511, ...) at most 256 rows name the same one
- prefix: int32 [32], P(('grp', 'ep')), may hold values from 25 to 128
- cotangent: bfloat16 [8192, 1024], P(('grp', 'ep')), may hold values from -6 to 6
Outputs:
- output: bfloat16 [8192, 1024], P(('grp', 'ep'))
- input_grad: float32 [8192, 1024], P(('grp', 'ep'))
- attn_gain_grad: float32 [1024], P(('grp', 'ep'))
- query_grad: float32 [1024, 1024], P(('grp', 'ep'))
- key_grad: float32 [1024, 1024], P(('grp', 'ep'))
- value_grad: float32 [1024, 1024], P(('grp', 'ep'))
- out_proj_grad: float32 [1024, 1024], P(('grp', 'ep'))
- centroid_grad: float32 [1024, 2], P(('grp', 'ep'))
- norm1_grad: float32 [2, 1024], P('ep', 'grp')
- norm2_grad: float32 [2, 1024], P('ep', 'grp')
- up_first_grad: float32 [2, 1024, 4096], P('ep', None, 'grp')
- down_first_grad: float32 [2, 4096, 1024], P('ep', 'grp')
- up_second_grad: float32 [2, 1024, 4096], P('ep', None, 'grp')
- down_second_grad: float32 [2, 4096, 1024], P('ep', 'grp')
- rms_values: float32 [4], replicated
The draws below stay inside these ranges and needn't reach their ends.
Inputs may be any that keep to these rules, and one draw needn't show every extreme that they name: `routes`: in the rows of one sequence no expert is named by more than 256 rows; in some sequence one expert is named by exactly 256.
All inputs are finite; a program needn't handle non-finite values.
Results may differ from the reference program's by a relative error of at most 0.012.
The reference program's roundings to bfloat16 on the way count: a program that leaves them out, or rounds other values in their place, can miss the bound.
Values may be sent and summed in bfloat16 or wider, within the bound.
A program may use at most 256 MiB of HBM per device.

```python
import math
import jax
import jax.numpy as jnp
import numpy as np
from jax import lax

D = 1024
HEADS = 16
FF = 4096
TOK_DEV = 256
HEAD_DIM = 64
SEQS = 32
TOKENS = 8192
EXPERTS = 2
CAP = 256


def draw_inputs(key, part):
    row_pos = jnp.arange(TOKENS, dtype=jnp.float32) / TOKENS
    base = jnp.clip(jax.random.normal(key, (TOKENS, D), jnp.float32), -2.6, 2.6)
    row_scale = 0.3 + 2.7 * row_pos
    return (base * row_scale[:, None]).astype(jnp.bfloat16)


def draw_w_value(key, part):
    base_key = jax.random.fold_in(key, 11)
    column_key = jax.random.fold_in(key, 23)
    base = jnp.clip(jax.random.normal(base_key, (D, D), jnp.float32), -4.0, 4.0)
    column = jnp.clip(jax.random.normal(column_key, (1, D), jnp.float32), -4.0, 4.0)
    return ((base + column) * D ** (-0.5)).astype(jnp.bfloat16)


def plant(drawn, key, least, top_value):
    longest = drawn.shape.index(max(drawn.shape))
    spots = []
    for shift in (0, 1):
        where = [jax.random.randint(jax.random.fold_in(key, axis), (), 0, length) for axis, length in enumerate(drawn.shape)]
        where[longest] = (where[longest] + shift) % drawn.shape[longest]
        spots.append(tuple(where))
    return drawn.at[spots[0]].set(least).at[spots[1]].set(top_value)


def steps_of(rng, shape, shards, smallest, top_value):
    level = 1.0
    for axis_at, shards_of in shards:
        draws = jax.random.uniform(jax.random.fold_in(jax.random.fold_in(rng, 6), axis_at), (shards_of,), jnp.float32, smallest / len(shards), top_value / len(shards))
        level = level * jnp.repeat(jnp.exp(draws), shape[axis_at] // shards_of).reshape((-1,) + (1,) * (len(shape) - 1 - axis_at))
    return level


def shared_out(key, own, number, rows, amount, top, limit, lean):
    ranking = jax.random.permutation(key, amount)
    packed, usual = load_shares(amount, rows * top, limit, lean, True), load_shares(amount, rows * top, limit, lean, False)
    places = jnp.arange(amount)

    def named(lengths, offset_by):
        used = int((lengths > 0).sum())
        fixed = max(1, used // 4)
        passed = fixed + (places - fixed + offset_by * (used - fixed)) % max(1, amount - fixed)
        return jnp.zeros((amount,), jnp.int32).at[ranking[jnp.where(places < fixed, places, passed)]].set(jnp.asarray(lengths, jnp.int32))

    lengths = jnp.where(number % 4 == 0, named(packed, number // 4), named(usual, number - number // 4 - 1))
    mixed = jax.random.permutation(jax.random.fold_in(own, 3), amount)
    giver, receiver = mixed[0:amount // 2 * 2:2], mixed[1:amount // 2 * 2:2]
    room = jnp.minimum(lengths[giver] - 1, limit - lengths[receiver]) // 2
    room = jnp.where((giver == ranking[0]) | (receiver == ranking[0]) | (lengths[receiver] == 0), 0, jnp.maximum(room, 0))
    passed = jax.random.randint(jax.random.fold_in(own, 4), (amount // 2,), 0, 1 << 20) % (room + 1)
    lengths = lengths.at[giver].add(-passed).at[receiver].add(passed)
    members = jnp.searchsorted(jnp.cumsum(lengths), jnp.arange(rows * top), side="right").astype(jnp.int32)
    grid = members.reshape(top, rows).T
    grid = grid[jax.random.permutation(jax.random.fold_in(own, 1), rows)]
    offset_by = jax.random.randint(jax.random.fold_in(own, 2), (rows, 1), 0, top)
    return jnp.take_along_axis(grid, (jnp.arange(top)[None, :] + offset_by) % top, axis=1)


def load_shares(amount, total, bound, lean, full):
    loads = [(1 << 20) // math.isqrt(rank ** lean) + 1 for rank in range(1, amount + 1)]
    largest = bound if full else min(bound, max(-(-total // amount), total * loads[0] // sum(loads)))
    least = 1 if total - largest >= amount - 1 else 0
    holding, rest = [largest] + [least] * (amount - 1), total - largest - least * (amount - 1)
    while rest > 0:
        candidates = [i for i in range(1, amount) if holding[i] < largest] or [i for i in range(1, amount) if holding[i] < bound]
        whole, left = sum([loads[i] for i in candidates]), rest
        for i in candidates:
            extra = min(bound - holding[i], max(1, left * loads[i] // whole), rest)
            holding[i] = holding[i] + extra
            rest = rest - extra
    return np.array(holding)


def centred(key, dims, deviation, most, split=(), kind=jnp.bfloat16):
    drawn = deviation * jax.random.normal(key, dims, jnp.float32)
    if split:
        drawn = drawn * steps_of(key, dims, split, -0.22, 0.18)
    return jnp.clip(drawn, -most, most).astype(kind)


def setup_inputs(seed: int = 0) -> dict:
    splits = jax.random.split(jax.random.key(seed), 17)
    inputs = draw_inputs(jax.random.fold_in(splits[16], 71), 0)
    attn_gain = jnp.clip(1.0 + 0.18 * jax.random.normal(splits[1], (D,), jnp.float32), 0.099609375, 1.8984375).astype(jnp.bfloat16)
    w_query = centred(splits[2], (D, D), D ** -0.5, 0.1875, ((0, 32),))
    w_key = centred(splits[3], (D, D), D ** -0.5, 0.1875, ((0, 32),))
    w_value = draw_w_value(jax.random.fold_in(splits[16], 71), 0)
    w_output = centred(splits[5], (D, D), (max(2, D // 256)) ** -0.5, 3.0, ((0, 32),))
    centroids = centred(splits[6], (D, EXPERTS), (4 * D) ** -0.5, 0.09375, ((0, 32),))
    norm1_gain = jnp.clip(1.0 + 0.18 * jax.random.normal(splits[7], (EXPERTS, D), jnp.float32), 0.099609375, 1.8984375).astype(jnp.bfloat16)
    norm2_gain = jnp.clip(1.0 + 0.18 * jax.random.normal(splits[8], (EXPERTS, D), jnp.float32), 0.099609375, 1.8984375).astype(jnp.bfloat16)
    up_first = centred(splits[9], (EXPERTS, D, FF), D ** -0.5, 0.1875, ((0, 2),))
    down_first = centred(splits[10], (EXPERTS, FF, D), FF ** -0.5, 0.09375, ((0, 2),))
    up_second = centred(splits[11], (EXPERTS, D, FF), D ** -0.5, 0.1875, ((0, 2),))
    down_second = centred(splits[12], (EXPERTS, FF, D), FF ** -0.5, 0.09375, ((0, 2),))
    routes_keys = jax.random.split(jax.random.fold_in(splits[13], 1), TOKENS // TOK_DEV)
    routes_turns = jax.random.permutation(jax.random.fold_in(splits[13], 3), TOKENS // TOK_DEV)
    routes = jax.vmap(lambda own, number: shared_out(jax.random.fold_in(splits[13], 2), own, number, TOK_DEV, EXPERTS, 1, CAP, 1))(routes_keys, routes_turns).reshape((TOKENS, 1))
    prefix = plant(jax.random.randint(splits[14], (SEQS,), max(1, TOK_DEV // 10), TOK_DEV // 2 + 1), jax.random.fold_in(splits[14], 1), max(1, TOK_DEV // 10), (TOK_DEV // 2 + 1) - 1).astype(jnp.int32)
    cotangent = centred(splits[15], (TOKENS, D), 1.0, 6.0, ((0, 32),))
    return {"inputs": inputs, "attn_gain": attn_gain, "w_query": w_query, "w_key": w_key, "w_value": w_value, "w_output": w_output, "centroids": centroids, "norm1_gain": norm1_gain, "norm2_gain": norm2_gain, "up_first": up_first, "down_first": down_first, "up_second": up_second, "down_second": down_second, "routes": routes, "prefix": prefix, "cotangent": cotangent}


@jax.custom_vjp
def low(v):
    return lax.optimization_barrier(v.astype(jnp.bfloat16)).astype(jnp.float32)

@jax.custom_vjp
def low_back(v):
    return v

def low_keep(v):
    return (low(v), None)

def low_pass(kept, grad):
    return (grad,)

def back_keep(v):
    return (v, None)

def back_low(kept, grad):
    return (low(grad),)
low.defvjp(low_keep, low_pass)
low_back.defvjp(back_keep, back_low)
EPSILON = 1e-05
HIGH = lax.Precision.HIGHEST

def precise_dot(left_side, right_side):
    return jnp.dot(left_side, right_side, precision=HIGH, preferred_element_type=jnp.float32)

def layer_norm(rows_in, gain_row):
    center = rows_in - lax.optimization_barrier(jnp.mean(rows_in, axis=-1, keepdims=True))
    spread = lax.optimization_barrier(jnp.mean(center * center, axis=-1, keepdims=True))
    return center * lax.rsqrt(spread + EPSILON) * gain_row

def attend(seq_rows, prefix_len, gain_attn, query_mat, key_mat, value_mat, output_mat):
    normed = low(layer_norm(seq_rows, gain_attn))
    queries = low(low_back(precise_dot(normed, query_mat))).reshape(TOK_DEV, HEADS, HEAD_DIM)
    key_heads = low(low_back(precise_dot(normed, key_mat))).reshape(TOK_DEV, HEADS, HEAD_DIM)
    value_heads = low(low_back(precise_dot(normed, value_mat))).reshape(TOK_DEV, HEADS, HEAD_DIM)
    scores = low_back(jnp.einsum('qhd,khd->hqk', queries, key_heads, precision=HIGH) * HEAD_DIM ** (-0.5))
    row_ids = jnp.arange(TOK_DEV, dtype=jnp.int32)[:, None]
    col_ids = jnp.arange(TOK_DEV, dtype=jnp.int32)[None, :]
    visible = (col_ids <= row_ids) | (col_ids < prefix_len)
    softmax_out = low(jax.nn.softmax(jnp.where(visible[None], scores, -1e+30), axis=-1))
    context = jnp.einsum('hqk,khd->qhd', softmax_out, value_heads, precision=HIGH).reshape(TOK_DEV, D)
    context = low(low_back(context))
    return low_back(precise_dot(context, output_mat))

def gelu_exact(preact):
    return jax.nn.gelu(preact, approximate=False)

def expert_delta(rows_in, gain_one, gain_two, up_first, down_first, up_second, down_second):
    normed_one = low(layer_norm(rows_in, gain_one))
    act_one = low(gelu_exact(low_back(precise_dot(normed_one, up_first))))
    sub_one = low_back(precise_dot(act_one, down_first))
    middle = rows_in + sub_one
    normed_two = low(layer_norm(middle, gain_two))
    act_two = low(gelu_exact(low_back(precise_dot(normed_two, up_second))))
    sub_two = precise_dot(act_two, down_second)
    delta = low(low_back(sub_one + sub_two))
    return (delta, jnp.sum(sub_one * sub_one), jnp.sum(sub_two * sub_two))

def reference(inputs, attn_gain, w_query, w_key, w_value, w_output, centroids, norm1_gain, norm2_gain, up_first, down_first, up_second, down_second, routes, prefix, cotangent):
    floats = tuple((array_in.astype(jnp.float32) for array_in in (inputs, attn_gain, w_query, w_key, w_value, w_output, centroids, norm1_gain, norm2_gain, up_first, down_first, up_second, down_second)))
    route_ids = routes[:, 0].astype(jnp.int32)
    expert_ids = jnp.arange(EXPERTS, dtype=jnp.int32)
    route_hot = (route_ids[:, None] == expert_ids[None, :]).astype(jnp.int32)
    route_weight = route_hot.astype(jnp.float32)
    hot_blocks = route_hot.reshape(SEQS, TOK_DEV, EXPERTS)
    position = lax.optimization_barrier(jnp.sum((jnp.cumsum(hot_blocks, axis=1).astype(jnp.int32) - 1) * hot_blocks, axis=-1)).astype(jnp.int32)
    target = (route_ids.reshape(SEQS, TOK_DEV) * CAP + position).astype(jnp.int32)
    block_ids = jnp.arange(SEQS, dtype=jnp.int32)[:, None]

    def forward(inputs_f, gain_attn, query_mat, key_mat, value_mat, output_mat, centroid_mat, gain_one, gain_two, up_one_mat, down_one_mat, up_two_mat, down_two_mat):

        def attend_one(seq_pair):
            return attend(seq_pair[0], seq_pair[1], gain_attn, query_mat, key_mat, value_mat, output_mat)
        branch = lax.map(jax.checkpoint(attend_one), (inputs_f.reshape(SEQS, TOK_DEV, D), prefix)).reshape(TOKENS, D)
        hidden = inputs_f + branch
        hidden_low = low(hidden)
        all_scores = precise_dot(hidden_low, centroid_mat)
        gate_value = jax.nn.sigmoid(lax.optimization_barrier(jnp.sum(all_scores * route_weight, axis=1)))
        sent_rows = low_back(hidden_low).reshape(SEQS, TOK_DEV, D)
        slot_rows = jnp.zeros((SEQS, EXPERTS * CAP, D), jnp.float32).at[block_ids, target].set(sent_rows)
        per_expert = slot_rows.reshape(SEQS, EXPERTS, CAP, D).transpose(1, 0, 2, 3)

        def run_expert(expert_pack):
            rows_all, one_gain, two_gain, up_one, down_one, up_two, down_two = expert_pack

            def one_block(block_rows):
                return expert_delta(block_rows, one_gain, two_gain, up_one, down_one, up_two, down_two)
            return lax.map(jax.checkpoint(one_block), rows_all)
        deltas, sums_one, sums_two = lax.map(run_expert, (per_expert, gain_one, gain_two, up_one_mat, down_one_mat, up_two_mat, down_two_mat))
        back_slots = deltas.transpose(1, 0, 2, 3).reshape(SEQS, EXPERTS * CAP, D)
        returned = back_slots[block_ids, target].reshape(TOKENS, D)
        result = hidden + gate_value[:, None] * returned
        cell_count = TOKENS * D
        statistics = jnp.sqrt(jnp.stack([jnp.sum(result * result), jnp.sum(branch * branch), jnp.sum(sums_one), jnp.sum(sums_two)]) / cell_count)
        return (result, statistics)
    result, pullback, statistics = jax.vjp(forward, *floats, has_aux=True)
    gradients = pullback(cotangent.astype(jnp.float32))
    return (result.astype(jnp.bfloat16), gradients[0], gradients[1], gradients[2], gradients[3], gradients[4], gradients[5], gradients[6], gradients[7], gradients[8], gradients[9], gradients[10], gradients[11], gradients[12], statistics)
```

```python
import functools

import jax
import jax.numpy as jnp
from jax import lax
from jax.experimental import pallas as pl
from jax.experimental.pallas import tpu as pltpu
from jax.sharding import PartitionSpec as P

HEADS = 16


EPSILON = 1e-05
SQRT_HALF = 0.7071067811865476
INV_ROOT_TWO_PI = 0.3989422804014327
HIGH = lax.Precision.HIGHEST
HALF_LOG2E = -0.7213475204444817
ERF_P = 0.3275911 * SQRT_HALF
ERF_A1 = 0.5 * 0.254829592
ERF_A2 = 0.5 * -0.284496736
ERF_A3 = 0.5 * 1.421413741
ERF_A4 = 0.5 * -1.453152027
ERF_A5 = 0.5 * 1.061405429


def norm_parts(rows_in):
    center = rows_in - jnp.mean(rows_in, axis=-1, keepdims=True)
    inverse = lax.rsqrt(jnp.mean(center * center, axis=-1, keepdims=True) + EPSILON)
    return (center * inverse, inverse)


def norm_back(grad_normed, normed, inverse):
    mean_grad = jnp.mean(grad_normed, axis=-1, keepdims=True)
    mean_dot = jnp.mean(grad_normed * normed, axis=-1, keepdims=True)
    return inverse * (grad_normed - mean_grad - normed * mean_dot)


def gelu_slope(preact):
    return (
        0.5 * (1.0 + jax.scipy.special.erf(preact * SQRT_HALF))
        + preact * jnp.exp(-0.5 * preact * preact) * INV_ROOT_TWO_PI
    )


def matmul(left_side, right_side):
    return jnp.dot(left_side, right_side, preferred_element_type=jnp.float32)


def dot_first(left_side, right_side):
    return lax.dot_general(
        left_side, right_side, (((0,), (0,)), ((), ())), preferred_element_type=jnp.float32
    )


def dot_last(left_side, right_side):
    return lax.dot_general(
        left_side, right_side, (((1,), (1,)), ((), ())), preferred_element_type=jnp.float32
    )


def visible_mask(row_start, row_count, key_count, prefix_len):
    row_ids = row_start + jnp.arange(row_count, dtype=jnp.int32)[:, None]
    col_ids = jnp.arange(key_count, dtype=jnp.int32)[None, :]
    return (col_ids <= row_ids) | (col_ids < prefix_len)


def fill_slots(rows_in, target, slot_total):
    return jnp.zeros((slot_total, rows_in.shape[1]), rows_in.dtype).at[target].set(rows_in)


MESH = pl.DeviceIdType.MESH
VMEM_CAP = 66 * 1000 * 1000


def place(zs):
    grp = lax.axis_index("grp")
    ep = lax.axis_index("ep")
    core = lax.rem(grp, 2)
    x = lax.rem(lax.div(grp, 2), 2)
    z = lax.div(grp, 4)
    return z, x, core, ep


def device(z, x, core, ep):
    return ((z * 2 + x) * 2 + core, ep)


def greet(peers):
    barrier = pltpu.get_barrier_semaphore()
    for peer in peers:
        pl.semaphore_signal(barrier, inc=1, device_id=peer, device_id_type=MESH)
    pl.semaphore_wait(barrier, len(peers))


def push(src, dst, send_sem, recv_sem, peer):
    return pltpu.make_async_remote_copy(
        src_ref=src, dst_ref=dst, send_sem=send_sem, recv_sem=recv_sem, device_id=peer, device_id_type=MESH
    )


def gather_kernel(zs, *refs):
    shard = refs[0:5]
    full = refs[5:10]
    own_sem, z_send, z_recv, p_send, p_recv, c_send, c_recv = refs[10:]
    z, x, core, ep = place(zs)
    right = device(jnp.minimum(z + 1, zs - 1), x, core, ep)
    left = device(jnp.maximum(z - 1, 0), x, core, ep)
    x_peer = device(z, 1 - x, core, ep)
    y_peer = device(z, x, core, 1 - ep)
    c_peer = device(z, x, 1 - core, ep)
    others = [device(lax.rem(z + k, zs), x, core, ep) for k in range(1, zs)]
    half = shard[0].shape[1] // 2
    items = []
    for w in range(4):
        items.append((w, slice(0, half), True))
        items.append((w, slice(half, 2 * half), False))
    items.append((4, slice(0, shard[4].shape[1]), True))
    count = len(items)

    def own(i):
        w, cols, _ = items[i]
        return pltpu.make_async_copy(shard[w].at[:, cols], full[w].at[z, x, core, ep, :, cols], own_sem.at[i])

    def z_copy(i, src, slot, way, hop, peer):
        w, cols, _ = items[i]
        return push(src, full[w].at[slot, x, core, ep, :, cols], z_send.at[i, way, hop], z_recv.at[i, way, hop], peer)

    def z_start(i):
        w, cols, _ = items[i]

        @pl.when(z < zs - 1)
        def _():
            z_copy(i, shard[w].at[:, cols], z, 0, 0, right).start()

        @pl.when(z > 0)
        def _():
            z_copy(i, shard[w].at[:, cols], z, 1, 0, left).start()

    def z_hop(i, hop):
        w, cols, _ = items[i]
        low = jnp.maximum(z - hop, 0)
        high = jnp.minimum(z + hop, zs - 1)
        from_left = full[w].at[low, x, core, ep, :, cols]
        from_right = full[w].at[high, x, core, ep, :, cols]

        @pl.when(z >= hop)
        def _():
            z_copy(i, from_left, low, 0, hop - 1, right).wait_recv()

        if hop < zs - 1:
            @pl.when((z >= hop) & (z < zs - 1))
            def _():
                z_copy(i, from_left, low, 0, hop, right).start()

        @pl.when(z + hop <= zs - 1)
        def _():
            z_copy(i, from_right, high, 1, hop - 1, left).wait_recv()

        if hop < zs - 1:
            @pl.when((z + hop <= zs - 1) & (z > 0))
            def _():
                z_copy(i, from_right, high, 1, hop, left).start()

    def z_drain(i):
        w, cols, _ = items[i]
        for hop in range(zs - 1):
            src = full[w].at[z, x, core, ep, :, cols]

            @pl.when((z < zs - 1) & (z >= hop))
            def _():
                z_copy(i, src, z, 0, hop, right).wait_send()

            @pl.when((z > 0) & (z + hop <= zs - 1))
            def _():
                z_copy(i, src, z, 1, hop, left).wait_send()

    def second(i):
        w, cols, x_first = items[i]
        part = full[w].at[:, x, core, ep, :, cols]
        return push(part, part, p_send.at[i, 0], p_recv.at[i, 0], x_peer if x_first else y_peer)

    def third(i):
        w, cols, x_first = items[i]
        part = full[w].at[:, :, core, ep, :, cols] if x_first else full[w].at[:, x, core, :, :, cols]
        return push(part, part, p_send.at[i, 1], p_recv.at[i, 1], y_peer if x_first else x_peer)

    def fourth(i):
        w, cols, _ = items[i]
        part = full[w].at[:, :, core, :, :, cols]
        return push(part, part, c_send.at[i], c_recv.at[i], c_peer)

    greet(others + [x_peer, y_peer, c_peer])
    for i in range(count):
        z_start(i)
    for i in range(count):
        own(i).start()
    order = [[8, 0, 1], [2, 3], [4, 5], [6, 7]]
    for t in range(len(order) + 2):
        if t < len(order):
            for hop in range(1, zs):
                for i in order[t]:
                    z_hop(i, hop)
            for i in order[t]:
                own(i).wait()
                second(i).start()
        if 1 <= t < len(order) + 1:
            for i in order[t - 1]:
                second(i).wait_recv()
                third(i).start()
        if t >= 2:
            for i in order[t - 2]:
                third(i).wait_recv()
                fourth(i).start()
    for i in range(count):
        fourth(i).wait_recv()
    for i in range(count):
        z_drain(i)
        second(i).wait_send()
        third(i).wait_send()
        fourth(i).wait_send()


def gather_weights(zs, shards):
    shapes = [jax.ShapeDtypeStruct((zs, 2, 2, 2) + s.shape, s.dtype) for s in shards]
    n = 2 * len(shards) - 1
    dma = pltpu.SemaphoreType.DMA
    return pl.pallas_call(
        functools.partial(gather_kernel, zs),
        out_shape=shapes,
        in_specs=[pl.BlockSpec(memory_space=pltpu.VMEM)] * len(shards),
        out_specs=[pl.BlockSpec(memory_space=pl.ANY)] * len(shards),
        scratch_shapes=[dma((n,)), dma((n, 2, zs)), dma((n, 2, zs)), dma((n, 2)), dma((n, 2)), dma((n,)), dma((n,))],
        compiler_params=pltpu.CompilerParams(collective_id=1, has_side_effects=True, vmem_limit_bytes=VMEM_CAP),
        name="gather_weights",
    )(*shards)


def layer_norm(v):
    center = v - jnp.mean(v, axis=-1, keepdims=True)
    inverse = lax.rsqrt(jnp.mean(center * center, axis=-1, keepdims=True) + EPSILON)
    return center * inverse, inverse


def gelu_pair(v):
    tail = jnp.exp2(v * v * HALF_LOG2E)
    t = 1.0 / (1.0 + ERF_P * jnp.abs(v))
    poly = ((((ERF_A5 * t + ERF_A4) * t + ERF_A3) * t + ERF_A2) * t + ERF_A1) * t
    upper = poly * tail
    phi = jnp.where(v >= 0.0, 1.0 - upper, upper)
    return v * phi, phi + v * (tail * INV_ROOT_TWO_PI)


def expert_forward_kernel(tiles, rows, gain1, gain2, up1, down1, up2, down2, in1, in2, act1, slope1, act2, slope2, middle, delta, sums, acc, sub):
    layer = pl.program_id(0)
    t = pl.program_id(1)

    @pl.when((layer == 0) & (t == 0))
    def _():
        normed, _ = layer_norm(rows[...].astype(jnp.float32))
        in1[...] = (normed * gain1[...].astype(jnp.float32)).astype(jnp.bfloat16)

    def step(source, up, down, act, slope):
        total = source.shape[0]
        part = total

        def pre_of(i):
            return jnp.dot(source[i * part : (i + 1) * part], up[0], preferred_element_type=jnp.float32)

        pre = pre_of(0)
        for i in range(1):
            nxt = None
            a, s = gelu_pair(pre)
            low = a.astype(jnp.bfloat16)
            act[i * part : (i + 1) * part] = low
            slope[i * part : (i + 1) * part] = s.astype(jnp.bfloat16)
            prod = jnp.dot(low, down[0], preferred_element_type=jnp.float32)
            span = slice(i * part, (i + 1) * part)

            @pl.when(t == 0)
            def _():
                acc[span] = prod

            @pl.when(t > 0)
            def _():
                acc[span] += prod

            pre = nxt

    @pl.when(layer == 0)
    def _():
        step(in1, up1, down1, act1, slope1)

        @pl.when(t == tiles - 1)
        def _():
            value = acc[...]
            sub[...] = value
            sums[0:1] = jnp.sum(value * value, axis=0, keepdims=True)
            mid = rows[...].astype(jnp.float32) + value
            middle[...] = mid
            normed, _ = layer_norm(mid)
            in2[...] = (normed * gain2[...].astype(jnp.float32)).astype(jnp.bfloat16)

    @pl.when(layer == 1)
    def _():
        step(in2, up2, down2, act2, slope2)

        @pl.when(t == tiles - 1)
        def _():
            value = acc[...]
            sums[1:2] = jnp.sum(value * value, axis=0, keepdims=True)
            sums[2:8] = jnp.zeros((6, value.shape[1]), jnp.float32)
            delta[...] = (sub[...] + value).astype(jnp.bfloat16)


def expert_forward(rows, gain1, gain2, up1, down1, up2, down2):
    n, feat = rows.shape
    hidden = up1.shape[2]
    tile = 1024
    tiles = hidden // tile
    last = tiles - 1
    bf, f32 = jnp.bfloat16, jnp.float32
    shape = jax.ShapeDtypeStruct
    whole = lambda s: pl.BlockSpec(s, lambda l, t: (0,) * len(s))
    first = lambda l, t: jnp.where(l == 0, t, last)
    second = lambda l, t: jnp.where(l == 0, 0, t)
    up = lambda f: pl.BlockSpec((1, feat, tile), lambda l, t: (0, 0, f(l, t)))
    down = lambda f: pl.BlockSpec((1, tile, feat), lambda l, t: (0, f(l, t), 0))
    wide = lambda f: pl.BlockSpec((n, tile), lambda l, t: (0, f(l, t)))
    return pl.pallas_call(
        functools.partial(expert_forward_kernel, tiles),
        grid=(2, tiles),
        in_specs=[whole((n, feat)), whole((1, feat)), whole((1, feat)), up(first), down(first), up(second), down(second)],
        out_specs=[whole((n, feat))] * 2 + [wide(first)] * 2 + [wide(second)] * 2 + [whole((n, feat))] * 2 + [whole((8, feat))],
        out_shape=[shape((n, feat), bf)] * 2 + [shape((n, hidden), bf)] * 4 + [shape((n, feat), f32), shape((n, feat), bf), shape((8, feat), f32)],
        scratch_shapes=[pltpu.VMEM((n, feat), f32), pltpu.VMEM((n, feat), f32)],
        compiler_params=pltpu.CompilerParams(vmem_limit_bytes=VMEM_CAP, dimension_semantics=("arbitrary", "arbitrary")),
        name="expert_forward",
    )(rows, gain1, gain2, up1, down1, up2, down2)


def attend_kernel(heads, x, gain, wq, wk, wv, wo, cents, routes, prefix, cotangent, attn_in, queries, keys, values, context, hidden, gate, pick, slot_rows, slot_grads, sums, ctx):
    bf, f32 = jnp.bfloat16, jnp.float32
    tokens, feat = x.shape
    pair = 2 * feat // heads
    scale = (feat // heads) ** -0.5
    wide = x[...].astype(f32)
    normed, _ = layer_norm(wide)
    attn_in[...] = (normed * gain[...].astype(f32)).astype(bf)
    for w, out in ((wq, queries), (wk, keys), (wv, values)):
        out[...] = jnp.dot(attn_in[...], w[...], preferred_element_type=f32).astype(bf)
    row_ids = lax.broadcasted_iota(jnp.int32, (tokens, tokens), 0)
    col_ids = lax.broadcasted_iota(jnp.int32, (tokens, tokens), 1)
    visible = (col_ids <= row_ids) | (col_ids < prefix[0])
    low_half = lax.broadcasted_iota(jnp.int32, (tokens, pair), 1) < pair // 2
    last_dims = (((1,), (1,)), ((), ()))

    def body(h, carry):
        cols = pl.ds(pl.multiple_of(h * pair, pair), pair)
        q, k, v = queries[:, cols], keys[:, cols], values[:, cols]
        outs = []
        for side in (low_half, jnp.logical_not(low_half)):
            mine = jnp.where(side, q, jnp.zeros_like(q))
            s = lax.dot_general(mine, k, last_dims, preferred_element_type=f32) * scale
            s = jnp.where(visible, s, -1e30)
            top = jnp.max(s, axis=-1, keepdims=True)
            total = top + jnp.log(jnp.sum(jnp.exp(s - top), axis=-1, keepdims=True))
            p = jnp.exp(s - total).astype(bf)
            outs.append(jnp.dot(p, v, preferred_element_type=f32))
        ctx[:, cols] = jnp.where(low_half, outs[0], outs[1]).astype(bf)
        return carry

    lax.fori_loop(0, heads // 2, body, 0)
    context[...] = ctx[...]
    branch = jnp.dot(ctx[...], wo[...], preferred_element_type=f32)
    sums[...] = jnp.broadcast_to(jnp.sum(branch * branch, axis=0, keepdims=True), sums.shape)
    hid = wide + branch
    hidden[...] = hid
    low = hid.astype(bf)
    scores = lax.dot_general(low, cents[...], last_dims, preferred_element_type=f32)
    lane = lax.broadcasted_iota(jnp.int32, scores.shape, 1)
    hot = (lane == routes[...]).astype(f32)
    g = 1.0 / (1.0 + jnp.exp(-jnp.sum(scores * hot, axis=1, keepdims=True)))
    gate[...] = g
    tri = (col_ids <= row_ids).astype(bf)
    count = jnp.dot(tri, hot.astype(bf), preferred_element_type=f32)
    position = jnp.sum(count * hot, axis=1, keepdims=True) - 1.0
    target = routes[...] * tokens + position.astype(jnp.int32)
    slots = lax.broadcasted_iota(jnp.int32, (tokens, 2 * tokens), 1)
    chosen = (slots == target).astype(bf)
    pick[...] = chosen
    first_dims = (((0,), (0,)), ((), ()))
    slot_rows[...] = lax.dot_general(chosen, low, first_dims, preferred_element_type=f32).astype(bf)
    grads = (g * cotangent[...].astype(f32)).astype(bf)
    slot_grads[...] = lax.dot_general(chosen, grads, first_dims, preferred_element_type=f32).astype(bf)


def attend(heads, x, gain, wq, wk, wv, wo, cents, routes, prefix, cotangent):
    tokens, feat = x.shape
    bf, f32 = jnp.bfloat16, jnp.float32
    shape = jax.ShapeDtypeStruct
    vm = pl.BlockSpec(memory_space=pltpu.VMEM)
    return pl.pallas_call(
        functools.partial(attend_kernel, heads),
        in_specs=[vm] * 8 + [pl.BlockSpec(memory_space=pltpu.SMEM), vm],
        out_specs=[vm] * 11,
        out_shape=[shape((tokens, feat), bf)] * 5
        + [shape((tokens, feat), f32), shape((tokens, 1), f32), shape((tokens, 2 * tokens), bf)]
        + [shape((2 * tokens, feat), bf)] * 2
        + [shape((8, feat), f32)],
        scratch_shapes=[pltpu.VMEM((tokens, feat), bf)],
        compiler_params=pltpu.CompilerParams(vmem_limit_bytes=VMEM_CAP),
        name="attend",
    )(x, gain, wq, wk, wv, wo, cents, routes, prefix, cotangent)


SLICES = 4
LEAD = 2
RING = 8


def step_kernel(zs, heads, *refs):
    (x_ref, attn_in_ref, q_ref, k_ref, v_ref, context_ref, cot_ref, hidden_ref, pick_ref, wq, wk, wv, wo) = refs[0:13]
    (act_one, act_two, slope_one, slope_two, in_one, in_two, grads, rows_ref, delta, middle, up1, down1, up2, down2) = refs[13:27]
    gain, cents, gain1, gain2, gate, routes, branch_sq, sub_sq, prefix = refs[27:36]
    out_w = refs[36]
    out_a = refs[37:41]
    small_grp, small_all, result, input_grad = refs[41:45]
    pre_two, pre_one, sub_grad, row_grad, wide_far, narrow_far, attn_far, back_far, grad_far = refs[45:54]
    (send, xrecv, zrecv, acc, tiles, sides, prod, ep_in, x_in, z_in, small_in, small_ref) = refs[54:66]
    (wd, wu, sl, ps, hb, accf, midf, loadf, picks) = refs[66:75]
    (wf_s, wf_r, nf_s, nf_r, xs, xr, zsem_s, zsem_r, es, er, axs, axr, azs, azr, ss, sr, tile_sem, side_sem) = refs[75:93]
    (af_s, af_r, y_s, y_r, w_sem, ps_sem, ld_sem, out_sem) = refs[93:]
    wide = (act_two, pre_two, act_one, pre_one)
    narrow = (grads, in_two, sub_grad, in_one)
    bf, f32 = jnp.bfloat16, jnp.float32
    z, x, core, ep = place(zs)
    tokens, feat = x_ref.shape
    rows = 2 * tokens
    hidden = act_one.shape[1]
    chunk = out_w.shape[1]
    per = prod.shape[4]
    blocks = 4 * zs
    size = chunk // SLICES
    right = device(jnp.minimum(z + 1, zs - 1), x, core, ep)
    left = device(jnp.maximum(z - 1, 0), x, core, ep)
    x_peer = device(z, 1 - x, core, ep)
    y_peer = device(z, x, core, 1 - ep)
    c_peer = device(z, x, 1 - core, ep)
    others = [device(lax.rem(z + k, zs), x, core, ep) for k in range(1, zs)]
    contract0 = (((0,), (0,)), ((), ()))
    last_dims = (((1,), (1,)), ((), ()))

    def dest(k):
        to_right = zs - 1 - z
        d = jnp.where(k < to_right, zs - 1 - k, k - to_right)
        return jnp.where(k < zs - 1, d, z)

    def begins(d):
        return ((d > z) & (z == 0)) | ((d < z) & (z == zs - 1))

    def fetch(pairs):
        copies = [pltpu.make_async_copy(src, dst, ld_sem.at[i]) for i, (src, dst) in enumerate(pairs)]
        for c in copies:
            c.start()
        for c in copies:
            c.wait()

    def two(slot):
        return hb.at[pl.ds(slot, 2)]

    def flat(slot):
        return hb[pl.ds(slot, 2)].reshape(rows, feat)

    greet(others + [x_peer, y_peer, c_peer])

    def far_wide(w, q):
        j = q * 2 + (1 - core)
        return push(
            wide[w].at[:, pl.ds(pl.multiple_of(j * chunk, chunk), chunk)], wide_far.at[w, q], wf_s.at[w], wf_r.at[w], c_peer
        )

    def far_narrow(w):
        return push(narrow[w], narrow_far.at[w], nf_s.at[w], nf_r.at[w], c_peer)

    def all_far(w):
        return push(wide_far.at[w], wide_far.at[w], wf_s.at[w], wf_r.at[w], c_peer)

    def send_wide(w):
        def send_far(q, carry):
            far_wide(w, q).start()
            return carry

        lax.fori_loop(0, 2 * zs, send_far, 0)

    def far_attn(i, src):
        return push(src, attn_far.at[i], af_s.at[i], af_r.at[i], c_peer)

    def far_delta():
        return push(delta.at[1 - ep], back_far, y_s.at[0], y_r.at[0], y_peer)

    def far_rows():
        return push(row_grad.at[1 - ep], grad_far, y_s.at[1], y_r.at[1], y_peer)

    far_narrow(0).start()
    send_wide(0)
    far_delta().start()
    far_narrow(1).start()
    far_narrow(3).start()
    far_attn(0, attn_in_ref).start()
    far_attn(1, context_ref).start()

    def load_tile(w, q, slot):
        j = q * 2 + core
        for i in range(4):
            @pl.when(w == i)
            def _():
                pltpu.make_async_copy(
                    wide[i].at[:, pl.ds(pl.multiple_of(j * chunk, chunk), chunk)],
                    tiles.at[slot, pl.ds(0, rows), :],
                    tile_sem.at[slot, 0],
                ).start()

        pltpu.make_async_copy(wide_far.at[w, q], tiles.at[slot, pl.ds(rows, rows), :], tile_sem.at[slot, 1]).start()

    def wait_tile(slot):
        for i in range(2):
            part = tiles.at[slot, pl.ds(i * rows, rows), :]
            pltpu.make_async_copy(part, part, tile_sem.at[slot, i]).wait()

    def load_side(w):
        slot = lax.rem(w, 2)
        for i in range(4):
            @pl.when(w == i)
            def _():
                pltpu.make_async_copy(narrow[i], sides.at[slot, pl.ds(0, 2)], side_sem.at[0]).start()

        pltpu.make_async_copy(narrow_far.at[w], sides.at[slot, pl.ds(2, 2)], side_sem.at[1]).start()

    def wait_side(w):
        slot = lax.rem(w, 2)
        for i in range(2):
            part = sides.at[slot, pl.ds(2 * i, 2)]
            pltpu.make_async_copy(part, part, side_sem.at[i]).wait()

    def product(w, slot):
        side = sides[lax.rem(w, 2)].reshape(2 * rows, feat)
        return lax.dot_general(tiles[slot], side, contract0, preferred_element_type=f32)

    def span(s):
        return pl.ds(pl.multiple_of(s * size, size), size)

    def x_copy(b, s):
        return push(send.at[lax.rem(b, RING), span(s), :], xrecv.at[b, span(s), :], xs.at[b, s], xr.at[b, s], x_peer)

    def z_copy(b, s):
        w = lax.div(b, zs)
        d = dest(lax.rem(b, zs))
        to_right = d > z
        nxt = jnp.where(to_right, z + 1, z - 1)
        slot = jnp.where(d != nxt, d, jnp.where(to_right, d, zs))
        return push(
            send.at[lax.rem(b, RING), span(s), :], zrecv.at[w, slot, span(s), :], zsem_s.at[b, s],
            zsem_r.at[w, slot, s], device(nxt, x, core, ep),
        )

    def z_wait(w, slot, s):
        ref = zrecv.at[w, slot, span(s), :]
        push(ref, ref, zsem_s.at[0, s], zsem_r.at[w, slot, s], x_peer).wait_recv()
        return ref[...].astype(f32)

    def z_sent(b):
        @pl.when(lax.rem(b, zs) < zs - 1)
        def _():
            for s in range(SLICES):
                z_copy(b, s).wait_send()

    def q_first(b):
        return dest(lax.rem(b, zs)) * 2 + (1 - x)

    def q_second(b):
        return dest(lax.rem(b, zs)) * 2 + x

    def far_wait(w):
        for i in range(4):
            @pl.when(w == i)
            def _():
                far_narrow(i).wait_recv()
                all_far(i).wait_recv()

    def stage_one(b):
        w = lax.div(b, zs)
        slot = lax.rem(b, 2)

        @pl.when(lax.rem(b, zs) == 0)
        def _():
            far_wait(w)
            load_side(w)
            load_tile(w, q_first(b), slot)
            wait_side(w)

        wait_tile(slot)

        @pl.when(lax.rem(b, zs) < zs - 1)
        def _():
            load_tile(w, q_first(b + 1), 1 - slot)

        @pl.when(b >= RING)
        def _():
            z_sent(b - RING)

        send[lax.rem(b, RING)] = product(w, slot).astype(bf)

    def stage_two(b):
        w = lax.div(b, zs)
        d = dest(lax.rem(b, zs))
        slot = 2 + lax.rem(b, 2)
        mine = lax.rem(b, RING)
        wait_tile(slot)

        @pl.when(b + 1 < blocks)
        def _():
            load_tile(lax.div(b + 1, zs), q_second(b + 1), 5 - slot)

        acc[...] = product(w, slot)

        def piece(s, carry):
            sp = span(s)
            x_copy(b, s).wait()
            acc[sp, :] += xrecv[b, sp, :].astype(f32)

            @pl.when(d != z)
            def _():
                @pl.when(jnp.logical_not(begins(d)))
                def _():
                    acc[sp, :] += z_wait(w, d, s)

                send[mine, sp, :] = acc[sp, :].astype(bf)

                @pl.when(s > 0)
                def _():
                    z_copy(b, s - 1).start()

            @pl.when(d == z)
            def _():
                acc[sp, :] += z_wait(w, jnp.where(z > 0, z, zs), s)

                @pl.when((z > 0) & (z < zs - 1))
                def _():
                    acc[sp, :] += z_wait(w, zs, s)

            return carry

        lax.fori_loop(0, SLICES, piece, 0)

        @pl.when(d != z)
        def _():
            z_copy(b, SLICES - 1).start()

        @pl.when(d == z)
        def _():
            copy = pltpu.make_async_copy(acc, out_w.at[w], out_sem)
            copy.start()
            copy.wait()

    tile = wd.shape[1]

    def stream(source, start, count, up, down, slope, pre):
        def copies(t, slot):
            cols = pl.ds(pl.multiple_of(t * tile, tile), tile)
            return (
                pltpu.make_async_copy(down.at[0, cols, :], wd.at[slot], w_sem.at[slot, 0]),
                pltpu.make_async_copy(up.at[0, :, cols], wu.at[slot], w_sem.at[slot, 1]),
                pltpu.make_async_copy(slope.at[pl.ds(start, count), cols], sl.at[slot, pl.ds(0, count), :], w_sem.at[slot, 2]),
            )

        def out(t, slot):
            cols = pl.ds(pl.multiple_of(t * tile, tile), tile)
            return pltpu.make_async_copy(ps.at[slot, pl.ds(0, count), :], pre.at[pl.ds(start, count), cols], ps_sem.at[slot])

        steps = hidden // tile
        for c in copies(0, 0):
            c.start()

        def body(t, carry):
            slot = lax.rem(t, 2)
            for c in copies(t, slot):
                c.wait()

            @pl.when(t + 1 < steps)
            def _():
                for c in copies(t + 1, 1 - slot):
                    c.start()

            g = lax.dot_general(source(), wd[slot], last_dims, preferred_element_type=f32)
            low = (g * sl[slot, 0:count].astype(f32)).astype(bf)

            @pl.when(t >= 2)
            def _():
                out(t - 2, slot).wait()

            ps[slot, 0:count] = low
            out(t, slot).start()
            value = lax.dot_general(low, wu[slot], last_dims, preferred_element_type=f32)

            @pl.when(t == 0)
            def _():
                accf[0:count] = value

            @pl.when(t > 0)
            def _():
                accf[0:count] += value

            return carry

        lax.fori_loop(0, steps, body, 0)
        out(steps - 2, lax.rem(steps - 2, 2)).wait()
        out(steps - 1, lax.rem(steps - 1, 2)).wait()

    part = 64

    def norm_parts_of(value, g, gain_row):
        normed, inverse = layer_norm(value)
        total = jnp.sum(g * normed, axis=0, keepdims=True)
        q = g * gain_row
        mean_q = jnp.mean(q, axis=-1, keepdims=True)
        mean_dot = jnp.mean(q * normed, axis=-1, keepdims=True)
        return total, inverse * (q - mean_q - normed * mean_dot)

    def event_second():
        fetch([(grads, two(0)), (middle, loadf), (rows_ref, two(2))])
        stream(lambda: flat(0), 0, rows, up2, down2, slope_two, pre_two)
        send_wide(1)
        small_ref[...] = jnp.zeros_like(small_ref)
        gain_row = gain2[...].astype(f32)
        per_block = tokens // part

        def body(i, carry):
            at = pl.ds(pl.multiple_of(i * part, part), part)
            total, value = norm_parts_of(loadf[at], accf[at], gain_row)
            small_ref[1:2] += total
            midf[at] = value
            blk = lax.div(i, per_block)
            sub = pl.ds(pl.multiple_of(lax.rem(i, per_block) * part, part), part)
            hb[4 + blk, sub] = (hb[blk, sub].astype(f32) + value).astype(bf)
            return carry

        lax.fori_loop(0, rows // part, body, 0)
        fetch([(two(4), sub_grad)])
        far_narrow(2).start()
        send_wide(2)

    def event_first(blk):
        start = pl.multiple_of(blk * tokens, tokens)
        stream(lambda: hb[4 + blk], start, tokens, up1, down1, slope_one, pre_one)
        gain_row = gain1[...].astype(f32)

        def body(i, carry):
            at = pl.ds(pl.multiple_of(i * part, part), part)
            value = hb[2 + blk, at].astype(f32)
            total, back = norm_parts_of(value, accf[at], gain_row)
            small_ref[0:1] += total
            mid = midf[pl.ds(pl.multiple_of(blk * tokens + i * part, part), part)]
            hb[6 + blk, at] = (back + mid).astype(bf)
            return carry

        lax.fori_loop(0, tokens // part, body, 0)
        fetch([(hb.at[6 + blk], row_grad.at[blk])])

    def event_first_far():
        event_first(1 - ep)
        far_rows().start()

    def event_first_own():
        event_first(ep)
        send_wide(3)

    def event_attend():
        far_delta().wait_recv()
        far_rows().wait_recv()
        fetch(
            [
                (cot_ref, hb.at[1]),
                (delta.at[ep], hb.at[3]),
                (back_far, hb.at[5]),
                (row_grad.at[ep], hb.at[7]),
                (grad_far, hb.at[9]),
                (q_ref, hb.at[12]),
                (k_ref, hb.at[13]),
                (v_ref, hb.at[14]),
                (x_ref, hb.at[11]),
                (attn_in_ref, hb.at[0]),
                (context_ref, hb.at[2]),
                (hidden_ref, loadf.at[pl.ds(0, tokens)]),
                (pick_ref, picks),
                (wo.at[pl.ds(0, feat // 2)], wd.at[0]),
                (wo.at[pl.ds(feat // 2, feat // 2)], wd.at[1]),
            ]
        )
        c = cents[...].astype(f32)

        def combine(i, carry):
            at = pl.ds(pl.multiple_of(i * part, part), part)
            own = picks[at, pl.ds(pl.multiple_of(ep * tokens, tokens), tokens)]
            far = picks[at, pl.ds(pl.multiple_of((1 - ep) * tokens, tokens), tokens)]
            returned = jnp.dot(own, hb[3], preferred_element_type=f32) + jnp.dot(far, hb[5], preferred_element_type=f32)
            back = jnp.dot(own, hb[7], preferred_element_type=f32) + jnp.dot(far, hb[9], preferred_element_type=f32)
            g = gate[at]
            hid = loadf[at]
            res = hid + g * returned
            hb[15, at] = res.astype(bf)
            small_ref[5:6] += jnp.sum(res * res, axis=0, keepdims=True)
            grad_out = hb[1, at].astype(f32)
            grad_score = jnp.sum(grad_out * returned, axis=1, keepdims=True) * g * (1.0 - g)
            is_first = routes[at] == 0
            weighted = grad_score * hid.astype(bf).astype(f32)
            zero = jnp.zeros_like(weighted)
            small_ref[3:4] += jnp.sum(jnp.where(is_first, weighted, zero), axis=0, keepdims=True)
            small_ref[4:5] += jnp.sum(jnp.where(is_first, zero, weighted), axis=0, keepdims=True)
            grad_hidden = grad_out + grad_score * jnp.where(is_first, c[0:1], c[1:2]) + back
            midf[at] = grad_hidden
            hb[10, at] = grad_hidden.astype(bf)
            return carry

        lax.fori_loop(0, tokens // part, combine, 0)
        fetch([(hb.at[15], result)])
        half = feat // 2
        for i in range(2):
            hb[15, :, i * half : (i + 1) * half] = lax.dot_general(
                hb[10], wd[i], last_dims, preferred_element_type=f32
            ).astype(bf)
        row_ids = lax.broadcasted_iota(jnp.int32, (tokens, tokens), 0)
        col_ids = lax.broadcasted_iota(jnp.int32, (tokens, tokens), 1)
        pair = 2 * feat // heads
        scale = (feat // heads) ** -0.5
        limit = prefix[...]

        def head(h, carry):
            visible = (col_ids <= row_ids) | (col_ids < limit)
            low_half = lax.broadcasted_iota(jnp.int32, (tokens, pair), 1) < pair // 2
            cols = pl.ds(pl.multiple_of(h * pair, pair), pair)
            q, k, v, gc = hb[12, :, cols], hb[13, :, cols], hb[14, :, cols], hb[15, :, cols]
            outs = []
            for side in (low_half, jnp.logical_not(low_half)):
                s = lax.dot_general(jnp.where(side, q, jnp.zeros_like(q)), k, last_dims, preferred_element_type=f32) * scale
                s = jnp.where(visible, s, -1e30)
                top = jnp.max(s, axis=-1, keepdims=True)
                total = top + jnp.log(jnp.sum(jnp.exp(s - top), axis=-1, keepdims=True))
                p = jnp.exp(s - total)
                gp = lax.dot_general(jnp.where(side, gc, jnp.zeros_like(gc)), v, last_dims, preferred_element_type=f32)
                dot = jnp.sum(gp * p, axis=-1, keepdims=True)
                gs = (p * (gp - dot)).astype(bf)
                outs.append(
                    (
                        jnp.dot(gs, k, preferred_element_type=f32),
                        lax.dot_general(gs, q, contract0, preferred_element_type=f32),
                        lax.dot_general(p.astype(bf), gc, contract0, preferred_element_type=f32),
                    )
                )
            hb[4, :, cols] = (jnp.where(low_half, outs[0][0], outs[1][0]) * scale).astype(bf)
            hb[6, :, cols] = (jnp.where(low_half, outs[0][1], outs[1][1]) * scale).astype(bf)
            hb[8, :, cols] = jnp.where(low_half, outs[0][2], outs[1][2]).astype(bf)
            return carry

        lax.fori_loop(0, heads // 2, head, 0)
        loads = [(m, i) for i in range(2) for m in (wq, wk, wv)]

        def weight_copy(n):
            m, i = loads[n]
            return pltpu.make_async_copy(m.at[pl.ds(i * half, half)], wd.at[n % 2], w_sem.at[n % 2, 0])

        weight_copy(0).start()
        for n in range(6):
            weight_copy(n).wait()
            if n < 5:
                weight_copy(n + 1).start()
            value = lax.dot_general(hb[4 + 2 * (n % 3)], wd[n % 2], last_dims, preferred_element_type=f32)
            cols = slice((n // 3) * half, (n // 3 + 1) * half)
            if n % 3 == 0:
                accf[0:tokens, cols] = value
            else:
                accf[0:tokens, cols] += value
        for i in range(4):
            far_attn(2 + i, hb.at[4 + 2 * i]).start()
        gain_row = gain[...].astype(f32)

        def norms(i, carry):
            at = pl.ds(pl.multiple_of(i * part, part), part)
            total, value = norm_parts_of(hb[11, at].astype(f32), accf[at], gain_row)
            small_ref[2:3] += total
            midf[at] += value
            return carry

        lax.fori_loop(0, tokens // part, norms, 0)
        small_ref[6:7] = branch_sq[0:1]
        small_ref[7:9] = sub_sq[0:2]
        start0()
        for i in range(6):
            far_attn(i, hb.at[0]).wait_recv()
        fetch(
            [(midf.at[pl.ds(0, tokens)], input_grad)]
            + [(attn_far.at[i], hb.at[2 * i + 1]) for i in range(6)]
        )
        step = 8 * per

        for w in range(4):
            lhs = 0 if w < 3 else 2
            rhs = 4 + 2 * w

            def form(m, carry):
                cols = pl.ds(pl.multiple_of(m * step, step), step)
                left_part = hb[pl.ds(lhs, 2), :, cols].reshape(rows, step)
                value = lax.dot_general(left_part, flat(rhs), contract0, preferred_element_type=f32)
                value = value.astype(bf).reshape(2, 2, 2 * per, feat)
                mine = jnp.where(core == 0, value[:, 0], value[:, 1])
                prod[w, m] = mine.reshape(2, 2, per, feat)
                return carry

            lax.fori_loop(0, zs, form, 0)
            if w > 0:
                attn_ep(w - 1).start()
        for i in range(6):
            far_attn(i, hb.at[0]).wait_send()
        attn_ep(3).start()

    def attn_ep(w):
        return push(prod.at[w, :, :, 1 - ep], ep_in.at[w], es.at[w], er.at[w], y_peer)

    def attn_x(w):
        return push(prod.at[w, :, 1 - x, ep], x_in.at[w], axs.at[w], axr.at[w], x_peer)

    def fold_ep(w):
        attn_ep(w).wait()

        def body(m, carry):
            for i in range(2):
                total = prod[w, m, i, ep].astype(f32) + ep_in[w, m, i].astype(f32)
                prod[w, m, i, ep] = total.astype(bf)
            return carry

        lax.fori_loop(0, zs, body, 0)

    def attn_z_copy(w, k):
        d = dest(k)
        to_right = d > z
        nxt = jnp.where(to_right, z + 1, z - 1)
        slot = jnp.where(d != nxt, d, jnp.where(to_right, d, zs))
        return push(prod.at[w, d, x, ep], z_in.at[w, slot], azs.at[w, k], azr.at[w, slot], device(nxt, x, core, ep))

    def attn_z_wait(w, slot):
        ref = z_in.at[w, slot]
        push(ref, ref, azs.at[w, 0], azr.at[w, slot], x_peer).wait_recv()
        return ref[...].astype(f32)

    def fold_x(w):
        attn_x(w).wait()

        def body(k, carry):
            d = dest(k)
            total = prod[w, d, x, ep].astype(f32) + x_in[w, d].astype(f32)
            prod[w, d, x, ep] = total.astype(bf)
            return carry

        lax.fori_loop(0, zs, body, 0)

    def fold_z(w):
        def body(k, carry):
            d = dest(k)

            @pl.when(jnp.logical_not(begins(d)))
            def _():
                total = prod[w, d, x, ep].astype(f32) + attn_z_wait(w, d)
                prod[w, d, x, ep] = total.astype(bf)

            attn_z_copy(w, k).start()
            return carry

        lax.fori_loop(0, zs - 1, body, 0)

    def last_z(w):
        first = jnp.where(z > 0, z, zs)
        out_a[w][...] = prod[w, z, x, ep].astype(f32) + attn_z_wait(w, first)

        @pl.when((z > 0) & (z < zs - 1))
        def _():
            out_a[w][...] += attn_z_wait(w, zs)

        for k in range(zs - 1):
            attn_z_copy(w, k).wait_send()

    def small_stage(stage, n, mine, peer_at, src):
        def copy(k):
            return push(src, small_in.at[stage, mine], ss.at[stage, k], sr.at[stage, k], peer_at(lax.rem(mine + k, n)))

        def start():
            for k in range(1, n):
                copy(k).start()

        def end():
            for k in range(1, n):
                copy(k).wait()
            small_in[stage, mine] = src[...]
            total = small_in[stage, 0]
            for i in range(1, n):
                total = total + small_in[stage, i]
            return total

        return start, end

    start0, end0 = small_stage(0, 2, core, lambda i: device(z, x, i, ep), small_ref)
    start1, end1 = small_stage(1, 2, x, lambda i: device(z, i, core, ep), small_in.at[3, 3])
    start2, end2 = small_stage(2, zs, z, lambda i: device(i, x, core, ep), small_in.at[3, 2])
    start3, end3 = small_stage(3, 2, ep, lambda i: device(z, x, core, i), small_grp)

    def event_x(w):
        def act():
            fold_ep(w)
            attn_x(w).start()

        return act

    def event_small1():
        small_in[3, 3] = end0()
        start1()

    def event_small2():
        small_in[3, 2] = end1()
        start2()

    def event_small3():
        small_grp[...] = end2()
        start3()

    def event_z(w):
        def act():
            fold_x(w)
            fold_z(w)

        return act

    def event_last():
        for w in range(4):
            last_z(w)
        small_all[...] = end3()

    events = EVENTS(
        event_second, event_first_far, event_first_own, event_attend, event_x, event_small1, event_small2, event_small3,
        event_z, event_last,
    )

    def pipeline(t, carry):
        for at, action in events:
            pl.when(t == at)(action)

        @pl.when(t < blocks)
        def _():
            stage_one(t)

        @pl.when((t > 0) & (t <= blocks))
        def _():
            for s in range(SLICES):
                x_copy(t - 1, s).start()

        @pl.when(t == LEAD - 1)
        def _():
            load_tile(0, q_second(0), 2)

        @pl.when(t >= LEAD)
        def _():
            stage_two(t - LEAD)

        return carry

    lax.fori_loop(0, blocks + LEAD, pipeline, 0)
    event_last()

    def drain(b, carry):
        z_sent(b)
        return carry

    lax.fori_loop(blocks - RING, blocks, drain, 0)
    for w in range(4):
        far_narrow(w).wait_send()
        all_far(w).wait_send()
    far_delta().wait_send()
    far_rows().wait_send()


def EVENTS(second, first_far, first_own, attend_event, x_of, small1, small2, small3, z_of, last):
    found = [(2, second), (5, first_far), (7, first_own), (9, attend_event)]
    found += [(11, small1), (12, small2), (13, small3)]
    found += [(11 + w, x_of(w)) for w in range(4)]
    found += [(14 + w, z_of(w)) for w in range(4)]
    return found


def backward_step(zs, heads, big, experts, little, prefix):
    x, hidden = big[0], experts[0].shape[1]
    tokens, feat = x.shape
    rows = 2 * tokens
    chunk = hidden // (4 * zs)
    per = feat // (8 * zs)
    f32, bf = jnp.float32, jnp.bfloat16
    shape = jax.ShapeDtypeStruct
    vm = pl.BlockSpec(memory_space=pltpu.VMEM)
    hbm = pl.BlockSpec(memory_space=pl.ANY)
    dma = pltpu.SemaphoreType.DMA
    outs = [shape((4, chunk, feat), f32)]
    outs += [shape((per, feat), f32)] * 4
    outs += [shape((16, feat), f32)] * 2
    outs += [shape((tokens, feat), bf), shape((tokens, feat), f32)]
    outs += [shape((rows, hidden), bf)] * 2 + [shape((2, tokens, feat), bf)] * 2
    outs += [shape((4, 2 * zs, rows, chunk), bf), shape((4, 2, tokens, feat), bf), shape((6, tokens, feat), bf)]
    outs += [shape((tokens, feat), bf)] * 2
    s = SLICES
    blocks = 4 * zs
    tile = 512
    vmem = pltpu.VMEM
    return pl.pallas_call(
        functools.partial(step_kernel, zs, heads),
        out_shape=outs,
        in_specs=[hbm] * 27 + [vm] * 9,
        out_specs=[hbm] + [vm] * 6 + [hbm] * 11,
        scratch_shapes=[
            vmem((RING, chunk, feat), bf),
            vmem((blocks, chunk, feat), bf),
            vmem((4, zs + 1, chunk, feat), bf),
            vmem((chunk, feat), f32),
            vmem((4, 2 * rows, chunk), bf),
            vmem((2, 4, tokens, feat), bf),
            vmem((4, zs, 2, 2, per, feat), bf),
            vmem((4, zs, 2, per, feat), bf),
            vmem((4, zs, per, feat), bf),
            vmem((4, zs + 1, per, feat), bf),
            vmem((4, max(zs, 4), 16, feat), f32),
            vmem((16, feat), f32),
            vmem((2, tile, feat), bf),
            vmem((2, feat, tile), bf),
            vmem((2, rows, tile), bf),
            vmem((2, rows, tile), bf),
            vmem((16, tokens, feat), bf),
            vmem((rows, feat), f32),
            vmem((rows, feat), f32),
            vmem((rows, feat), f32),
            vmem((tokens, rows), bf),
            dma((4,)), dma((4,)), dma((4,)), dma((4,)),
            dma((blocks, s)), dma((blocks, s)), dma((blocks, s)), dma((4, zs + 1, s)),
            dma((4,)), dma((4,)), dma((4,)), dma((4,)), dma((4, zs)), dma((4, zs + 1)),
            dma((4, zs)), dma((4, zs)), dma((4, 2)), dma((2,)),
            dma((6,)), dma((6,)), dma((2,)), dma((2,)), dma((2, 3)), dma((2,)), dma((16,)), dma,
        ],
        compiler_params=pltpu.CompilerParams(collective_id=2, has_side_effects=True, vmem_limit_bytes=VMEM_CAP),
        name="backward_step",
    )(*big, *experts, *little, prefix)


def shards(
    inputs,
    attn_gain,
    w_query,
    w_key,
    w_value,
    w_output,
    centroids,
    norm1_gain,
    norm2_gain,
    up_first,
    down_first,
    up_second,
    down_second,
    routes,
    prefix,
    cotangent,
):
    gathered = (
        lax.all_gather(attn_gain, ("grp", "ep"), axis=0, tiled=True),
        lax.all_gather(w_query, ("grp", "ep"), axis=0, tiled=True),
        lax.all_gather(w_key, ("grp", "ep"), axis=0, tiled=True),
        lax.all_gather(w_value, ("grp", "ep"), axis=0, tiled=True),
        lax.all_gather(w_output, ("grp", "ep"), axis=0, tiled=True),
        lax.all_gather(centroids, ("grp", "ep"), axis=0, tiled=True),
    )
    gain_attn, query_mat, key_mat, value_mat, output_mat, centroid_mat = gathered
    token_count, feature_width = inputs.shape
    head_count = HEADS
    head_width = feature_width // head_count
    scale_factor = head_width ** (-0.5)
    block_rows = min(512, token_count)
    prefix_len = prefix[0]
    inputs_wide = inputs.astype(jnp.float32)
    normed_attn, inverse_attn = norm_parts(inputs_wide)
    gain_attn_wide = gain_attn.astype(jnp.float32)
    attn_in = (normed_attn * gain_attn_wide).astype(jnp.bfloat16)
    queries = (
        matmul(attn_in, query_mat).astype(jnp.bfloat16).reshape(token_count, head_count, head_width)
    )
    key_heads = (
        matmul(attn_in, key_mat).astype(jnp.bfloat16).reshape(token_count, head_count, head_width)
    )
    value_heads = (
        matmul(attn_in, value_mat).astype(jnp.bfloat16).reshape(token_count, head_count, head_width)
    )

    def block_scores(block_index):
        row_start = block_index * block_rows
        scores = (
            jnp.einsum("qhd,khd->hqk", queries, key_heads, preferred_element_type=jnp.float32)
            * scale_factor
        )
        visible = visible_mask(row_start, block_rows, token_count, prefix_len)
        return (queries, jnp.where(visible[None], scores, -1e30))

    block_index = 0
    query_block, scores = block_scores(block_index)
    row_max = jnp.max(scores, axis=-1, keepdims=True)
    expsum = jnp.sum(jnp.exp(scores - row_max), axis=-1, keepdims=True)
    log_total = row_max + jnp.log(expsum)
    probs_low = jnp.exp(scores - log_total).astype(jnp.bfloat16)
    context_parts = jnp.einsum(
        "hqk,khd->qhd", probs_low, value_heads, preferred_element_type=jnp.float32
    ).astype(jnp.bfloat16)
    lse_parts = [log_total]
    context = context_parts.reshape(token_count, feature_width)
    branch = matmul(context, output_mat)
    hidden = inputs_wide + branch
    hidden_low = hidden.astype(jnp.bfloat16)
    expert_total = lax.axis_size("ep")
    group_total = lax.axis_size("grp")
    capacity = 2 * token_count // expert_total
    route_ids = routes[:, 0]
    expert_ids = jnp.arange(expert_total, dtype=jnp.int32)
    route_hot = (route_ids[:, None] == expert_ids[None, :]).astype(jnp.int32)
    position = jnp.sum((jnp.cumsum(route_hot, axis=0) - 1) * route_hot, axis=1)
    target = route_ids * capacity + position
    route_weight = route_hot.astype(jnp.float32)
    all_scores = matmul(hidden_low, centroid_mat)
    gate_value = jax.nn.sigmoid(jnp.sum(all_scores * route_weight, axis=1))
    slot_rows = fill_slots(hidden_low, target, expert_total * capacity).reshape(
        expert_total, capacity, feature_width
    )
    received = lax.all_to_all(slot_rows, "ep", split_axis=0, concat_axis=0, tiled=True).reshape(
        expert_total * capacity, feature_width
    )
    gain_one = norm1_gain[0].astype(jnp.float32)
    gain_two = norm2_gain[0].astype(jnp.float32)
    up_one = up_first[0]
    down_one = down_first[0]
    up_two = up_second[0]
    down_two = down_second[0]
    rows_wide = received.astype(jnp.float32)
    normed_one, inverse_one = norm_parts(rows_wide)
    in_one = (normed_one * gain_one).astype(jnp.bfloat16)
    pre_one = matmul(in_one, up_one)
    act_one = jax.nn.gelu(pre_one, approximate=False).astype(jnp.bfloat16)
    sub_one = matmul(act_one, down_one)
    middle = rows_wide + sub_one
    normed_two, inverse_two = norm_parts(middle)
    in_two = (normed_two * gain_two).astype(jnp.bfloat16)
    pre_two = matmul(in_two, up_two)
    act_two = jax.nn.gelu(pre_two, approximate=False).astype(jnp.bfloat16)
    sub_two = matmul(act_two, down_two)
    delta = (sub_one + sub_two).astype(jnp.bfloat16).reshape(expert_total, capacity, feature_width)
    back_slots = lax.all_to_all(delta, "ep", split_axis=0, concat_axis=0, tiled=True).reshape(
        expert_total * capacity, feature_width
    )
    returned = back_slots[target].astype(jnp.float32)
    result = hidden + gate_value[:, None] * returned
    square_terms = jnp.stack(
        [
            jnp.sum(result * result),
            jnp.sum(branch * branch),
            jnp.sum(sub_one * sub_one),
            jnp.sum(sub_two * sub_two),
        ]
    )
    square_totals = lax.psum(square_terms, ("grp", "ep"))
    cell_count = float(token_count * feature_width * group_total * expert_total)
    rms_values = jnp.sqrt(square_totals / cell_count)
    grad_out = cotangent.astype(jnp.float32)
    grad_gate = jnp.sum(grad_out * returned, axis=1)
    grad_score = grad_gate * gate_value * (1.0 - gate_value)
    grad_delta_tok = (gate_value[:, None] * grad_out).astype(jnp.bfloat16)
    grad_slots = fill_slots(grad_delta_tok, target, expert_total * capacity).reshape(
        expert_total, capacity, feature_width
    )
    grad_sum = lax.all_to_all(grad_slots, "ep", split_axis=0, concat_axis=0, tiled=True).reshape(
        expert_total * capacity, feature_width
    )
    grad_pre_two = (dot_last(grad_sum, down_two) * gelu_slope(pre_two)).astype(jnp.bfloat16)
    grad_in_two = dot_last(grad_pre_two, up_two)
    grad_gain_two = jnp.sum(grad_in_two * normed_two, axis=0)
    grad_middle = norm_back(grad_in_two * gain_two, normed_two, inverse_two)
    grad_sub_one = (grad_sum.astype(jnp.float32) + grad_middle).astype(jnp.bfloat16)
    grad_pre_one = (dot_last(grad_sub_one, down_one) * gelu_slope(pre_one)).astype(jnp.bfloat16)
    grad_in_one = dot_last(grad_pre_one, up_one)
    grad_gain_one = jnp.sum(grad_in_one * normed_one, axis=0)
    grad_rows = (norm_back(grad_in_one * gain_one, normed_one, inverse_one) + grad_middle).astype(
        jnp.bfloat16
    )
    grad_back = lax.all_to_all(
        grad_rows.reshape(expert_total, capacity, feature_width),
        "ep",
        split_axis=0,
        concat_axis=0,
        tiled=True,
    ).reshape(expert_total * capacity, feature_width)
    grad_down_two = dot_first(act_two, grad_sum)
    grad_up_two = dot_first(in_two, grad_pre_two)
    grad_down_one = dot_first(act_one, grad_sub_one)
    grad_up_one = dot_first(in_one, grad_pre_one)
    expert_sums = (
        lax.psum_scatter(grad_up_one[None], "grp", scatter_dimension=2, tiled=True),
        lax.psum_scatter(grad_down_one[None], "grp", scatter_dimension=1, tiled=True),
        lax.psum_scatter(grad_up_two[None], "grp", scatter_dimension=2, tiled=True),
        lax.psum_scatter(grad_down_two[None], "grp", scatter_dimension=1, tiled=True),
        lax.psum_scatter(grad_gain_one[None], "grp", scatter_dimension=1, tiled=True),
        lax.psum_scatter(grad_gain_two[None], "grp", scatter_dimension=1, tiled=True),
    )
    up_one_sum, down_one_sum, up_two_sum, down_two_sum, gain_one_sum, gain_two_sum = expert_sums
    centroid_wide = centroid_mat.astype(jnp.float32)
    score_weight = route_weight * grad_score[:, None]
    grad_hidden = (
        grad_out
        + jnp.dot(score_weight, centroid_wide.T, precision=HIGH)
        + grad_back[target].astype(jnp.float32)
    )
    grad_centroid = lax.dot_general(
        hidden_low.astype(jnp.float32), score_weight, (((0,), (0,)), ((), ())), precision=HIGH
    )
    grad_branch = grad_hidden.astype(jnp.bfloat16)
    grad_output_mat = dot_first(context, grad_branch)
    grad_context = (
        dot_last(grad_branch, output_mat)
        .astype(jnp.bfloat16)
        .reshape(token_count, head_count, head_width)
    )
    block_index = 0
    query_block, scores = block_scores(block_index)
    probs_wide = jnp.exp(scores - lse_parts[block_index])
    probs_low = probs_wide.astype(jnp.bfloat16)
    row_start = block_index * block_rows
    grad_value_sum = jnp.einsum(
        "hqk,qhd->khd", probs_low, grad_context, preferred_element_type=jnp.float32
    )
    grad_probs = jnp.einsum(
        "qhd,khd->hqk", grad_context, value_heads, preferred_element_type=jnp.float32
    )
    row_dot = jnp.sum(grad_probs * probs_wide, axis=-1, keepdims=True)
    grad_scores = (probs_wide * (grad_probs - row_dot)).astype(jnp.bfloat16)
    grad_query_parts = (
        jnp.einsum("hqk,khd->qhd", grad_scores, key_heads, preferred_element_type=jnp.float32)
        * scale_factor
    ).astype(jnp.bfloat16)
    grad_key_sum = (
        jnp.einsum("hqk,qhd->khd", grad_scores, query_block, preferred_element_type=jnp.float32)
        * scale_factor
    )
    grad_queries = grad_query_parts.reshape(token_count, feature_width)
    grad_keys = grad_key_sum.astype(jnp.bfloat16).reshape(token_count, feature_width)
    grad_values = grad_value_sum.astype(jnp.bfloat16).reshape(token_count, feature_width)
    grad_query_mat = dot_first(attn_in, grad_queries)
    grad_key_mat = dot_first(attn_in, grad_keys)
    grad_value_mat = dot_first(attn_in, grad_values)
    grad_attn_in = (
        dot_last(grad_queries, query_mat)
        + dot_last(grad_keys, key_mat)
        + dot_last(grad_values, value_mat)
    )
    grad_gain_attn = jnp.sum(grad_attn_in * normed_attn, axis=0)
    input_grad = grad_hidden + norm_back(grad_attn_in * gain_attn_wide, normed_attn, inverse_attn)
    attn_terms = (
        grad_gain_attn,
        grad_query_mat,
        grad_key_mat,
        grad_value_mat,
        grad_output_mat,
        grad_centroid,
    )
    outer_sums = (
        lax.psum_scatter(attn_terms[0], "grp", scatter_dimension=0, tiled=True),
        lax.psum_scatter(attn_terms[1], "grp", scatter_dimension=0, tiled=True),
        lax.psum_scatter(attn_terms[2], "grp", scatter_dimension=0, tiled=True),
        lax.psum_scatter(attn_terms[3], "grp", scatter_dimension=0, tiled=True),
        lax.psum_scatter(attn_terms[4], "grp", scatter_dimension=0, tiled=True),
        lax.psum_scatter(attn_terms[5], "grp", scatter_dimension=0, tiled=True),
    )
    attn_sums = (
        lax.psum_scatter(outer_sums[0], "ep", scatter_dimension=0, tiled=True),
        lax.psum_scatter(outer_sums[1], "ep", scatter_dimension=0, tiled=True),
        lax.psum_scatter(outer_sums[2], "ep", scatter_dimension=0, tiled=True),
        lax.psum_scatter(outer_sums[3], "ep", scatter_dimension=0, tiled=True),
        lax.psum_scatter(outer_sums[4], "ep", scatter_dimension=0, tiled=True),
        lax.psum_scatter(outer_sums[5], "ep", scatter_dimension=0, tiled=True),
    )
    return (
        result.astype(jnp.bfloat16),
        input_grad,
        attn_sums[0],
        attn_sums[1],
        attn_sums[2],
        attn_sums[3],
        attn_sums[4],
        attn_sums[5],
        gain_one_sum,
        gain_two_sum,
        up_one_sum,
        down_one_sum,
        up_two_sum,
        down_two_sum,
        rms_values,
    )


def fast_shards(
    inputs,
    attn_gain,
    w_query,
    w_key,
    w_value,
    w_output,
    centroids,
    norm1_gain,
    norm2_gain,
    up_first,
    down_first,
    up_second,
    down_second,
    routes,
    prefix,
    cotangent,
):
    zs = lax.axis_size("grp") // 4
    group_total = lax.axis_size("grp")
    ep_size = lax.axis_size("ep")
    per = w_query.shape[0]
    tokens, width = inputs.shape
    extra = jnp.concatenate([attn_gain[None, :], centroids.T], axis=0)
    extra = jnp.pad(extra, ((0, 16 - extra.shape[0]), (0, 128 - per)))
    full = gather_weights(zs, [w_query, w_key, w_value, w_output, extra])
    mats = [f.reshape(width, width) for f in full[:4]]
    extras = full[4].reshape(width // per, 16, 128)[:, :3, :per].transpose(1, 0, 2).reshape(3, width)
    gain, cents = extras[0:1], extras[1:3]
    attn_in, queries, keys, values, context, hidden, gate, pick, slot_rows, slot_grads, branch_sq = attend(
        HEADS, inputs, gain, *mats, cents, routes, prefix, cotangent
    )

    def swap(rows):
        return lax.all_to_all(
            rows.reshape(ep_size, tokens, width), "ep", split_axis=0, concat_axis=0, tiled=True
        ).reshape(ep_size * tokens, width)

    rows = swap(slot_rows)
    grads = swap(slot_grads)
    gain1, gain2 = norm1_gain, norm2_gain
    weights = (up_first, down_first, up_second, down_second)
    in_one, in_two, act_one, slope_one, act_two, slope_two, middle, delta, sub_sq = expert_forward(
        rows, gain1, gain2, *weights
    )
    pieces = lambda a: a.reshape(ep_size, tokens, width)
    reduced = backward_step(
        zs,
        HEADS,
        [inputs, attn_in, queries, keys, values, context, cotangent, hidden, pick, *mats],
        [act_one, act_two, slope_one, slope_two, pieces(in_one), pieces(in_two), pieces(grads), pieces(rows),
         pieces(delta), middle, *weights],
        [gain, cents, gain1, gain2, gate, routes, branch_sq, sub_sq],
        prefix.reshape(1, 1),
    )
    result, input_grad = reduced[7:9]
    down_two_sum, up_two_sum, down_one_sum, up_one_sum = (reduced[0][i] for i in range(4))
    query_sum, key_sum, value_sum, output_sum = reduced[1:5]
    grp_sum, all_sum = reduced[5], reduced[6]
    grp_at = lax.axis_index("grp") * (width // group_total)
    all_at = (lax.axis_index("grp") * ep_size + lax.axis_index("ep")) * per
    gains = lax.dynamic_slice(grp_sum, (0, grp_at), (2, width // group_total))
    outer = lax.dynamic_slice(all_sum, (0, all_at), (5, per))
    cell_count = float(tokens * width * group_total * ep_size)
    rms_values = jnp.sqrt(jnp.sum(all_sum[5:9], axis=1) / cell_count)
    return (
        result,
        input_grad,
        outer[2],
        query_sum,
        key_sum,
        value_sum,
        output_sum,
        outer[3:5].T,
        gains[0:1],
        gains[1:2],
        up_one_sum.T[None],
        down_one_sum[None],
        up_two_sum.T[None],
        down_two_sum[None],
        rms_values,
    )


def solution(mesh):
    fast = mesh.shape["ep"] == 2 and mesh.shape["grp"] == 16
    in_specs = (
        P(("grp", "ep"), None),
        P(("grp", "ep")),
        P(("grp", "ep"), None),
        P(("grp", "ep"), None),
        P(("grp", "ep"), None),
        P(("grp", "ep"), None),
        P(("grp", "ep"), None),
        P("ep", None),
        P("ep", None),
        P("ep", None, None),
        P("ep", None, None),
        P("ep", None, None),
        P("ep", None, None),
        P(("grp", "ep"), None),
        P(("grp", "ep")),
        P(("grp", "ep"), None),
    )
    out_specs = (
        P(("grp", "ep"), None),
        P(("grp", "ep"), None),
        P(("grp", "ep")),
        P(("grp", "ep"), None),
        P(("grp", "ep"), None),
        P(("grp", "ep"), None),
        P(("grp", "ep"), None),
        P(("grp", "ep"), None),
        P("ep", "grp"),
        P("ep", "grp"),
        P("ep", None, "grp"),
        P("ep", "grp", None),
        P("ep", None, "grp"),
        P("ep", "grp", None),
        P(),
    )
    return jax.shard_map(fast_shards if fast else shards, mesh=mesh, in_specs=in_specs, out_specs=out_specs, check_vma=False)
```

```python
import functools

import jax
import jax.numpy as jnp
from jax import lax
from jax.experimental import pallas as pl
from jax.experimental.pallas import tpu as pltpu
from jax.sharding import PartitionSpec as P

HEADS = 16


EPSILON = 1e-05
SQRT_HALF = 0.7071067811865476
INV_ROOT_TWO_PI = 0.3989422804014327
HIGH = lax.Precision.HIGHEST
HALF_LOG2E = -0.7213475204444817
ERF_P = 0.3275911 * SQRT_HALF
ERF_A1 = 0.5 * 0.254829592
ERF_A2 = 0.5 * -0.284496736
ERF_A3 = 0.5 * 1.421413741
ERF_A4 = 0.5 * -1.453152027
ERF_A5 = 0.5 * 1.061405429


def norm_parts(rows_in):
    center = rows_in - jnp.mean(rows_in, axis=-1, keepdims=True)
    inverse = lax.rsqrt(jnp.mean(center * center, axis=-1, keepdims=True) + EPSILON)
    return (center * inverse, inverse)


def norm_back(grad_normed, normed, inverse):
    mean_grad = jnp.mean(grad_normed, axis=-1, keepdims=True)
    mean_dot = jnp.mean(grad_normed * normed, axis=-1, keepdims=True)
    return inverse * (grad_normed - mean_grad - normed * mean_dot)


def gelu_slope(preact):
    return (
        0.5 * (1.0 + jax.scipy.special.erf(preact * SQRT_HALF))
        + preact * jnp.exp(-0.5 * preact * preact) * INV_ROOT_TWO_PI
    )


def matmul(left_side, right_side):
    return jnp.dot(left_side, right_side, preferred_element_type=jnp.float32)


def dot_first(left_side, right_side):
    return lax.dot_general(
        left_side, right_side, (((0,), (0,)), ((), ())), preferred_element_type=jnp.float32
    )


def dot_last(left_side, right_side):
    return lax.dot_general(
        left_side, right_side, (((1,), (1,)), ((), ())), preferred_element_type=jnp.float32
    )


def visible_mask(row_start, row_count, key_count, prefix_len):
    row_ids = row_start + jnp.arange(row_count, dtype=jnp.int32)[:, None]
    col_ids = jnp.arange(key_count, dtype=jnp.int32)[None, :]
    return (col_ids <= row_ids) | (col_ids < prefix_len)


def fill_slots(rows_in, target, slot_total):
    return jnp.zeros((slot_total, rows_in.shape[1]), rows_in.dtype).at[target].set(rows_in)


MESH = pl.DeviceIdType.MESH
VMEM_CAP = 66 * 1000 * 1000


def place(zs):
    grp = lax.axis_index("grp")
    ep = lax.axis_index("ep")
    core = lax.rem(grp, 2)
    x = lax.rem(lax.div(grp, 2), 2)
    z = lax.div(grp, 4)
    return z, x, core, ep


def device(z, x, core, ep):
    return ((z * 2 + x) * 2 + core, ep)


def greet(peers):
    barrier = pltpu.get_barrier_semaphore()
    for peer in peers:
        pl.semaphore_signal(barrier, inc=1, device_id=peer, device_id_type=MESH)
    pl.semaphore_wait(barrier, len(peers))


def push(src, dst, send_sem, recv_sem, peer):
    return pltpu.make_async_remote_copy(
        src_ref=src, dst_ref=dst, send_sem=send_sem, recv_sem=recv_sem, device_id=peer, device_id_type=MESH
    )


def gather_kernel(zs, *refs):
    shard = refs[0:5]
    full = refs[5:10]
    own_sem, z_send, z_recv, p_send, p_recv, c_send, c_recv = refs[10:]
    z, x, core, ep = place(zs)
    right = device(jnp.minimum(z + 1, zs - 1), x, core, ep)
    left = device(jnp.maximum(z - 1, 0), x, core, ep)
    x_peer = device(z, 1 - x, core, ep)
    y_peer = device(z, x, core, 1 - ep)
    c_peer = device(z, x, 1 - core, ep)
    others = [device(lax.rem(z + k, zs), x, core, ep) for k in range(1, zs)]
    half = shard[0].shape[1] // 2
    items = []
    for w in range(4):
        items.append((w, slice(0, half), True))
        items.append((w, slice(half, 2 * half), False))
    items.append((4, slice(0, shard[4].shape[1]), True))
    count = len(items)

    def own(i):
        w, cols, _ = items[i]
        return pltpu.make_async_copy(shard[w].at[:, cols], full[w].at[z, x, core, ep, :, cols], own_sem.at[i])

    def z_copy(i, src, slot, way, hop, peer):
        w, cols, _ = items[i]
        return push(src, full[w].at[slot, x, core, ep, :, cols], z_send.at[i, way, hop], z_recv.at[i, way, hop], peer)

    def z_start(i):
        w, cols, _ = items[i]

        @pl.when(z < zs - 1)
        def _():
            z_copy(i, shard[w].at[:, cols], z, 0, 0, right).start()

        @pl.when(z > 0)
        def _():
            z_copy(i, shard[w].at[:, cols], z, 1, 0, left).start()

    def z_hop(i, hop):
        w, cols, _ = items[i]
        low = jnp.maximum(z - hop, 0)
        high = jnp.minimum(z + hop, zs - 1)
        from_left = full[w].at[low, x, core, ep, :, cols]
        from_right = full[w].at[high, x, core, ep, :, cols]

        @pl.when(z >= hop)
        def _():
            z_copy(i, from_left, low, 0, hop - 1, right).wait_recv()

        if hop < zs - 1:
            @pl.when((z >= hop) & (z < zs - 1))
            def _():
                z_copy(i, from_left, low, 0, hop, right).start()

        @pl.when(z + hop <= zs - 1)
        def _():
            z_copy(i, from_right, high, 1, hop - 1, left).wait_recv()

        if hop < zs - 1:
            @pl.when((z + hop <= zs - 1) & (z > 0))
            def _():
                z_copy(i, from_right, high, 1, hop, left).start()

    def z_drain(i):
        w, cols, _ = items[i]
        for hop in range(zs - 1):
            src = full[w].at[z, x, core, ep, :, cols]

            @pl.when((z < zs - 1) & (z >= hop))
            def _():
                z_copy(i, src, z, 0, hop, right).wait_send()

            @pl.when((z > 0) & (z + hop <= zs - 1))
            def _():
                z_copy(i, src, z, 1, hop, left).wait_send()

    def second(i):
        w, cols, x_first = items[i]
        part = full[w].at[:, x, core, ep, :, cols]
        return push(part, part, p_send.at[i, 0], p_recv.at[i, 0], x_peer if x_first else y_peer)

    def third(i):
        w, cols, x_first = items[i]
        part = full[w].at[:, :, core, ep, :, cols] if x_first else full[w].at[:, x, core, :, :, cols]
        return push(part, part, p_send.at[i, 1], p_recv.at[i, 1], y_peer if x_first else x_peer)

    def fourth(i):
        w, cols, _ = items[i]
        part = full[w].at[:, :, core, :, :, cols]
        return push(part, part, c_send.at[i], c_recv.at[i], c_peer)

    greet(others + [x_peer, y_peer, c_peer])
    for i in range(count):
        z_start(i)
    for i in range(count):
        own(i).start()
    order = [[8, 0, 1], [2, 3], [4, 5], [6, 7]]
    for t in range(len(order) + 2):
        if t < len(order):
            for hop in range(1, zs):
                for i in order[t]:
                    z_hop(i, hop)
            for i in order[t]:
                own(i).wait()
                second(i).start()
        if 1 <= t < len(order) + 1:
            for i in order[t - 1]:
                second(i).wait_recv()
                third(i).start()
        if t >= 2:
            for i in order[t - 2]:
                third(i).wait_recv()
                fourth(i).start()
    for i in range(count):
        fourth(i).wait_recv()
    for i in range(count):
        z_drain(i)
        second(i).wait_send()
        third(i).wait_send()
        fourth(i).wait_send()


def gather_weights(zs, shards):
    shapes = [jax.ShapeDtypeStruct((zs, 2, 2, 2) + s.shape, s.dtype) for s in shards]
    n = 2 * len(shards) - 1
    dma = pltpu.SemaphoreType.DMA
    return pl.pallas_call(
        functools.partial(gather_kernel, zs),
        out_shape=shapes,
        in_specs=[pl.BlockSpec(memory_space=pltpu.VMEM)] * len(shards),
        out_specs=[pl.BlockSpec(memory_space=pl.ANY)] * len(shards),
        scratch_shapes=[dma((n,)), dma((n, 2, zs)), dma((n, 2, zs)), dma((n, 2)), dma((n, 2)), dma((n,)), dma((n,))],
        compiler_params=pltpu.CompilerParams(collective_id=1, has_side_effects=True, vmem_limit_bytes=VMEM_CAP),
        name="gather_weights",
    )(*shards)


def layer_norm(v):
    center = v - jnp.mean(v, axis=-1, keepdims=True)
    inverse = lax.rsqrt(jnp.mean(center * center, axis=-1, keepdims=True) + EPSILON)
    return center * inverse, inverse


def gelu_pair(v):
    tail = jnp.exp2(v * v * HALF_LOG2E)
    t = 1.0 / (1.0 + ERF_P * jnp.abs(v))
    poly = ((((ERF_A5 * t + ERF_A4) * t + ERF_A3) * t + ERF_A2) * t + ERF_A1) * t
    upper = poly * tail
    phi = jnp.where(v >= 0.0, 1.0 - upper, upper)
    return v * phi, phi + v * (tail * INV_ROOT_TWO_PI)


def expert_forward_kernel(tiles, slots, slot_grads, gain1, gain2, up1, down1, up2, down2, in1, in2, act1, slope1, act2, slope2, middle, delta, sums, rows, grads, acc, sub, near, stage, send_sem, recv_sem, copy_sem):
    layer = pl.program_id(0)
    t = pl.program_id(1)
    bf, f32 = jnp.bfloat16, jnp.float32
    z, x, core, ep = place(0)
    y_peer = device(z, x, core, 1 - ep)
    count = near.shape[1]

    def far_rows():
        return push(slots.at[1], rows.at[1], send_sem.at[0], recv_sem.at[0], y_peer)

    def far_grads():
        return push(slot_grads.at[1], grads.at[1], send_sem.at[1], recv_sem.at[1], y_peer)

    def copy(src, dst, i):
        return pltpu.make_async_copy(src, dst, copy_sem.at[i])

    def norm_rows(half):
        normed, _ = layer_norm(near[half].astype(f32))
        in1[half * count : (half + 1) * count] = (normed * gain1[...].astype(f32)).astype(bf)

    @pl.when((layer == 0) & (t == 0))
    def _():
        greet([y_peer])
        far_rows().start()
        far_grads().start()
        copy(slots.at[0], near.at[0], 0).start()
        copy(slot_grads.at[0], stage, 1).start()
        copy(slots.at[0], near.at[0], 0).wait()
        copy(slot_grads.at[0], stage, 1).wait()
        copy(near.at[0], rows.at[0], 0).start()
        copy(stage, grads.at[0], 1).start()
        norm_rows(0)

    @pl.when((layer == 1) & (t == 0))
    def _():
        copy(near.at[0], rows.at[0], 0).wait()
        copy(stage, grads.at[0], 1).wait()
        far_rows().wait()
        copy(rows.at[1], near.at[1], 0).start()
        copy(rows.at[1], near.at[1], 0).wait()
        norm_rows(1)

    def step(source, span, up, down, act, slope):
        pre = jnp.dot(source[span], up[0], preferred_element_type=f32)
        a, s = gelu_pair(pre)
        low = a.astype(bf)
        act[...] = low
        slope[...] = s.astype(bf)
        prod = jnp.dot(low, down[0], preferred_element_type=f32)

        @pl.when(t == 0)
        def _():
            acc[span] = prod

        @pl.when(t > 0)
        def _():
            acc[span] += prod

    for half in range(2):
        @pl.when(layer == half)
        def _():
            span = slice(half * count, (half + 1) * count)
            step(in1, span, up1, down1, act1, slope1)

            @pl.when(t == tiles - 1)
            def _():
                value = acc[span]
                sub[span] = value
                square = jnp.sum(value * value, axis=0, keepdims=True)
                if half == 0:
                    sums[0:1] = square
                else:
                    sums[0:1] += square
                mid = near[half].astype(f32) + value
                middle[span] = mid
                normed, _ = layer_norm(mid)
                in2[span] = (normed * gain2[...].astype(f32)).astype(bf)

    @pl.when(layer == 2)
    def _():
        step(in2, slice(0, 2 * count), up2, down2, act2, slope2)

        @pl.when(t == tiles - 1)
        def _():
            value = acc[...]
            sums[1:2] = jnp.sum(value * value, axis=0, keepdims=True)
            sums[2:8] = jnp.zeros((6, value.shape[1]), f32)
            delta[...] = (sub[...] + value).astype(bf)
            far_grads().wait()


def expert_forward(slots, slot_grads, gain1, gain2, up1, down1, up2, down2):
    _, count, feat = slots.shape
    n = 2 * count
    hidden = up1.shape[2]
    tile = 1024
    tiles = hidden // tile
    last = tiles - 1
    bf, f32 = jnp.bfloat16, jnp.float32
    shape = jax.ShapeDtypeStruct
    hbm = pl.BlockSpec(memory_space=pl.ANY)
    whole = lambda s: pl.BlockSpec(s, lambda l, t: (0,) * len(s))
    first = lambda l, t: jnp.where(l < 2, t, last)
    second = lambda l, t: jnp.where(l < 2, 0, t)
    up = lambda f: pl.BlockSpec((1, feat, tile), lambda l, t: (0, 0, f(l, t)))
    down = lambda f: pl.BlockSpec((1, tile, feat), lambda l, t: (0, f(l, t), 0))
    halves = pl.BlockSpec((count, tile), lambda l, t: (jnp.minimum(l, 1), first(l, t)))
    wide = pl.BlockSpec((n, tile), lambda l, t: (0, second(l, t)))
    dma = pltpu.SemaphoreType.DMA
    return pl.pallas_call(
        functools.partial(expert_forward_kernel, tiles),
        grid=(3, tiles),
        in_specs=[hbm, hbm, whole((1, feat)), whole((1, feat)), up(first), down(first), up(second), down(second)],
        out_specs=[whole((n, feat))] * 2 + [halves] * 2 + [wide] * 2 + [whole((n, feat))] * 2 + [whole((8, feat)), hbm, hbm],
        out_shape=[shape((n, feat), bf)] * 2
        + [shape((n, hidden), bf)] * 4
        + [shape((n, feat), f32), shape((n, feat), bf), shape((8, feat), f32)]
        + [shape((2, count, feat), bf)] * 2,
        scratch_shapes=[
            pltpu.VMEM((n, feat), f32),
            pltpu.VMEM((n, feat), f32),
            pltpu.VMEM((2, count, feat), bf),
            pltpu.VMEM((count, feat), bf),
            dma((2,)),
            dma((2,)),
            dma((2,)),
        ],
        compiler_params=pltpu.CompilerParams(
            collective_id=3, has_side_effects=True, vmem_limit_bytes=VMEM_CAP, dimension_semantics=("arbitrary", "arbitrary")
        ),
        name="expert_forward",
    )(slots, slot_grads, gain1, gain2, up1, down1, up2, down2)


def attend_kernel(heads, x, gain, wq, wk, wv, wo, cents, routes, prefix, cotangent, attn_in, queries, keys, values, context, hidden, gate, pick, slot_rows, slot_grads, sums, ctx):
    bf, f32 = jnp.bfloat16, jnp.float32
    tokens, feat = x.shape
    pair = 2 * feat // heads
    scale = (feat // heads) ** -0.5
    wide = x[...].astype(f32)
    normed, _ = layer_norm(wide)
    attn_in[...] = (normed * gain[...].astype(f32)).astype(bf)
    for w, out in ((wq, queries), (wk, keys), (wv, values)):
        out[...] = jnp.dot(attn_in[...], w[...], preferred_element_type=f32).astype(bf)
    row_ids = lax.broadcasted_iota(jnp.int32, (tokens, tokens), 0)
    col_ids = lax.broadcasted_iota(jnp.int32, (tokens, tokens), 1)
    visible = (col_ids <= row_ids) | (col_ids < prefix[0])
    low_half = lax.broadcasted_iota(jnp.int32, (tokens, pair), 1) < pair // 2
    last_dims = (((1,), (1,)), ((), ()))

    def body(h, carry):
        cols = pl.ds(pl.multiple_of(h * pair, pair), pair)
        q, k, v = queries[:, cols], keys[:, cols], values[:, cols]
        outs = []
        for side in (low_half, jnp.logical_not(low_half)):
            mine = jnp.where(side, q, jnp.zeros_like(q))
            s = lax.dot_general(mine, k, last_dims, preferred_element_type=f32) * scale
            s = jnp.where(visible, s, -1e30)
            top = jnp.max(s, axis=-1, keepdims=True)
            total = top + jnp.log(jnp.sum(jnp.exp(s - top), axis=-1, keepdims=True))
            p = jnp.exp(s - total).astype(bf)
            outs.append(jnp.dot(p, v, preferred_element_type=f32))
        ctx[:, cols] = jnp.where(low_half, outs[0], outs[1]).astype(bf)
        return carry

    lax.fori_loop(0, heads // 2, body, 0)
    context[...] = ctx[...]
    branch = jnp.dot(ctx[...], wo[...], preferred_element_type=f32)
    sums[...] = jnp.broadcast_to(jnp.sum(branch * branch, axis=0, keepdims=True), sums.shape)
    hid = wide + branch
    hidden[...] = hid
    low = hid.astype(bf)
    scores = lax.dot_general(low, cents[...], last_dims, preferred_element_type=f32)
    lane = lax.broadcasted_iota(jnp.int32, scores.shape, 1)
    hot = (lane == routes[...]).astype(f32)
    g = 1.0 / (1.0 + jnp.exp(-jnp.sum(scores * hot, axis=1, keepdims=True)))
    gate[...] = g
    tri = (col_ids <= row_ids).astype(bf)
    count = jnp.dot(tri, hot.astype(bf), preferred_element_type=f32)
    position = jnp.sum(count * hot, axis=1, keepdims=True) - 1.0
    away = (routes[...] != lax.axis_index("ep")).astype(jnp.int32)
    target = away * tokens + position.astype(jnp.int32)
    slots = lax.broadcasted_iota(jnp.int32, (tokens, 2 * tokens), 1)
    chosen = (slots == target).astype(bf)
    pick[...] = chosen
    first_dims = (((0,), (0,)), ((), ()))
    slot_rows[...] = lax.dot_general(chosen, low, first_dims, preferred_element_type=f32).astype(bf)
    grads = (g * cotangent[...].astype(f32)).astype(bf)
    slot_grads[...] = lax.dot_general(chosen, grads, first_dims, preferred_element_type=f32).astype(bf)


def attend(heads, x, gain, wq, wk, wv, wo, cents, routes, prefix, cotangent):
    tokens, feat = x.shape
    bf, f32 = jnp.bfloat16, jnp.float32
    shape = jax.ShapeDtypeStruct
    vm = pl.BlockSpec(memory_space=pltpu.VMEM)
    return pl.pallas_call(
        functools.partial(attend_kernel, heads),
        in_specs=[vm] * 8 + [pl.BlockSpec(memory_space=pltpu.SMEM), vm],
        out_specs=[vm] * 11,
        out_shape=[shape((tokens, feat), bf)] * 5
        + [shape((tokens, feat), f32), shape((tokens, 1), f32), shape((tokens, 2 * tokens), bf)]
        + [shape((2 * tokens, feat), bf)] * 2
        + [shape((8, feat), f32)],
        scratch_shapes=[pltpu.VMEM((tokens, feat), bf)],
        compiler_params=pltpu.CompilerParams(vmem_limit_bytes=VMEM_CAP),
        name="attend",
    )(x, gain, wq, wk, wv, wo, cents, routes, prefix, cotangent)


SLICES = 4
X_SLICES = 1
LEAD = 2
LAG = 3
RING = 8


def step_kernel(zs, heads, *refs):
    (x_ref, attn_in_ref, q_ref, k_ref, v_ref, context_ref, cot_ref, hidden_ref, pick_ref, wq, wk, wv, wo) = refs[0:13]
    (act_one, act_two, slope_one, slope_two, in_one, in_two, grads, rows_ref, delta, middle, up1, down1, up2, down2) = refs[13:27]
    gain, cents, gain1, gain2, gate, routes, branch_sq, sub_sq, prefix = refs[27:36]
    out_w = refs[36]
    out_a = refs[37:41]
    small_grp, small_all, result, input_grad = refs[41:45]
    pre_two, pre_one, sub_grad, row_grad, wide_far, narrow_far, attn_far, back_far, grad_far = refs[45:54]
    (send, xrecv, zrecv, acc, tiles, sides, prod, ep_in, x_in, z_in, small_in, small_ref) = refs[54:66]
    (wd, wu, sl, ps, hb, accf, midf, loadf, picks) = refs[66:75]
    (wf_s, wf_r, nf_s, nf_r, xs, xr, zsem_s, zsem_r, es, er, axs, axr, azs, azr, ss, sr, tile_sem, side_sem) = refs[75:93]
    (af_s, af_r, y_s, y_r, w_sem, ps_sem, ld_sem, out_sem, free_sem) = refs[93:]
    wide = (act_two, pre_two, act_one, pre_one)
    narrow = (grads, in_two, sub_grad, in_one)
    bf, f32 = jnp.bfloat16, jnp.float32
    z, x, core, ep = place(zs)
    tokens, feat = x_ref.shape
    rows = 2 * tokens
    hidden = act_one.shape[1]
    chunk = out_w.shape[1]
    per = prod.shape[4]
    blocks = 4 * zs
    size = chunk // SLICES
    right = device(jnp.minimum(z + 1, zs - 1), x, core, ep)
    left = device(jnp.maximum(z - 1, 0), x, core, ep)
    x_peer = device(z, 1 - x, core, ep)
    y_peer = device(z, x, core, 1 - ep)
    c_peer = device(z, x, 1 - core, ep)
    others = [device(lax.rem(z + k, zs), x, core, ep) for k in range(1, zs)]
    contract0 = (((0,), (0,)), ((), ()))
    last_dims = (((1,), (1,)), ((), ()))

    def dest(k):
        to_right = zs - 1 - z
        lower = jnp.where(k < to_right, zs - 1 - k, k - to_right)
        upper = jnp.where(k < z, k, zs - 1 - (k - z))
        return jnp.where(k < zs - 1, jnp.where(z < zs // 2, lower, upper), z)

    def begins(d):
        return ((d > z) & (z == 0)) | ((d < z) & (z == zs - 1))

    def loads(pairs, at=0):
        return [pltpu.make_async_copy(src, dst, ld_sem.at[at + i]) for i, (src, dst) in enumerate(pairs)]

    def begin(copies):
        for c in copies:
            c.start()

    def end(copies):
        for c in copies:
            c.wait()

    def fetch(pairs):
        copies = loads(pairs)
        begin(copies)
        end(copies)

    def two(slot):
        return hb.at[pl.ds(slot, 2)]

    def flat(slot):
        return hb[pl.ds(slot, 2)].reshape(rows, feat)

    greet(others + [x_peer, y_peer, c_peer])

    def far_wide(w, q):
        j = q * 2 + (1 - core)
        return push(
            wide[w].at[:, pl.ds(pl.multiple_of(j * chunk, chunk), chunk)], wide_far.at[w, q], wf_s.at[w], wf_r.at[w], c_peer
        )

    def far_narrow(w):
        return push(narrow[w], narrow_far.at[w], nf_s.at[w], nf_r.at[w], c_peer)

    def all_far(w):
        return push(wide_far.at[w], wide_far.at[w], wf_s.at[w], wf_r.at[w], c_peer)

    def send_wide(w):
        def send_far(q, carry):
            far_wide(w, q).start()
            return carry

        lax.fori_loop(0, 2 * zs, send_far, 0)

    def far_attn(i, src):
        return push(src, attn_far.at[i], af_s.at[i], af_r.at[i], c_peer)

    def far_delta():
        return push(delta.at[1], back_far, y_s.at[0], y_r.at[0], y_peer)

    def far_rows():
        return push(row_grad, grad_far, y_s.at[1], y_r.at[1], y_peer)

    far_narrow(0).start()
    send_wide(0)
    far_delta().start()
    far_narrow(1).start()
    far_narrow(3).start()
    far_attn(0, attn_in_ref).start()
    far_attn(1, context_ref).start()

    def load_tile(w, q, slot):
        j = q * 2 + core
        for i in range(4):
            @pl.when(w == i)
            def _():
                pltpu.make_async_copy(
                    wide[i].at[:, pl.ds(pl.multiple_of(j * chunk, chunk), chunk)],
                    tiles.at[slot, pl.ds(0, rows), :],
                    tile_sem.at[slot, 0],
                ).start()

        pltpu.make_async_copy(wide_far.at[w, q], tiles.at[slot, pl.ds(rows, rows), :], tile_sem.at[slot, 1]).start()

    def wait_tile(slot):
        for i in range(2):
            part = tiles.at[slot, pl.ds(i * rows, rows), :]
            pltpu.make_async_copy(part, part, tile_sem.at[slot, i]).wait()

    def load_side(w):
        slot = lax.rem(w, 2)
        for i in range(4):
            @pl.when(w == i)
            def _():
                pltpu.make_async_copy(narrow[i], sides.at[slot, pl.ds(0, 2)], side_sem.at[0]).start()

        pltpu.make_async_copy(narrow_far.at[w], sides.at[slot, pl.ds(2, 2)], side_sem.at[1]).start()

    def wait_side(w):
        slot = lax.rem(w, 2)
        for i in range(2):
            part = sides.at[slot, pl.ds(2 * i, 2)]
            pltpu.make_async_copy(part, part, side_sem.at[i]).wait()

    def product(w, slot):
        side = sides[lax.rem(w, 2)].reshape(2 * rows, feat)
        return lax.dot_general(tiles[slot], side, contract0, preferred_element_type=f32)

    def span(s):
        return pl.ds(pl.multiple_of(s * size, size), size)

    def x_copy(b, s):
        wide_size = chunk // X_SLICES
        at = pl.ds(pl.multiple_of(s * wide_size, wide_size), wide_size)
        return push(send.at[lax.rem(b, RING), at, :], xrecv.at[lax.rem(b, RING), at, :], xs.at[b, s], xr.at[b, s], x_peer)

    def z_copy(b, s):
        w = lax.div(b, zs)
        d = dest(lax.rem(b, zs))
        to_right = d > z
        nxt = jnp.where(to_right, z + 1, z - 1)
        slot = jnp.where(d != nxt, d, jnp.where(to_right, d, zs))
        return push(
            send.at[lax.rem(b, RING), span(s), :], zrecv.at[w, slot, span(s), :], zsem_s.at[b, s],
            zsem_r.at[w, slot, s], device(nxt, x, core, ep),
        )

    def z_wait(w, slot, s):
        ref = zrecv.at[w, slot, span(s), :]
        push(ref, ref, zsem_s.at[0, s], zsem_r.at[w, slot, s], x_peer).wait_recv()
        return ref[...].astype(f32)

    def z_sent(b):
        @pl.when(lax.rem(b, zs) < zs - 1)
        def _():
            for s in range(SLICES):
                z_copy(b, s).wait_send()

    def q_first(b):
        return dest(lax.rem(b, zs)) * 2 + (1 - x)

    def q_second(b):
        return dest(lax.rem(b, zs)) * 2 + x

    def far_wait(w):
        for i in range(4):
            @pl.when(w == i)
            def _():
                far_narrow(i).wait_recv()
                all_far(i).wait_recv()

    def stage_one(b):
        w = lax.div(b, zs)
        slot = lax.rem(b, 2)

        @pl.when(lax.rem(b, zs) == 0)
        def _():
            far_wait(w)
            load_side(w)
            load_tile(w, q_first(b), slot)
            wait_side(w)

        wait_tile(slot)

        @pl.when(lax.rem(b, zs) < zs - 1)
        def _():
            load_tile(w, q_first(b + 1), 1 - slot)

        @pl.when(b >= RING)
        def _():
            z_sent(b - RING)

        send[lax.rem(b, RING)] = product(w, slot).astype(bf)

    def stage_two(b):
        w = lax.div(b, zs)
        d = dest(lax.rem(b, zs))
        slot = 2 + lax.rem(b, 2)
        mine = lax.rem(b, RING)
        wait_tile(slot)

        @pl.when(b + 1 < blocks)
        def _():
            load_tile(lax.div(b + 1, zs), q_second(b + 1), 5 - slot)

        keep = lax.rem(b, LAG + 1)
        acc[keep] = product(w, slot)

        def piece(s, carry):
            sp = span(s)
            per_x = SLICES // X_SLICES

            @pl.when(lax.rem(s, per_x) == 0)
            def _():
                x_copy(b, lax.div(s, per_x)).wait()

            total = acc[keep, sp, :] + xrecv[mine, sp, :].astype(f32)
            acc[keep, sp, :] = total

            @pl.when(begins(d))
            def _():
                send[mine, sp, :] = total.astype(bf)

            return carry

        lax.fori_loop(0, SLICES, piece, 0)

        @pl.when(b < blocks - RING)
        def _():
            pl.semaphore_signal(free_sem, inc=1, device_id=x_peer, device_id_type=MESH)

        @pl.when(begins(d))
        def _():
            for s in range(SLICES):
                z_copy(b, s).start()

    def stage_three(b):
        w = lax.div(b, zs)
        d = dest(lax.rem(b, zs))
        mine = lax.rem(b, RING)
        keep = lax.rem(b, LAG + 1)

        @pl.when((d != z) & jnp.logical_not(begins(d)))
        def _():
            def piece(s, carry):
                sp = span(s)
                send[mine, sp, :] = (acc[keep, sp, :] + z_wait(w, d, s)).astype(bf)

                @pl.when(s > 0)
                def _():
                    z_copy(b, s - 1).start()

                return carry

            lax.fori_loop(0, SLICES, piece, 0)
            z_copy(b, SLICES - 1).start()

        @pl.when(d == z)
        def _():
            def piece(s, carry):
                sp = span(s)
                acc[keep, sp, :] += z_wait(w, jnp.where(z > 0, z, zs), s)

                @pl.when((z > 0) & (z < zs - 1))
                def _():
                    acc[keep, sp, :] += z_wait(w, zs, s)

                return carry

            lax.fori_loop(0, SLICES, piece, 0)
            copy = pltpu.make_async_copy(acc.at[keep], out_w.at[w], out_sem)
            copy.start()
            copy.wait()

    tile = wd.shape[1]

    def stream(source, start, count, up, down, slope, pre, low_step, high_step):
        def copies(t, slot):
            cols = pl.ds(pl.multiple_of(t * tile, tile), tile)
            return (
                pltpu.make_async_copy(down.at[0, cols, :], wd.at[slot], w_sem.at[slot, 0]),
                pltpu.make_async_copy(up.at[0, :, cols], wu.at[slot], w_sem.at[slot, 1]),
                pltpu.make_async_copy(slope.at[pl.ds(start, count), cols], sl.at[slot, pl.ds(0, count), :], w_sem.at[slot, 2]),
            )

        def out(t, slot):
            cols = pl.ds(pl.multiple_of(t * tile, tile), tile)
            return pltpu.make_async_copy(ps.at[slot, pl.ds(0, count), :], pre.at[pl.ds(start, count), cols], ps_sem.at[slot])

        for c in copies(low_step, low_step % 2):
            c.start()

        def body(t, carry):
            slot = lax.rem(t, 2)
            for c in copies(t, slot):
                c.wait()

            @pl.when(t + 1 < high_step)
            def _():
                for c in copies(t + 1, 1 - slot):
                    c.start()

            g = lax.dot_general(source(), wd[slot], last_dims, preferred_element_type=f32)
            low = (g * sl[slot, 0:count].astype(f32)).astype(bf)

            @pl.when(t >= low_step + 2)
            def _():
                out(t - 2, slot).wait()

            ps[slot, 0:count] = low
            out(t, slot).start()
            value = lax.dot_general(low, wu[slot], last_dims, preferred_element_type=f32)

            @pl.when(t == 0)
            def _():
                accf[0:count] = value

            @pl.when(t > 0)
            def _():
                accf[0:count] += value

            return carry

        lax.fori_loop(low_step, high_step, body, 0)
        for t in range(high_step - 2, high_step):
            out(t, t % 2).wait()

    part = 64

    def norm_parts_of(value, g, gain_row):
        normed, inverse = layer_norm(value)
        total = jnp.sum(g * normed, axis=0, keepdims=True)
        q = g * gain_row
        mean_q = jnp.mean(q, axis=-1, keepdims=True)
        mean_dot = jnp.mean(q * normed, axis=-1, keepdims=True)
        return total, inverse * (q - mean_q - normed * mean_dot)

    steps = hidden // tile
    part_loads = loads(
        [
            (cot_ref, hb.at[1]),
            (attn_in_ref, hb.at[0]),
            (q_ref, hb.at[12]),
            (k_ref, hb.at[13]),
            (v_ref, hb.at[14]),
            (x_ref, hb.at[11]),
            (hidden_ref, loadf.at[pl.ds(0, tokens)]),
            (pick_ref, picks),
        ]
    )
    late_loads = loads(
        [
            (delta.at[0], hb.at[3]),
            (context_ref, hb.at[2]),
            (wo.at[pl.ds(0, feat // 2)], wd.at[0]),
            (wo.at[pl.ds(feat // 2, feat // 2)], wd.at[1]),
            (back_far, hb.at[5]),
        ],
        8,
    )
    expert_loads = loads([(middle, loadf), (rows_ref, two(2))], 14)

    def event_second_start():
        fetch([(grads, two(0))])
        begin(expert_loads)
        stream(lambda: flat(0), 0, rows, up2, down2, slope_two, pre_two, 0, steps // 2)

    def event_second_end():
        stream(lambda: flat(0), 0, rows, up2, down2, slope_two, pre_two, steps // 2, steps)
        send_wide(1)
        end(expert_loads)
        small_ref[...] = jnp.zeros_like(small_ref)
        gain_row = gain2[...].astype(f32)
        per_block = tokens // part

        def body(i, carry):
            at = pl.ds(pl.multiple_of(i * part, part), part)
            total, value = norm_parts_of(loadf[at], accf[at], gain_row)
            small_ref[1:2] += total
            midf[at] = value
            blk = lax.div(i, per_block)
            sub = pl.ds(pl.multiple_of(lax.rem(i, per_block) * part, part), part)
            hb[4 + blk, sub] = (hb[blk, sub].astype(f32) + value).astype(bf)
            return carry

        lax.fori_loop(0, rows // part, body, 0)
        fetch([(two(4), sub_grad)])
        far_narrow(2).start()
        send_wide(2)
        begin(part_loads)

    def first_stream(blk, low_step, high_step):
        start = blk * tokens
        stream(lambda: hb[4 + blk], start, tokens, up1, down1, slope_one, pre_one, low_step, high_step)

    def first_norm(blk):
        gain_row = gain1[...].astype(f32)

        def body(i, carry):
            at = pl.ds(pl.multiple_of(i * part, part), part)
            value = hb[2 + blk, at].astype(f32)
            total, back = norm_parts_of(value, accf[at], gain_row)
            small_ref[0:1] += total
            mid = midf[pl.ds(pl.multiple_of(blk * tokens + i * part, part), part)]
            hb[6 + blk, at] = (back + mid).astype(bf)
            return carry

        lax.fori_loop(0, tokens // part, body, 0)

    def event_far_start():
        first_stream(1, 0, steps // 2)

    def event_far_end():
        first_stream(1, steps // 2, steps)
        first_norm(1)
        fetch_out = pltpu.make_async_copy(hb.at[7], row_grad, out_sem)
        fetch_out.start()
        fetch_out.wait()
        far_rows().start()

    def event_own_start():
        first_stream(0, 0, steps // 2)

    def event_own_end():
        first_stream(0, steps // 2, steps)
        first_norm(0)
        send_wide(3)
        far_delta().wait_recv()
        begin(late_loads)

    half = feat // 2

    def event_combine():
        far_rows().wait_recv()
        row_load = pltpu.make_async_copy(grad_far, hb.at[9], out_sem)
        row_load.start()
        end(part_loads)
        end(late_loads)
        row_load.wait()
        c = cents[...].astype(f32)

        def combine(i, carry):
            at = pl.ds(pl.multiple_of(i * part, part), part)
            own = picks[at, 0:tokens]
            far = picks[at, tokens : 2 * tokens]
            returned = jnp.dot(own, hb[3], preferred_element_type=f32) + jnp.dot(far, hb[5], preferred_element_type=f32)
            back = jnp.dot(own, hb[6], preferred_element_type=f32) + jnp.dot(far, hb[9], preferred_element_type=f32)
            g = gate[at]
            hid = loadf[at]
            res = hid + g * returned
            hb[15, at] = res.astype(bf)
            small_ref[5:6] += jnp.sum(res * res, axis=0, keepdims=True)
            grad_out = hb[1, at].astype(f32)
            grad_score = jnp.sum(grad_out * returned, axis=1, keepdims=True) * g * (1.0 - g)
            is_first = routes[at] == 0
            weighted = grad_score * hid.astype(bf).astype(f32)
            zero = jnp.zeros_like(weighted)
            small_ref[3:4] += jnp.sum(jnp.where(is_first, weighted, zero), axis=0, keepdims=True)
            small_ref[4:5] += jnp.sum(jnp.where(is_first, zero, weighted), axis=0, keepdims=True)
            grad_hidden = grad_out + grad_score * jnp.where(is_first, c[0:1], c[1:2]) + back
            midf[at] = grad_hidden
            hb[10, at] = grad_hidden.astype(bf)
            return carry

        lax.fori_loop(0, tokens // part, combine, 0)
        fetch([(hb.at[15], result)])
        for i in range(2):
            hb[15, :, i * half : (i + 1) * half] = lax.dot_general(
                hb[10], wd[i], last_dims, preferred_element_type=f32
            ).astype(bf)

    def event_heads(low_pair, high_pair):
        row_ids = lax.broadcasted_iota(jnp.int32, (tokens, tokens), 0)
        col_ids = lax.broadcasted_iota(jnp.int32, (tokens, tokens), 1)
        pair = 2 * feat // heads
        scale = (feat // heads) ** -0.5
        limit = prefix[...]

        def head(h, carry):
            visible = (col_ids <= row_ids) | (col_ids < limit)
            low_half = lax.broadcasted_iota(jnp.int32, (tokens, pair), 1) < pair // 2
            cols = pl.ds(pl.multiple_of(h * pair, pair), pair)
            q, k, v, gc = hb[12, :, cols], hb[13, :, cols], hb[14, :, cols], hb[15, :, cols]
            outs = []
            for side in (low_half, jnp.logical_not(low_half)):
                s = lax.dot_general(jnp.where(side, q, jnp.zeros_like(q)), k, last_dims, preferred_element_type=f32) * scale
                s = jnp.where(visible, s, -1e30)
                top = jnp.max(s, axis=-1, keepdims=True)
                total = top + jnp.log(jnp.sum(jnp.exp(s - top), axis=-1, keepdims=True))
                p = jnp.exp(s - total)
                gp = lax.dot_general(jnp.where(side, gc, jnp.zeros_like(gc)), v, last_dims, preferred_element_type=f32)
                dot = jnp.sum(gp * p, axis=-1, keepdims=True)
                gs = (p * (gp - dot)).astype(bf)
                outs.append(
                    (
                        jnp.dot(gs, k, preferred_element_type=f32),
                        lax.dot_general(gs, q, contract0, preferred_element_type=f32),
                        lax.dot_general(p.astype(bf), gc, contract0, preferred_element_type=f32),
                    )
                )
            hb[4, :, cols] = (jnp.where(low_half, outs[0][0], outs[1][0]) * scale).astype(bf)
            hb[6, :, cols] = (jnp.where(low_half, outs[0][1], outs[1][1]) * scale).astype(bf)
            hb[8, :, cols] = jnp.where(low_half, outs[0][2], outs[1][2]).astype(bf)
            return carry

        lax.fori_loop(low_pair, high_pair, head, 0)

    def event_inputs():
        order = [(m, i) for i in range(2) for m in (wq, wk, wv)]

        def weight_copy(n):
            m, i = order[n]
            return pltpu.make_async_copy(m.at[pl.ds(i * half, half)], wd.at[n % 2], w_sem.at[n % 2, 0])

        weight_copy(0).start()
        for n in range(6):
            weight_copy(n).wait()
            if n < 5:
                weight_copy(n + 1).start()
            value = lax.dot_general(hb[4 + 2 * (n % 3)], wd[n % 2], last_dims, preferred_element_type=f32)
            cols = slice((n // 3) * half, (n // 3 + 1) * half)
            if n % 3 == 0:
                accf[0:tokens, cols] = value
            else:
                accf[0:tokens, cols] += value
        for i in range(4):
            far_attn(2 + i, hb.at[4 + 2 * i]).start()
        gain_row = gain[...].astype(f32)

        def norms(i, carry):
            at = pl.ds(pl.multiple_of(i * part, part), part)
            total, value = norm_parts_of(hb[11, at].astype(f32), accf[at], gain_row)
            small_ref[2:3] += total
            midf[at] += value
            return carry

        lax.fori_loop(0, tokens // part, norms, 0)
        small_ref[6:7] = branch_sq[0:1]
        small_ref[7:9] = sub_sq[0:2]
        start0()

    def event_products():
        for i in range(6):
            far_attn(i, hb.at[0]).wait_recv()
        fetch(
            [(midf.at[pl.ds(0, tokens)], input_grad)]
            + [(attn_far.at[i], hb.at[2 * i + 1]) for i in range(6)]
        )
        step = 8 * per

        for w in range(4):
            lhs = 0 if w < 3 else 2
            rhs = 4 + 2 * w

            def form(m, carry):
                cols = pl.ds(pl.multiple_of(m * step, step), step)
                left_part = hb[pl.ds(lhs, 2), :, cols].reshape(rows, step)
                value = lax.dot_general(left_part, flat(rhs), contract0, preferred_element_type=f32)
                value = value.astype(bf).reshape(2, 2, 2 * per, feat)
                mine = jnp.where(core == 0, value[:, 0], value[:, 1])
                prod[w, m] = mine.reshape(2, 2, per, feat)
                return carry

            lax.fori_loop(0, zs, form, 0)
            if w > 0:
                attn_ep(w - 1).start()
        for i in range(6):
            far_attn(i, hb.at[0]).wait_send()
        attn_ep(3).start()

    def attn_ep(w):
        return push(prod.at[w, :, :, 1 - ep], ep_in.at[w], es.at[w], er.at[w], y_peer)

    def attn_x(w):
        return push(prod.at[w, :, 1 - x, ep], x_in.at[w], axs.at[w], axr.at[w], x_peer)

    def fold_ep(w):
        attn_ep(w).wait()

        def body(m, carry):
            for i in range(2):
                total = prod[w, m, i, ep].astype(f32) + ep_in[w, m, i].astype(f32)
                prod[w, m, i, ep] = total.astype(bf)
            return carry

        lax.fori_loop(0, zs, body, 0)

    def attn_z_copy(w, k):
        d = dest(k)
        to_right = d > z
        nxt = jnp.where(to_right, z + 1, z - 1)
        slot = jnp.where(d != nxt, d, jnp.where(to_right, d, zs))
        return push(prod.at[w, d, x, ep], z_in.at[w, slot], azs.at[w, k], azr.at[w, slot], device(nxt, x, core, ep))

    def attn_z_wait(w, slot):
        ref = z_in.at[w, slot]
        push(ref, ref, azs.at[w, 0], azr.at[w, slot], x_peer).wait_recv()
        return ref[...].astype(f32)

    def fold_x(w):
        attn_x(w).wait()

        def body(k, carry):
            d = dest(k)
            total = prod[w, d, x, ep].astype(f32) + x_in[w, d].astype(f32)
            prod[w, d, x, ep] = total.astype(bf)
            return carry

        lax.fori_loop(0, zs, body, 0)

    def fold_z(w):
        def body(k, carry):
            d = dest(k)

            @pl.when(jnp.logical_not(begins(d)))
            def _():
                total = prod[w, d, x, ep].astype(f32) + attn_z_wait(w, d)
                prod[w, d, x, ep] = total.astype(bf)

            attn_z_copy(w, k).start()
            return carry

        lax.fori_loop(0, zs - 1, body, 0)

    def last_z(w):
        first = jnp.where(z > 0, z, zs)
        out_a[w][...] = prod[w, z, x, ep].astype(f32) + attn_z_wait(w, first)

        @pl.when((z > 0) & (z < zs - 1))
        def _():
            out_a[w][...] += attn_z_wait(w, zs)

        for k in range(zs - 1):
            attn_z_copy(w, k).wait_send()

    def small_stage(stage, n, mine, peer_at, src):
        def copy(k):
            return push(src, small_in.at[stage, mine], ss.at[stage, k], sr.at[stage, k], peer_at(lax.rem(mine + k, n)))

        def start():
            for k in range(1, n):
                copy(k).start()

        def end():
            for k in range(1, n):
                copy(k).wait()
            small_in[stage, mine] = src[...]
            total = small_in[stage, 0]
            for i in range(1, n):
                total = total + small_in[stage, i]
            return total

        return start, end

    start0, end0 = small_stage(0, 2, core, lambda i: device(z, x, i, ep), small_ref)
    start1, end1 = small_stage(1, 2, x, lambda i: device(z, i, core, ep), small_in.at[3, 3])
    start2, end2 = small_stage(2, zs, z, lambda i: device(i, x, core, ep), small_in.at[3, 2])
    start3, end3 = small_stage(3, 2, ep, lambda i: device(z, x, core, i), small_grp)

    def event_x(w):
        def act():
            fold_ep(w)
            attn_x(w).start()

        return act

    def event_small1():
        small_in[3, 3] = end0()
        start1()

    def event_small2():
        small_in[3, 2] = end1()
        start2()

    def event_small3():
        small_grp[...] = end2()
        start3()

    def event_z(w):
        def act():
            fold_x(w)
            fold_z(w)

        return act

    def event_last():
        for w in range(4):
            last_z(w)
        small_all[...] = end3()

    pairs = heads // 2
    steps_at = [
        (1, event_second_start),
        (2, event_second_end),
        (3, event_far_start),
        (4, event_far_end),
        (5, event_own_start),
        (6, event_own_end),
        (7, event_combine),
        (8, lambda: event_heads(0, pairs // 2)),
        (9, lambda: event_heads(pairs // 2, pairs)),
        (10, event_inputs),
        (11, event_products),
        (11, event_small1),
        (12, event_small2),
        (13, event_small3),
    ]
    steps_at += [(12 + w, event_x(w)) for w in range(4)]
    steps_at += [(14 + w, event_z(w)) for w in range(4)]

    def pipeline(t, carry):
        @pl.when(t < blocks)
        def _():
            stage_one(t)

        @pl.when((t > 0) & (t <= blocks))
        def _():
            @pl.when(t - 1 >= RING)
            def _():
                pl.semaphore_wait(free_sem, 1)

            for s in range(X_SLICES):
                x_copy(t - 1, s).start()

        for at, action in steps_at:
            pl.when(t == at)(action)

        @pl.when(t == LEAD - 1)
        def _():
            load_tile(0, q_second(0), 2)

        @pl.when((t >= LEAD) & (t < blocks + LEAD))
        def _():
            stage_two(t - LEAD)

        late = t - LEAD - jnp.where((z == 0) | (z == zs - 1), LAG, LAG - 1)

        @pl.when((late >= 0) & (late < blocks))
        def _():
            stage_three(late)

        return carry

    lax.fori_loop(0, blocks + LEAD + LAG, pipeline, 0)
    event_last()

    def drain(b, carry):
        z_sent(b)
        return carry

    lax.fori_loop(blocks - RING, blocks, drain, 0)
    for w in range(4):
        far_narrow(w).wait_send()
        all_far(w).wait_send()
    far_delta().wait_send()
    far_rows().wait_send()


def backward_step(zs, heads, big, experts, little, prefix):
    x, hidden = big[0], experts[0].shape[1]
    tokens, feat = x.shape
    rows = 2 * tokens
    chunk = hidden // (4 * zs)
    per = feat // (8 * zs)
    f32, bf = jnp.float32, jnp.bfloat16
    shape = jax.ShapeDtypeStruct
    vm = pl.BlockSpec(memory_space=pltpu.VMEM)
    hbm = pl.BlockSpec(memory_space=pl.ANY)
    dma = pltpu.SemaphoreType.DMA
    outs = [shape((4, chunk, feat), f32)]
    outs += [shape((per, feat), f32)] * 4
    outs += [shape((16, feat), f32)] * 2
    outs += [shape((tokens, feat), bf), shape((tokens, feat), f32)]
    outs += [shape((rows, hidden), bf)] * 2 + [shape((2, tokens, feat), bf), shape((tokens, feat), bf)]
    outs += [shape((4, 2 * zs, rows, chunk), bf), shape((4, 2, tokens, feat), bf), shape((6, tokens, feat), bf)]
    outs += [shape((tokens, feat), bf)] * 2
    s = SLICES
    blocks = 4 * zs
    tile = 512
    vmem = pltpu.VMEM
    return pl.pallas_call(
        functools.partial(step_kernel, zs, heads),
        out_shape=outs,
        in_specs=[hbm] * 27 + [vm] * 9,
        out_specs=[hbm] + [vm] * 6 + [hbm] * 11,
        scratch_shapes=[
            vmem((RING, chunk, feat), bf),
            vmem((RING, chunk, feat), bf),
            vmem((4, zs + 1, chunk, feat), bf),
            vmem((LAG + 1, chunk, feat), f32),
            vmem((4, 2 * rows, chunk), bf),
            vmem((2, 4, tokens, feat), bf),
            vmem((4, zs, 2, 2, per, feat), bf),
            vmem((4, zs, 2, per, feat), bf),
            vmem((4, zs, per, feat), bf),
            vmem((4, zs + 1, per, feat), bf),
            vmem((4, max(zs, 4), 16, feat), f32),
            vmem((16, feat), f32),
            vmem((2, tile, feat), bf),
            vmem((2, feat, tile), bf),
            vmem((2, rows, tile), bf),
            vmem((2, rows, tile), bf),
            vmem((16, tokens, feat), bf),
            vmem((rows, feat), f32),
            vmem((rows, feat), f32),
            vmem((rows, feat), f32),
            vmem((tokens, rows), bf),
            dma((4,)), dma((4,)), dma((4,)), dma((4,)),
            dma((blocks, s)), dma((blocks, s)), dma((blocks, s)), dma((4, zs + 1, s)),
            dma((4,)), dma((4,)), dma((4,)), dma((4,)), dma((4, zs)), dma((4, zs + 1)),
            dma((4, zs)), dma((4, zs)), dma((4, 2)), dma((2,)),
            dma((6,)), dma((6,)), dma((2,)), dma((2,)), dma((2, 3)), dma((2,)), dma((16,)), dma, pltpu.SemaphoreType.REGULAR,
        ],
        compiler_params=pltpu.CompilerParams(collective_id=2, has_side_effects=True, vmem_limit_bytes=VMEM_CAP),
        name="backward_step",
    )(*big, *experts, *little, prefix)


def shards(
    inputs,
    attn_gain,
    w_query,
    w_key,
    w_value,
    w_output,
    centroids,
    norm1_gain,
    norm2_gain,
    up_first,
    down_first,
    up_second,
    down_second,
    routes,
    prefix,
    cotangent,
):
    gathered = (
        lax.all_gather(attn_gain, ("grp", "ep"), axis=0, tiled=True),
        lax.all_gather(w_query, ("grp", "ep"), axis=0, tiled=True),
        lax.all_gather(w_key, ("grp", "ep"), axis=0, tiled=True),
        lax.all_gather(w_value, ("grp", "ep"), axis=0, tiled=True),
        lax.all_gather(w_output, ("grp", "ep"), axis=0, tiled=True),
        lax.all_gather(centroids, ("grp", "ep"), axis=0, tiled=True),
    )
    gain_attn, query_mat, key_mat, value_mat, output_mat, centroid_mat = gathered
    token_count, feature_width = inputs.shape
    head_count = HEADS
    head_width = feature_width // head_count
    scale_factor = head_width ** (-0.5)
    block_rows = min(512, token_count)
    prefix_len = prefix[0]
    inputs_wide = inputs.astype(jnp.float32)
    normed_attn, inverse_attn = norm_parts(inputs_wide)
    gain_attn_wide = gain_attn.astype(jnp.float32)
    attn_in = (normed_attn * gain_attn_wide).astype(jnp.bfloat16)
    queries = (
        matmul(attn_in, query_mat).astype(jnp.bfloat16).reshape(token_count, head_count, head_width)
    )
    key_heads = (
        matmul(attn_in, key_mat).astype(jnp.bfloat16).reshape(token_count, head_count, head_width)
    )
    value_heads = (
        matmul(attn_in, value_mat).astype(jnp.bfloat16).reshape(token_count, head_count, head_width)
    )

    def block_scores(block_index):
        row_start = block_index * block_rows
        scores = (
            jnp.einsum("qhd,khd->hqk", queries, key_heads, preferred_element_type=jnp.float32)
            * scale_factor
        )
        visible = visible_mask(row_start, block_rows, token_count, prefix_len)
        return (queries, jnp.where(visible[None], scores, -1e30))

    block_index = 0
    query_block, scores = block_scores(block_index)
    row_max = jnp.max(scores, axis=-1, keepdims=True)
    expsum = jnp.sum(jnp.exp(scores - row_max), axis=-1, keepdims=True)
    log_total = row_max + jnp.log(expsum)
    probs_low = jnp.exp(scores - log_total).astype(jnp.bfloat16)
    context_parts = jnp.einsum(
        "hqk,khd->qhd", probs_low, value_heads, preferred_element_type=jnp.float32
    ).astype(jnp.bfloat16)
    lse_parts = [log_total]
    context = context_parts.reshape(token_count, feature_width)
    branch = matmul(context, output_mat)
    hidden = inputs_wide + branch
    hidden_low = hidden.astype(jnp.bfloat16)
    expert_total = lax.axis_size("ep")
    group_total = lax.axis_size("grp")
    capacity = 2 * token_count // expert_total
    route_ids = routes[:, 0]
    expert_ids = jnp.arange(expert_total, dtype=jnp.int32)
    route_hot = (route_ids[:, None] == expert_ids[None, :]).astype(jnp.int32)
    position = jnp.sum((jnp.cumsum(route_hot, axis=0) - 1) * route_hot, axis=1)
    target = route_ids * capacity + position
    route_weight = route_hot.astype(jnp.float32)
    all_scores = matmul(hidden_low, centroid_mat)
    gate_value = jax.nn.sigmoid(jnp.sum(all_scores * route_weight, axis=1))
    slot_rows = fill_slots(hidden_low, target, expert_total * capacity).reshape(
        expert_total, capacity, feature_width
    )
    received = lax.all_to_all(slot_rows, "ep", split_axis=0, concat_axis=0, tiled=True).reshape(
        expert_total * capacity, feature_width
    )
    gain_one = norm1_gain[0].astype(jnp.float32)
    gain_two = norm2_gain[0].astype(jnp.float32)
    up_one = up_first[0]
    down_one = down_first[0]
    up_two = up_second[0]
    down_two = down_second[0]
    rows_wide = received.astype(jnp.float32)
    normed_one, inverse_one = norm_parts(rows_wide)
    in_one = (normed_one * gain_one).astype(jnp.bfloat16)
    pre_one = matmul(in_one, up_one)
    act_one = jax.nn.gelu(pre_one, approximate=False).astype(jnp.bfloat16)
    sub_one = matmul(act_one, down_one)
    middle = rows_wide + sub_one
    normed_two, inverse_two = norm_parts(middle)
    in_two = (normed_two * gain_two).astype(jnp.bfloat16)
    pre_two = matmul(in_two, up_two)
    act_two = jax.nn.gelu(pre_two, approximate=False).astype(jnp.bfloat16)
    sub_two = matmul(act_two, down_two)
    delta = (sub_one + sub_two).astype(jnp.bfloat16).reshape(expert_total, capacity, feature_width)
    back_slots = lax.all_to_all(delta, "ep", split_axis=0, concat_axis=0, tiled=True).reshape(
        expert_total * capacity, feature_width
    )
    returned = back_slots[target].astype(jnp.float32)
    result = hidden + gate_value[:, None] * returned
    square_terms = jnp.stack(
        [
            jnp.sum(result * result),
            jnp.sum(branch * branch),
            jnp.sum(sub_one * sub_one),
            jnp.sum(sub_two * sub_two),
        ]
    )
    square_totals = lax.psum(square_terms, ("grp", "ep"))
    cell_count = float(token_count * feature_width * group_total * expert_total)
    rms_values = jnp.sqrt(square_totals / cell_count)
    grad_out = cotangent.astype(jnp.float32)
    grad_gate = jnp.sum(grad_out * returned, axis=1)
    grad_score = grad_gate * gate_value * (1.0 - gate_value)
    grad_delta_tok = (gate_value[:, None] * grad_out).astype(jnp.bfloat16)
    grad_slots = fill_slots(grad_delta_tok, target, expert_total * capacity).reshape(
        expert_total, capacity, feature_width
    )
    grad_sum = lax.all_to_all(grad_slots, "ep", split_axis=0, concat_axis=0, tiled=True).reshape(
        expert_total * capacity, feature_width
    )
    grad_pre_two = (dot_last(grad_sum, down_two) * gelu_slope(pre_two)).astype(jnp.bfloat16)
    grad_in_two = dot_last(grad_pre_two, up_two)
    grad_gain_two = jnp.sum(grad_in_two * normed_two, axis=0)
    grad_middle = norm_back(grad_in_two * gain_two, normed_two, inverse_two)
    grad_sub_one = (grad_sum.astype(jnp.float32) + grad_middle).astype(jnp.bfloat16)
    grad_pre_one = (dot_last(grad_sub_one, down_one) * gelu_slope(pre_one)).astype(jnp.bfloat16)
    grad_in_one = dot_last(grad_pre_one, up_one)
    grad_gain_one = jnp.sum(grad_in_one * normed_one, axis=0)
    grad_rows = (norm_back(grad_in_one * gain_one, normed_one, inverse_one) + grad_middle).astype(
        jnp.bfloat16
    )
    grad_back = lax.all_to_all(
        grad_rows.reshape(expert_total, capacity, feature_width),
        "ep",
        split_axis=0,
        concat_axis=0,
        tiled=True,
    ).reshape(expert_total * capacity, feature_width)
    grad_down_two = dot_first(act_two, grad_sum)
    grad_up_two = dot_first(in_two, grad_pre_two)
    grad_down_one = dot_first(act_one, grad_sub_one)
    grad_up_one = dot_first(in_one, grad_pre_one)
    expert_sums = (
        lax.psum_scatter(grad_up_one[None], "grp", scatter_dimension=2, tiled=True),
        lax.psum_scatter(grad_down_one[None], "grp", scatter_dimension=1, tiled=True),
        lax.psum_scatter(grad_up_two[None], "grp", scatter_dimension=2, tiled=True),
        lax.psum_scatter(grad_down_two[None], "grp", scatter_dimension=1, tiled=True),
        lax.psum_scatter(grad_gain_one[None], "grp", scatter_dimension=1, tiled=True),
        lax.psum_scatter(grad_gain_two[None], "grp", scatter_dimension=1, tiled=True),
    )
    up_one_sum, down_one_sum, up_two_sum, down_two_sum, gain_one_sum, gain_two_sum = expert_sums
    centroid_wide = centroid_mat.astype(jnp.float32)
    score_weight = route_weight * grad_score[:, None]
    grad_hidden = (
        grad_out
        + jnp.dot(score_weight, centroid_wide.T, precision=HIGH)
        + grad_back[target].astype(jnp.float32)
    )
    grad_centroid = lax.dot_general(
        hidden_low.astype(jnp.float32), score_weight, (((0,), (0,)), ((), ())), precision=HIGH
    )
    grad_branch = grad_hidden.astype(jnp.bfloat16)
    grad_output_mat = dot_first(context, grad_branch)
    grad_context = (
        dot_last(grad_branch, output_mat)
        .astype(jnp.bfloat16)
        .reshape(token_count, head_count, head_width)
    )
    block_index = 0
    query_block, scores = block_scores(block_index)
    probs_wide = jnp.exp(scores - lse_parts[block_index])
    probs_low = probs_wide.astype(jnp.bfloat16)
    row_start = block_index * block_rows
    grad_value_sum = jnp.einsum(
        "hqk,qhd->khd", probs_low, grad_context, preferred_element_type=jnp.float32
    )
    grad_probs = jnp.einsum(
        "qhd,khd->hqk", grad_context, value_heads, preferred_element_type=jnp.float32
    )
    row_dot = jnp.sum(grad_probs * probs_wide, axis=-1, keepdims=True)
    grad_scores = (probs_wide * (grad_probs - row_dot)).astype(jnp.bfloat16)
    grad_query_parts = (
        jnp.einsum("hqk,khd->qhd", grad_scores, key_heads, preferred_element_type=jnp.float32)
        * scale_factor
    ).astype(jnp.bfloat16)
    grad_key_sum = (
        jnp.einsum("hqk,qhd->khd", grad_scores, query_block, preferred_element_type=jnp.float32)
        * scale_factor
    )
    grad_queries = grad_query_parts.reshape(token_count, feature_width)
    grad_keys = grad_key_sum.astype(jnp.bfloat16).reshape(token_count, feature_width)
    grad_values = grad_value_sum.astype(jnp.bfloat16).reshape(token_count, feature_width)
    grad_query_mat = dot_first(attn_in, grad_queries)
    grad_key_mat = dot_first(attn_in, grad_keys)
    grad_value_mat = dot_first(attn_in, grad_values)
    grad_attn_in = (
        dot_last(grad_queries, query_mat)
        + dot_last(grad_keys, key_mat)
        + dot_last(grad_values, value_mat)
    )
    grad_gain_attn = jnp.sum(grad_attn_in * normed_attn, axis=0)
    input_grad = grad_hidden + norm_back(grad_attn_in * gain_attn_wide, normed_attn, inverse_attn)
    attn_terms = (
        grad_gain_attn,
        grad_query_mat,
        grad_key_mat,
        grad_value_mat,
        grad_output_mat,
        grad_centroid,
    )
    outer_sums = (
        lax.psum_scatter(attn_terms[0], "grp", scatter_dimension=0, tiled=True),
        lax.psum_scatter(attn_terms[1], "grp", scatter_dimension=0, tiled=True),
        lax.psum_scatter(attn_terms[2], "grp", scatter_dimension=0, tiled=True),
        lax.psum_scatter(attn_terms[3], "grp", scatter_dimension=0, tiled=True),
        lax.psum_scatter(attn_terms[4], "grp", scatter_dimension=0, tiled=True),
        lax.psum_scatter(attn_terms[5], "grp", scatter_dimension=0, tiled=True),
    )
    attn_sums = (
        lax.psum_scatter(outer_sums[0], "ep", scatter_dimension=0, tiled=True),
        lax.psum_scatter(outer_sums[1], "ep", scatter_dimension=0, tiled=True),
        lax.psum_scatter(outer_sums[2], "ep", scatter_dimension=0, tiled=True),
        lax.psum_scatter(outer_sums[3], "ep", scatter_dimension=0, tiled=True),
        lax.psum_scatter(outer_sums[4], "ep", scatter_dimension=0, tiled=True),
        lax.psum_scatter(outer_sums[5], "ep", scatter_dimension=0, tiled=True),
    )
    return (
        result.astype(jnp.bfloat16),
        input_grad,
        attn_sums[0],
        attn_sums[1],
        attn_sums[2],
        attn_sums[3],
        attn_sums[4],
        attn_sums[5],
        gain_one_sum,
        gain_two_sum,
        up_one_sum,
        down_one_sum,
        up_two_sum,
        down_two_sum,
        rms_values,
    )


def fast_shards(
    inputs,
    attn_gain,
    w_query,
    w_key,
    w_value,
    w_output,
    centroids,
    norm1_gain,
    norm2_gain,
    up_first,
    down_first,
    up_second,
    down_second,
    routes,
    prefix,
    cotangent,
):
    zs = lax.axis_size("grp") // 4
    group_total = lax.axis_size("grp")
    ep_size = lax.axis_size("ep")
    per = w_query.shape[0]
    tokens, width = inputs.shape
    extra = jnp.concatenate([attn_gain[None, :], centroids.T], axis=0)
    extra = jnp.pad(extra, ((0, 16 - extra.shape[0]), (0, 128 - per)))
    full = gather_weights(zs, [w_query, w_key, w_value, w_output, extra])
    mats = [f.reshape(width, width) for f in full[:4]]
    extras = full[4].reshape(width // per, 16, 128)[:, :3, :per].transpose(1, 0, 2).reshape(3, width)
    gain, cents = extras[0:1], extras[1:3]
    attn_in, queries, keys, values, context, hidden, gate, pick, slot_rows, slot_grads, branch_sq = attend(
        HEADS, inputs, gain, *mats, cents, routes, prefix, cotangent
    )

    gain1, gain2 = norm1_gain, norm2_gain
    weights = (up_first, down_first, up_second, down_second)
    in_one, in_two, act_one, slope_one, act_two, slope_two, middle, delta, sub_sq, rows, grads = expert_forward(
        slot_rows.reshape(2, tokens, width), slot_grads.reshape(2, tokens, width), gain1, gain2, *weights
    )
    pieces = lambda a: a.reshape(ep_size, tokens, width)
    reduced = backward_step(
        zs,
        HEADS,
        [inputs, attn_in, queries, keys, values, context, cotangent, hidden, pick, *mats],
        [act_one, act_two, slope_one, slope_two, pieces(in_one), pieces(in_two), grads, rows,
         pieces(delta), middle, *weights],
        [gain, cents, gain1, gain2, gate, routes, branch_sq, sub_sq],
        prefix.reshape(1, 1),
    )
    result, input_grad = reduced[7:9]
    down_two_sum, up_two_sum, down_one_sum, up_one_sum = (reduced[0][i] for i in range(4))
    query_sum, key_sum, value_sum, output_sum = reduced[1:5]
    grp_sum, all_sum = reduced[5], reduced[6]
    grp_at = lax.axis_index("grp") * (width // group_total)
    all_at = (lax.axis_index("grp") * ep_size + lax.axis_index("ep")) * per
    gains = lax.dynamic_slice(grp_sum, (0, grp_at), (2, width // group_total))
    outer = lax.dynamic_slice(all_sum, (0, all_at), (5, per))
    cell_count = float(tokens * width * group_total * ep_size)
    rms_values = jnp.sqrt(jnp.sum(all_sum[5:9], axis=1) / cell_count)
    return (
        result,
        input_grad,
        outer[2],
        query_sum,
        key_sum,
        value_sum,
        output_sum,
        outer[3:5].T,
        gains[0:1],
        gains[1:2],
        up_one_sum.T[None],
        down_one_sum[None],
        up_two_sum.T[None],
        down_two_sum[None],
        rms_values,
    )


def solution(mesh):
    fast = mesh.shape["ep"] == 2 and mesh.shape["grp"] == 16
    in_specs = (
        P(("grp", "ep"), None),
        P(("grp", "ep")),
        P(("grp", "ep"), None),
        P(("grp", "ep"), None),
        P(("grp", "ep"), None),
        P(("grp", "ep"), None),
        P(("grp", "ep"), None),
        P("ep", None),
        P("ep", None),
        P("ep", None, None),
        P("ep", None, None),
        P("ep", None, None),
        P("ep", None, None),
        P(("grp", "ep"), None),
        P(("grp", "ep")),
        P(("grp", "ep"), None),
    )
    out_specs = (
        P(("grp", "ep"), None),
        P(("grp", "ep"), None),
        P(("grp", "ep")),
        P(("grp", "ep"), None),
        P(("grp", "ep"), None),
        P(("grp", "ep"), None),
        P(("grp", "ep"), None),
        P(("grp", "ep"), None),
        P("ep", "grp"),
        P("ep", "grp"),
        P("ep", None, "grp"),
        P("ep", "grp", None),
        P("ep", None, "grp"),
        P("ep", "grp", None),
        P(),
    )
    return jax.shard_map(fast_shards if fast else shards, mesh=mesh, in_specs=in_specs, out_specs=out_specs, check_vma=False)
```

```python
import functools

import jax
import jax.numpy as jnp
from jax import lax
from jax.experimental import pallas as pl
from jax.experimental.pallas import tpu as pltpu
from jax.sharding import PartitionSpec as P

HEADS = 16


EPSILON = 1e-05
SQRT_HALF = 0.7071067811865476
INV_ROOT_TWO_PI = 0.3989422804014327
HIGH = lax.Precision.HIGHEST
HALF_LOG2E = -0.7213475204444817
ERF_P = 0.3275911 * SQRT_HALF
ERF_A1 = 0.5 * 0.254829592
ERF_A2 = 0.5 * -0.284496736
ERF_A3 = 0.5 * 1.421413741
ERF_A4 = 0.5 * -1.453152027
ERF_A5 = 0.5 * 1.061405429


def norm_parts(rows_in):
    center = rows_in - jnp.mean(rows_in, axis=-1, keepdims=True)
    inverse = lax.rsqrt(jnp.mean(center * center, axis=-1, keepdims=True) + EPSILON)
    return (center * inverse, inverse)


def norm_back(grad_normed, normed, inverse):
    mean_grad = jnp.mean(grad_normed, axis=-1, keepdims=True)
    mean_dot = jnp.mean(grad_normed * normed, axis=-1, keepdims=True)
    return inverse * (grad_normed - mean_grad - normed * mean_dot)


def gelu_slope(preact):
    return (
        0.5 * (1.0 + jax.scipy.special.erf(preact * SQRT_HALF))
        + preact * jnp.exp(-0.5 * preact * preact) * INV_ROOT_TWO_PI
    )


def matmul(left_side, right_side):
    return jnp.dot(left_side, right_side, preferred_element_type=jnp.float32)


def dot_first(left_side, right_side):
    return lax.dot_general(
        left_side, right_side, (((0,), (0,)), ((), ())), preferred_element_type=jnp.float32
    )


def dot_last(left_side, right_side):
    return lax.dot_general(
        left_side, right_side, (((1,), (1,)), ((), ())), preferred_element_type=jnp.float32
    )


def visible_mask(row_start, row_count, key_count, prefix_len):
    row_ids = row_start + jnp.arange(row_count, dtype=jnp.int32)[:, None]
    col_ids = jnp.arange(key_count, dtype=jnp.int32)[None, :]
    return (col_ids <= row_ids) | (col_ids < prefix_len)


def fill_slots(rows_in, target, slot_total):
    return jnp.zeros((slot_total, rows_in.shape[1]), rows_in.dtype).at[target].set(rows_in)


MESH = pl.DeviceIdType.MESH
VMEM_CAP = 66 * 1000 * 1000


def place(zs):
    grp = lax.axis_index("grp")
    ep = lax.axis_index("ep")
    core = lax.rem(grp, 2)
    x = lax.rem(lax.div(grp, 2), 2)
    z = lax.div(grp, 4)
    return z, x, core, ep


def device(z, x, core, ep):
    return ((z * 2 + x) * 2 + core, ep)


def greet(peers):
    barrier = pltpu.get_barrier_semaphore()
    for peer in peers:
        pl.semaphore_signal(barrier, inc=1, device_id=peer, device_id_type=MESH)
    pl.semaphore_wait(barrier, len(peers))


def push(src, dst, send_sem, recv_sem, peer):
    return pltpu.make_async_remote_copy(
        src_ref=src, dst_ref=dst, send_sem=send_sem, recv_sem=recv_sem, device_id=peer, device_id_type=MESH
    )


def layer_norm(v):
    center = v - jnp.mean(v, axis=-1, keepdims=True)
    inverse = lax.rsqrt(jnp.mean(center * center, axis=-1, keepdims=True) + EPSILON)
    return center * inverse, inverse


def gelu_pair(v):
    tail = jnp.exp2(v * v * HALF_LOG2E)
    t = 1.0 / (1.0 + ERF_P * jnp.abs(v))
    poly = ((((ERF_A5 * t + ERF_A4) * t + ERF_A3) * t + ERF_A2) * t + ERF_A1) * t
    upper = poly * tail
    phi = jnp.where(v >= 0.0, 1.0 - upper, upper)
    return v * phi, phi + v * (tail * INV_ROOT_TWO_PI)


def expert_forward_kernel(tiles, slots, slot_grads, gain1, gain2, up1, down1, up2, down2, in1, in2, act1, slope1, act2, slope2, middle, delta, sums, rows, grads, acc, sub, near, stage, send_sem, recv_sem, copy_sem):
    layer = pl.program_id(0)
    t = pl.program_id(1)
    bf, f32 = jnp.bfloat16, jnp.float32
    z, x, core, ep = place(0)
    y_peer = device(z, x, core, 1 - ep)
    count = near.shape[1]

    def far_rows():
        return push(slots.at[1], rows.at[1], send_sem.at[0], recv_sem.at[0], y_peer)

    def far_grads():
        return push(slot_grads.at[1], grads.at[1], send_sem.at[1], recv_sem.at[1], y_peer)

    def copy(src, dst, i):
        return pltpu.make_async_copy(src, dst, copy_sem.at[i])

    def norm_rows(half):
        normed, _ = layer_norm(near[half].astype(f32))
        in1[half * count : (half + 1) * count] = (normed * gain1[...].astype(f32)).astype(bf)

    @pl.when((layer == 0) & (t == 0))
    def _():
        greet([y_peer])
        far_rows().start()
        far_grads().start()
        copy(slots.at[0], near.at[0], 0).start()
        copy(slot_grads.at[0], stage, 1).start()
        copy(slots.at[0], near.at[0], 0).wait()
        copy(slot_grads.at[0], stage, 1).wait()
        copy(near.at[0], rows.at[0], 0).start()
        copy(stage, grads.at[0], 1).start()
        norm_rows(0)

    @pl.when((layer == 1) & (t == 0))
    def _():
        copy(near.at[0], rows.at[0], 0).wait()
        copy(stage, grads.at[0], 1).wait()
        far_rows().wait()
        copy(rows.at[1], near.at[1], 0).start()
        copy(rows.at[1], near.at[1], 0).wait()
        norm_rows(1)

    def step(source, span, up, down, act, slope):
        pre = jnp.dot(source[span], up[0], preferred_element_type=f32)
        a, s = gelu_pair(pre)
        low = a.astype(bf)
        act[...] = low
        slope[...] = s.astype(bf)
        prod = jnp.dot(low, down[0], preferred_element_type=f32)

        @pl.when(t == 0)
        def _():
            acc[span] = prod

        @pl.when(t > 0)
        def _():
            acc[span] += prod

    for half in range(2):
        @pl.when(layer == half)
        def _():
            span = slice(half * count, (half + 1) * count)
            step(in1, span, up1, down1, act1, slope1)

            @pl.when(t == tiles - 1)
            def _():
                value = acc[span]
                sub[span] = value
                square = jnp.sum(value * value, axis=0, keepdims=True)
                if half == 0:
                    sums[0:1] = square
                else:
                    sums[0:1] += square
                mid = near[half].astype(f32) + value
                middle[span] = mid
                normed, _ = layer_norm(mid)
                in2[span] = (normed * gain2[...].astype(f32)).astype(bf)

    @pl.when(layer == 2)
    def _():
        step(in2, slice(0, 2 * count), up2, down2, act2, slope2)

        @pl.when(t == tiles - 1)
        def _():
            value = acc[...]
            sums[1:2] = jnp.sum(value * value, axis=0, keepdims=True)
            sums[2:8] = jnp.zeros((6, value.shape[1]), f32)
            delta[...] = (sub[...] + value).astype(bf)
            far_grads().wait()


def expert_forward(slots, slot_grads, gain1, gain2, up1, down1, up2, down2):
    _, count, feat = slots.shape
    n = 2 * count
    hidden = up1.shape[2]
    tile = 1024
    tiles = hidden // tile
    last = tiles - 1
    bf, f32 = jnp.bfloat16, jnp.float32
    shape = jax.ShapeDtypeStruct
    hbm = pl.BlockSpec(memory_space=pl.ANY)
    whole = lambda s: pl.BlockSpec(s, lambda l, t: (0,) * len(s))
    first = lambda l, t: jnp.where(l < 2, t, last)
    second = lambda l, t: jnp.where(l < 2, 0, t)
    up = lambda f: pl.BlockSpec((1, feat, tile), lambda l, t: (0, 0, f(l, t)))
    down = lambda f: pl.BlockSpec((1, tile, feat), lambda l, t: (0, f(l, t), 0))
    halves = pl.BlockSpec((count, tile), lambda l, t: (jnp.minimum(l, 1), first(l, t)))
    wide = pl.BlockSpec((n, tile), lambda l, t: (0, second(l, t)))
    dma = pltpu.SemaphoreType.DMA
    return pl.pallas_call(
        functools.partial(expert_forward_kernel, tiles),
        grid=(3, tiles),
        in_specs=[hbm, hbm, whole((1, feat)), whole((1, feat)), up(first), down(first), up(second), down(second)],
        out_specs=[whole((n, feat))] * 2 + [halves] * 2 + [wide] * 2 + [whole((n, feat))] * 2 + [whole((8, feat)), hbm, hbm],
        out_shape=[shape((n, feat), bf)] * 2
        + [shape((n, hidden), bf)] * 4
        + [shape((n, feat), f32), shape((n, feat), bf), shape((8, feat), f32)]
        + [shape((2, count, feat), bf)] * 2,
        scratch_shapes=[
            pltpu.VMEM((n, feat), f32),
            pltpu.VMEM((n, feat), f32),
            pltpu.VMEM((2, count, feat), bf),
            pltpu.VMEM((count, feat), bf),
            dma((2,)),
            dma((2,)),
            dma((2,)),
        ],
        compiler_params=pltpu.CompilerParams(
            collective_id=3, has_side_effects=True, vmem_limit_bytes=VMEM_CAP, dimension_semantics=("arbitrary", "arbitrary")
        ),
        name="expert_forward",
    )(slots, slot_grads, gain1, gain2, up1, down1, up2, down2)


def front_kernel(zs, heads, *refs):
    shard = refs[0:5]
    x, routes, cotangent, prefix = refs[5:9]
    out_full = refs[9:13]
    attn_in, queries, keys, values, context, hidden, gate, pick, slot_rows, slot_grads, sums, gain, cents = refs[13:26]
    full = refs[26:31]
    ctx, own_sem, z_send, z_recv, p_send, p_recv, c_send, c_recv, out_sem = refs[31:]
    bf, f32 = jnp.bfloat16, jnp.float32
    tokens, feat = x.shape
    pair = 2 * feat // heads
    scale = (feat // heads) ** -0.5
    z, xx, core, ep = place(zs)
    right = device(jnp.minimum(z + 1, zs - 1), xx, core, ep)
    left = device(jnp.maximum(z - 1, 0), xx, core, ep)
    x_peer = device(z, 1 - xx, core, ep)
    y_peer = device(z, xx, core, 1 - ep)
    c_peer = device(z, xx, 1 - core, ep)
    others = [device(lax.rem(z + k, zs), xx, core, ep) for k in range(1, zs)]
    half = shard[0].shape[1] // 2
    per = shard[0].shape[0]
    items = []
    for w in range(4):
        items.append((w, slice(0, half), True))
        items.append((w, slice(half, 2 * half), False))
    items.append((4, slice(0, shard[4].shape[1]), True))
    count = len(items)

    def own(i):
        w, cols, _ = items[i]
        return pltpu.make_async_copy(shard[w].at[:, cols], full[w].at[z, xx, core, ep, :, cols], own_sem.at[i])

    def z_copy(i, src, slot, way, hop, peer):
        w, cols, _ = items[i]
        return push(src, full[w].at[slot, xx, core, ep, :, cols], z_send.at[i, way, hop], z_recv.at[i, way, hop], peer)

    def z_start(i):
        w, cols, _ = items[i]

        @pl.when(z < zs - 1)
        def _():
            z_copy(i, shard[w].at[:, cols], z, 0, 0, right).start()

        @pl.when(z > 0)
        def _():
            z_copy(i, shard[w].at[:, cols], z, 1, 0, left).start()

    def z_hop(i, hop):
        w, cols, _ = items[i]
        low = jnp.maximum(z - hop, 0)
        high = jnp.minimum(z + hop, zs - 1)
        from_left = full[w].at[low, xx, core, ep, :, cols]
        from_right = full[w].at[high, xx, core, ep, :, cols]

        @pl.when(z >= hop)
        def _():
            z_copy(i, from_left, low, 0, hop - 1, right).wait_recv()

        if hop < zs - 1:
            @pl.when((z >= hop) & (z < zs - 1))
            def _():
                z_copy(i, from_left, low, 0, hop, right).start()

        @pl.when(z + hop <= zs - 1)
        def _():
            z_copy(i, from_right, high, 1, hop - 1, left).wait_recv()

        if hop < zs - 1:
            @pl.when((z + hop <= zs - 1) & (z > 0))
            def _():
                z_copy(i, from_right, high, 1, hop, left).start()

    def z_drain(i):
        w, cols, _ = items[i]
        for hop in range(zs - 1):
            src = full[w].at[z, xx, core, ep, :, cols]

            @pl.when((z < zs - 1) & (z >= hop))
            def _():
                z_copy(i, src, z, 0, hop, right).wait_send()

            @pl.when((z > 0) & (z + hop <= zs - 1))
            def _():
                z_copy(i, src, z, 1, hop, left).wait_send()

    def second(i):
        w, cols, x_first = items[i]
        part = full[w].at[:, xx, core, ep, :, cols]
        return push(part, part, p_send.at[i, 0], p_recv.at[i, 0], x_peer if x_first else y_peer)

    def third(i):
        w, cols, x_first = items[i]
        part = full[w].at[:, :, core, ep, :, cols] if x_first else full[w].at[:, xx, core, :, :, cols]
        return push(part, part, p_send.at[i, 1], p_recv.at[i, 1], y_peer if x_first else x_peer)

    def fourth(i):
        w, cols, _ = items[i]
        part = full[w].at[:, :, core, :, :, cols]
        return push(part, part, c_send.at[i], c_recv.at[i], c_peer)

    def put_out(w):
        return pltpu.make_async_copy(full[w], out_full[w], out_sem.at[w])

    def matrix(w):
        return full[w][...].reshape(feat, feat)

    last_dims = (((1,), (1,)), ((), ()))
    first_dims = (((0,), (0,)), ((), ()))

    def spread_extras():
        table = full[4][...].reshape(feat // per, 16, 128)
        lane = lax.broadcasted_iota(jnp.int32, (128, feat), 1)
        source = lax.broadcasted_iota(jnp.int32, (128, feat), 0)
        choose = (lax.rem(lane, per) == source).astype(bf)
        dev = lax.broadcasted_iota(jnp.int32, (feat // per, feat), 0)
        home = lax.div(lax.broadcasted_iota(jnp.int32, (feat // per, feat), 1), per)
        for r in range(3):
            spread = jnp.dot(table[:, r, :], choose, preferred_element_type=f32)
            row = jnp.sum(jnp.where(dev == home, spread, 0.0), axis=0, keepdims=True).astype(bf)
            if r == 0:
                gain[...] = row
            else:
                cents[r - 1 : r] = row
        normed, _ = layer_norm(x[...].astype(f32))
        attn_in[...] = (normed * gain[...].astype(f32)).astype(bf)

    def project(w):
        out = (queries, keys, values)[w]
        out[...] = jnp.dot(attn_in[...], matrix(w), preferred_element_type=f32).astype(bf)

    row_ids = lax.broadcasted_iota(jnp.int32, (tokens, tokens), 0)
    col_ids = lax.broadcasted_iota(jnp.int32, (tokens, tokens), 1)

    def attention():
        low_half = lax.broadcasted_iota(jnp.int32, (tokens, pair), 1) < pair // 2

        def body(h, carry):
            visible = (col_ids <= row_ids) | (col_ids < prefix[0])
            cols = pl.ds(pl.multiple_of(h * pair, pair), pair)
            q, k, v = queries[:, cols], keys[:, cols], values[:, cols]
            outs = []
            for side in (low_half, jnp.logical_not(low_half)):
                mine = jnp.where(side, q, jnp.zeros_like(q))
                s = lax.dot_general(mine, k, last_dims, preferred_element_type=f32) * scale
                s = jnp.where(visible, s, -1e30)
                top = jnp.max(s, axis=-1, keepdims=True)
                total = top + jnp.log(jnp.sum(jnp.exp(s - top), axis=-1, keepdims=True))
                p = jnp.exp(s - total).astype(bf)
                outs.append(jnp.dot(p, v, preferred_element_type=f32))
            ctx[:, cols] = jnp.where(low_half, outs[0], outs[1]).astype(bf)
            return carry

        lax.fori_loop(0, heads // 2, body, 0)
        context[...] = ctx[...]

    def dispatch():
        branch = jnp.dot(ctx[...], matrix(3), preferred_element_type=f32)
        sums[...] = jnp.broadcast_to(jnp.sum(branch * branch, axis=0, keepdims=True), sums.shape)
        hid = x[...].astype(f32) + branch
        hidden[...] = hid
        low = hid.astype(bf)
        scores = lax.dot_general(low, cents[...], last_dims, preferred_element_type=f32)
        lane = lax.broadcasted_iota(jnp.int32, scores.shape, 1)
        hot = (lane == routes[...]).astype(f32)
        g = 1.0 / (1.0 + jnp.exp(-jnp.sum(scores * hot, axis=1, keepdims=True)))
        gate[...] = g
        tri = (col_ids <= row_ids).astype(bf)
        counted = jnp.dot(tri, hot.astype(bf), preferred_element_type=f32)
        position = jnp.sum(counted * hot, axis=1, keepdims=True) - 1.0
        away = (routes[...] != ep).astype(jnp.int32)
        target = away * tokens + position.astype(jnp.int32)
        slots = lax.broadcasted_iota(jnp.int32, (tokens, 2 * tokens), 1)
        chosen = (slots == target).astype(bf)
        pick[...] = chosen
        slot_rows[...] = lax.dot_general(chosen, low, first_dims, preferred_element_type=f32).astype(bf)
        grads = (g * cotangent[...].astype(f32)).astype(bf)
        slot_grads[...] = lax.dot_general(chosen, grads, first_dims, preferred_element_type=f32).astype(bf)

    greet(others + [x_peer, y_peer, c_peer])
    order = [[8, 0, 1], [2, 3], [4, 5], [6, 7]]
    for i in order[0] + order[1]:
        z_start(i)
    for i in range(count):
        own(i).start()
    for t in range(len(order) + 3):
        if t < len(order):
            for hop in range(1, zs):
                for i in order[t]:
                    z_hop(i, hop)
            for i in order[t]:
                own(i).wait()
                second(i).start()
            if t + 2 < len(order):
                for i in order[t + 2]:
                    z_start(i)
        if 1 <= t < len(order) + 1:
            for i in order[t - 1]:
                second(i).wait_recv()
                third(i).start()

        def pass_on():
            for i in order[t - 2]:
                third(i).wait_recv()
                fourth(i).start()

        if 2 <= t < len(order) + 1:
            pass_on()
        if t >= 3:
            w = t - 3
            for i in order[w]:
                fourth(i).wait_recv()
            put_out(w).start()
            if w == 0:
                spread_extras()
            if w < 3:
                project(w)
            if w == 2:
                attention()
        if t == len(order) + 1:
            pass_on()
    dispatch()
    for w in range(4):
        put_out(w).wait()
    for i in range(count):
        z_drain(i)
        second(i).wait_send()
        third(i).wait_send()
        fourth(i).wait_send()


def front(zs, heads, shards_in, x, routes, cotangent, prefix):
    tokens, feat = x.shape
    bf, f32 = jnp.bfloat16, jnp.float32
    shape = jax.ShapeDtypeStruct
    vm = pl.BlockSpec(memory_space=pltpu.VMEM)
    hbm = pl.BlockSpec(memory_space=pl.ANY)
    n = 2 * len(shards_in) - 1
    dma = pltpu.SemaphoreType.DMA
    wholes = [(zs, 2, 2, 2) + s.shape for s in shards_in]
    shapes = [shape(s, bf) for s in wholes[:4]]
    shapes += [shape((tokens, feat), bf)] * 5
    shapes += [shape((tokens, feat), f32), shape((tokens, 1), f32), shape((tokens, 2 * tokens), bf)]
    shapes += [shape((2 * tokens, feat), bf)] * 2 + [shape((8, feat), f32), shape((1, feat), bf), shape((2, feat), bf)]
    return pl.pallas_call(
        functools.partial(front_kernel, zs, heads),
        out_shape=shapes,
        in_specs=[vm] * 8 + [pl.BlockSpec(memory_space=pltpu.SMEM)],
        out_specs=[hbm] * 4 + [vm] * 13,
        scratch_shapes=[pltpu.VMEM(s, bf) for s in wholes]
        + [
            pltpu.VMEM((tokens, feat), bf),
            dma((n,)), dma((n, 2, zs)), dma((n, 2, zs)), dma((n, 2)), dma((n, 2)), dma((n,)), dma((n,)), dma((4,)),
        ],
        compiler_params=pltpu.CompilerParams(collective_id=1, has_side_effects=True, vmem_limit_bytes=VMEM_CAP),
        name="front",
    )(*shards_in, x, routes, cotangent, prefix)


SLICES = 4
X_SLICES = 1
LEAD = 2
LAG = 3
RING = 8


def step_kernel(zs, heads, *refs):
    (x_ref, attn_in_ref, q_ref, k_ref, v_ref, context_ref, cot_ref, hidden_ref, pick_ref, wq, wk, wv, wo) = refs[0:13]
    (act_one, act_two, slope_one, slope_two, in_one, in_two, grads, rows_ref, delta, middle, up1, down1, up2, down2) = refs[13:27]
    gain, cents, gain1, gain2, gate, routes, branch_sq, sub_sq, prefix = refs[27:36]
    out_w = refs[36]
    out_a = refs[37:41]
    small_grp, small_all, result, input_grad = refs[41:45]
    pre_two, pre_one, sub_grad, row_grad, wide_far, narrow_far, attn_far, back_far, grad_far = refs[45:54]
    (send, xrecv, zrecv, acc, tiles, sides, prod, ep_in, x_in, z_in, small_in, small_ref) = refs[54:66]
    (wd, wu, sl, ps, hb, accf, midf, loadf, picks) = refs[66:75]
    (wf_s, wf_r, nf_s, nf_r, xs, xr, zsem_s, zsem_r, es, er, axs, axr, azs, azr, ss, sr, tile_sem, side_sem) = refs[75:93]
    (af_s, af_r, y_s, y_r, w_sem, ps_sem, ld_sem, out_sem, free_sem) = refs[93:]
    wide = (act_two, pre_two, act_one, pre_one)
    narrow = (grads, in_two, sub_grad, in_one)
    bf, f32 = jnp.bfloat16, jnp.float32
    z, x, core, ep = place(zs)
    tokens, feat = x_ref.shape
    rows = 2 * tokens
    hidden = act_one.shape[1]
    chunk = out_w.shape[1]
    per = prod.shape[4]
    blocks = 4 * zs
    size = chunk // SLICES
    right = device(jnp.minimum(z + 1, zs - 1), x, core, ep)
    left = device(jnp.maximum(z - 1, 0), x, core, ep)
    x_peer = device(z, 1 - x, core, ep)
    y_peer = device(z, x, core, 1 - ep)
    c_peer = device(z, x, 1 - core, ep)
    others = [device(lax.rem(z + k, zs), x, core, ep) for k in range(1, zs)]
    contract0 = (((0,), (0,)), ((), ()))
    last_dims = (((1,), (1,)), ((), ()))

    def dest(k):
        to_right = zs - 1 - z
        lower = jnp.where(k < to_right, zs - 1 - k, k - to_right)
        upper = jnp.where(k < z, k, zs - 1 - (k - z))
        return jnp.where(k < zs - 1, jnp.where(z < zs // 2, lower, upper), z)

    def begins(d):
        return ((d > z) & (z == 0)) | ((d < z) & (z == zs - 1))

    def loads(pairs, at=0):
        return [pltpu.make_async_copy(src, dst, ld_sem.at[at + i]) for i, (src, dst) in enumerate(pairs)]

    def begin(copies):
        for c in copies:
            c.start()

    def end(copies):
        for c in copies:
            c.wait()

    def fetch(pairs):
        copies = loads(pairs)
        begin(copies)
        end(copies)

    def two(slot):
        return hb.at[pl.ds(slot, 2)]

    def flat(slot):
        return hb[pl.ds(slot, 2)].reshape(rows, feat)

    greet(others + [x_peer, y_peer, c_peer])

    def far_wide(w, q):
        j = q * 2 + (1 - core)
        return push(
            wide[w].at[:, pl.ds(pl.multiple_of(j * chunk, chunk), chunk)], wide_far.at[w, q], wf_s.at[w], wf_r.at[w], c_peer
        )

    def far_narrow(w):
        return push(narrow[w], narrow_far.at[w], nf_s.at[w], nf_r.at[w], c_peer)

    def all_far(w):
        return push(wide_far.at[w], wide_far.at[w], wf_s.at[w], wf_r.at[w], c_peer)

    def send_wide(w):
        def send_far(q, carry):
            far_wide(w, q).start()
            return carry

        lax.fori_loop(0, 2 * zs, send_far, 0)

    def far_attn(i, src):
        return push(src, attn_far.at[i], af_s.at[i], af_r.at[i], c_peer)

    def far_delta():
        return push(delta.at[1], back_far, y_s.at[0], y_r.at[0], y_peer)

    def far_rows():
        return push(row_grad, grad_far, y_s.at[1], y_r.at[1], y_peer)

    far_narrow(0).start()
    send_wide(0)
    far_delta().start()
    far_narrow(1).start()
    far_narrow(3).start()
    far_attn(0, attn_in_ref).start()
    far_attn(1, context_ref).start()

    def load_tile(w, q, slot):
        j = q * 2 + core
        for i in range(4):
            @pl.when(w == i)
            def _():
                pltpu.make_async_copy(
                    wide[i].at[:, pl.ds(pl.multiple_of(j * chunk, chunk), chunk)],
                    tiles.at[slot, pl.ds(0, rows), :],
                    tile_sem.at[slot, 0],
                ).start()

        pltpu.make_async_copy(wide_far.at[w, q], tiles.at[slot, pl.ds(rows, rows), :], tile_sem.at[slot, 1]).start()

    def wait_tile(slot):
        for i in range(2):
            part = tiles.at[slot, pl.ds(i * rows, rows), :]
            pltpu.make_async_copy(part, part, tile_sem.at[slot, i]).wait()

    def load_side(w):
        slot = lax.rem(w, 2)
        for i in range(4):
            @pl.when(w == i)
            def _():
                pltpu.make_async_copy(narrow[i], sides.at[slot, pl.ds(0, 2)], side_sem.at[0]).start()

        pltpu.make_async_copy(narrow_far.at[w], sides.at[slot, pl.ds(2, 2)], side_sem.at[1]).start()

    def wait_side(w):
        slot = lax.rem(w, 2)
        for i in range(2):
            part = sides.at[slot, pl.ds(2 * i, 2)]
            pltpu.make_async_copy(part, part, side_sem.at[i]).wait()

    def product(w, slot):
        side = sides[lax.rem(w, 2)].reshape(2 * rows, feat)
        return lax.dot_general(tiles[slot], side, contract0, preferred_element_type=f32)

    def span(s):
        return pl.ds(pl.multiple_of(s * size, size), size)

    def x_copy(b, s):
        wide_size = chunk // X_SLICES
        at = pl.ds(pl.multiple_of(s * wide_size, wide_size), wide_size)
        return push(send.at[lax.rem(b, RING), at, :], xrecv.at[lax.rem(b, RING), at, :], xs.at[b, s], xr.at[b, s], x_peer)

    def z_copy(b, s):
        w = lax.div(b, zs)
        d = dest(lax.rem(b, zs))
        to_right = d > z
        nxt = jnp.where(to_right, z + 1, z - 1)
        slot = jnp.where(d != nxt, d, jnp.where(to_right, d, zs))
        return push(
            send.at[lax.rem(b, RING), span(s), :], zrecv.at[w, slot, span(s), :], zsem_s.at[b, s],
            zsem_r.at[w, slot, s], device(nxt, x, core, ep),
        )

    def z_wait(w, slot, s):
        ref = zrecv.at[w, slot, span(s), :]
        push(ref, ref, zsem_s.at[0, s], zsem_r.at[w, slot, s], x_peer).wait_recv()
        return ref[...].astype(f32)

    def z_sent(b):
        @pl.when(lax.rem(b, zs) < zs - 1)
        def _():
            for s in range(SLICES):
                z_copy(b, s).wait_send()

    def q_first(b):
        return dest(lax.rem(b, zs)) * 2 + (1 - x)

    def q_second(b):
        return dest(lax.rem(b, zs)) * 2 + x

    def far_wait(w):
        for i in range(4):
            @pl.when(w == i)
            def _():
                far_narrow(i).wait_recv()
                all_far(i).wait_recv()

    def stage_one(b):
        w = lax.div(b, zs)
        slot = lax.rem(b, 2)

        @pl.when(lax.rem(b, zs) == 0)
        def _():
            far_wait(w)
            load_side(w)
            load_tile(w, q_first(b), slot)
            wait_side(w)

        wait_tile(slot)

        @pl.when(lax.rem(b, zs) < zs - 1)
        def _():
            load_tile(w, q_first(b + 1), 1 - slot)

        @pl.when(b >= RING)
        def _():
            z_sent(b - RING)

        send[lax.rem(b, RING)] = product(w, slot).astype(bf)

    def stage_two(b):
        w = lax.div(b, zs)
        d = dest(lax.rem(b, zs))
        slot = 2 + lax.rem(b, 2)
        mine = lax.rem(b, RING)
        wait_tile(slot)

        @pl.when(b + 1 < blocks)
        def _():
            load_tile(lax.div(b + 1, zs), q_second(b + 1), 5 - slot)

        keep = lax.rem(b, LAG + 1)
        acc[keep] = product(w, slot)

        def piece(s, carry):
            sp = span(s)
            per_x = SLICES // X_SLICES

            @pl.when(lax.rem(s, per_x) == 0)
            def _():
                x_copy(b, lax.div(s, per_x)).wait()

            total = acc[keep, sp, :] + xrecv[mine, sp, :].astype(f32)
            acc[keep, sp, :] = total

            @pl.when(begins(d))
            def _():
                send[mine, sp, :] = total.astype(bf)

            return carry

        lax.fori_loop(0, SLICES, piece, 0)

        @pl.when(b < blocks - RING)
        def _():
            pl.semaphore_signal(free_sem, inc=1, device_id=x_peer, device_id_type=MESH)

        @pl.when(begins(d))
        def _():
            for s in range(SLICES):
                z_copy(b, s).start()

    def stage_three(b):
        w = lax.div(b, zs)
        d = dest(lax.rem(b, zs))
        mine = lax.rem(b, RING)
        keep = lax.rem(b, LAG + 1)

        @pl.when((d != z) & jnp.logical_not(begins(d)))
        def _():
            def piece(s, carry):
                sp = span(s)
                send[mine, sp, :] = (acc[keep, sp, :] + z_wait(w, d, s)).astype(bf)

                @pl.when(s > 0)
                def _():
                    z_copy(b, s - 1).start()

                return carry

            lax.fori_loop(0, SLICES, piece, 0)
            z_copy(b, SLICES - 1).start()

        @pl.when(d == z)
        def _():
            def piece(s, carry):
                sp = span(s)
                acc[keep, sp, :] += z_wait(w, jnp.where(z > 0, z, zs), s)

                @pl.when((z > 0) & (z < zs - 1))
                def _():
                    acc[keep, sp, :] += z_wait(w, zs, s)

                return carry

            lax.fori_loop(0, SLICES, piece, 0)
            copy = pltpu.make_async_copy(acc.at[keep], out_w.at[w], out_sem)
            copy.start()
            copy.wait()

    tile = wd.shape[1]

    def stream(source, start, count, up, down, slope, pre, low_step, high_step):
        def copies(t, slot):
            cols = pl.ds(pl.multiple_of(t * tile, tile), tile)
            return (
                pltpu.make_async_copy(down.at[0, cols, :], wd.at[slot], w_sem.at[slot, 0]),
                pltpu.make_async_copy(up.at[0, :, cols], wu.at[slot], w_sem.at[slot, 1]),
                pltpu.make_async_copy(slope.at[pl.ds(start, count), cols], sl.at[slot, pl.ds(0, count), :], w_sem.at[slot, 2]),
            )

        def out(t, slot):
            cols = pl.ds(pl.multiple_of(t * tile, tile), tile)
            return pltpu.make_async_copy(ps.at[slot, pl.ds(0, count), :], pre.at[pl.ds(start, count), cols], ps_sem.at[slot])

        for c in copies(low_step, low_step % 2):
            c.start()

        def body(t, carry):
            slot = lax.rem(t, 2)
            for c in copies(t, slot):
                c.wait()

            @pl.when(t + 1 < high_step)
            def _():
                for c in copies(t + 1, 1 - slot):
                    c.start()

            g = lax.dot_general(source(), wd[slot], last_dims, preferred_element_type=f32)
            low = (g * sl[slot, 0:count].astype(f32)).astype(bf)

            @pl.when(t >= low_step + 2)
            def _():
                out(t - 2, slot).wait()

            ps[slot, 0:count] = low
            out(t, slot).start()
            value = lax.dot_general(low, wu[slot], last_dims, preferred_element_type=f32)

            @pl.when(t == 0)
            def _():
                accf[0:count] = value

            @pl.when(t > 0)
            def _():
                accf[0:count] += value

            return carry

        lax.fori_loop(low_step, high_step, body, 0)
        for t in range(high_step - 2, high_step):
            out(t, t % 2).wait()

    part = 64

    def norm_parts_of(value, g, gain_row):
        normed, inverse = layer_norm(value)
        total = jnp.sum(g * normed, axis=0, keepdims=True)
        q = g * gain_row
        mean_q = jnp.mean(q, axis=-1, keepdims=True)
        mean_dot = jnp.mean(q * normed, axis=-1, keepdims=True)
        return total, inverse * (q - mean_q - normed * mean_dot)

    steps = hidden // tile
    part_loads = loads(
        [
            (cot_ref, hb.at[1]),
            (attn_in_ref, hb.at[0]),
            (q_ref, hb.at[12]),
            (k_ref, hb.at[13]),
            (v_ref, hb.at[14]),
            (x_ref, hb.at[11]),
            (hidden_ref, loadf.at[pl.ds(0, tokens)]),
            (pick_ref, picks),
        ]
    )
    late_loads = loads(
        [
            (delta.at[0], hb.at[3]),
            (context_ref, hb.at[2]),
            (wo.at[pl.ds(0, feat // 2)], wd.at[0]),
            (wo.at[pl.ds(feat // 2, feat // 2)], wd.at[1]),
            (back_far, hb.at[5]),
        ],
        8,
    )
    expert_loads = loads([(middle, loadf), (rows_ref, two(2))], 14)

    def event_second_start():
        fetch([(grads, two(0))])
        begin(expert_loads)
        stream(lambda: flat(0), 0, rows, up2, down2, slope_two, pre_two, 0, steps // 2)

    def event_second_end():
        stream(lambda: flat(0), 0, rows, up2, down2, slope_two, pre_two, steps // 2, steps)
        send_wide(1)
        end(expert_loads)
        small_ref[...] = jnp.zeros_like(small_ref)
        gain_row = gain2[...].astype(f32)
        per_block = tokens // part

        def body(i, carry):
            at = pl.ds(pl.multiple_of(i * part, part), part)
            total, value = norm_parts_of(loadf[at], accf[at], gain_row)
            small_ref[1:2] += total
            midf[at] = value
            blk = lax.div(i, per_block)
            sub = pl.ds(pl.multiple_of(lax.rem(i, per_block) * part, part), part)
            hb[4 + blk, sub] = (hb[blk, sub].astype(f32) + value).astype(bf)
            return carry

        lax.fori_loop(0, rows // part, body, 0)
        fetch([(two(4), sub_grad)])
        far_narrow(2).start()
        send_wide(2)
        begin(part_loads)

    def first_stream(blk, low_step, high_step):
        start = blk * tokens
        stream(lambda: hb[4 + blk], start, tokens, up1, down1, slope_one, pre_one, low_step, high_step)

    def first_norm(blk):
        gain_row = gain1[...].astype(f32)

        def body(i, carry):
            at = pl.ds(pl.multiple_of(i * part, part), part)
            value = hb[2 + blk, at].astype(f32)
            total, back = norm_parts_of(value, accf[at], gain_row)
            small_ref[0:1] += total
            mid = midf[pl.ds(pl.multiple_of(blk * tokens + i * part, part), part)]
            hb[6 + blk, at] = (back + mid).astype(bf)
            return carry

        lax.fori_loop(0, tokens // part, body, 0)

    def event_far_start():
        first_stream(1, 0, steps // 2)

    def event_far_end():
        first_stream(1, steps // 2, steps)
        first_norm(1)
        fetch_out = pltpu.make_async_copy(hb.at[7], row_grad, out_sem)
        fetch_out.start()
        fetch_out.wait()
        far_rows().start()

    def event_own_start():
        first_stream(0, 0, steps // 2)

    def event_own_end():
        first_stream(0, steps // 2, steps)
        first_norm(0)
        send_wide(3)
        far_delta().wait_recv()
        begin(late_loads)

    half = feat // 2

    def event_combine():
        far_rows().wait_recv()
        row_load = pltpu.make_async_copy(grad_far, hb.at[9], out_sem)
        row_load.start()
        end(part_loads)
        end(late_loads)
        row_load.wait()
        c = cents[...].astype(f32)

        def combine(i, carry):
            at = pl.ds(pl.multiple_of(i * part, part), part)
            own = picks[at, 0:tokens]
            far = picks[at, tokens : 2 * tokens]
            returned = jnp.dot(own, hb[3], preferred_element_type=f32) + jnp.dot(far, hb[5], preferred_element_type=f32)
            back = jnp.dot(own, hb[6], preferred_element_type=f32) + jnp.dot(far, hb[9], preferred_element_type=f32)
            g = gate[at]
            hid = loadf[at]
            res = hid + g * returned
            hb[15, at] = res.astype(bf)
            small_ref[5:6] += jnp.sum(res * res, axis=0, keepdims=True)
            grad_out = hb[1, at].astype(f32)
            grad_score = jnp.sum(grad_out * returned, axis=1, keepdims=True) * g * (1.0 - g)
            is_first = routes[at] == 0
            weighted = grad_score * hid.astype(bf).astype(f32)
            zero = jnp.zeros_like(weighted)
            small_ref[3:4] += jnp.sum(jnp.where(is_first, weighted, zero), axis=0, keepdims=True)
            small_ref[4:5] += jnp.sum(jnp.where(is_first, zero, weighted), axis=0, keepdims=True)
            grad_hidden = grad_out + grad_score * jnp.where(is_first, c[0:1], c[1:2]) + back
            midf[at] = grad_hidden
            hb[10, at] = grad_hidden.astype(bf)
            return carry

        lax.fori_loop(0, tokens // part, combine, 0)
        fetch([(hb.at[15], result)])
        for i in range(2):
            hb[15, :, i * half : (i + 1) * half] = lax.dot_general(
                hb[10], wd[i], last_dims, preferred_element_type=f32
            ).astype(bf)

    def event_heads(low_pair, high_pair):
        row_ids = lax.broadcasted_iota(jnp.int32, (tokens, tokens), 0)
        col_ids = lax.broadcasted_iota(jnp.int32, (tokens, tokens), 1)
        pair = 2 * feat // heads
        scale = (feat // heads) ** -0.5
        limit = prefix[...]

        def head(h, carry):
            visible = (col_ids <= row_ids) | (col_ids < limit)
            low_half = lax.broadcasted_iota(jnp.int32, (tokens, pair), 1) < pair // 2
            cols = pl.ds(pl.multiple_of(h * pair, pair), pair)
            q, k, v, gc = hb[12, :, cols], hb[13, :, cols], hb[14, :, cols], hb[15, :, cols]
            outs = []
            for side in (low_half, jnp.logical_not(low_half)):
                s = lax.dot_general(jnp.where(side, q, jnp.zeros_like(q)), k, last_dims, preferred_element_type=f32) * scale
                s = jnp.where(visible, s, -1e30)
                top = jnp.max(s, axis=-1, keepdims=True)
                total = top + jnp.log(jnp.sum(jnp.exp(s - top), axis=-1, keepdims=True))
                p = jnp.exp(s - total)
                gp = lax.dot_general(jnp.where(side, gc, jnp.zeros_like(gc)), v, last_dims, preferred_element_type=f32)
                dot = jnp.sum(gp * p, axis=-1, keepdims=True)
                gs = (p * (gp - dot)).astype(bf)
                outs.append(
                    (
                        jnp.dot(gs, k, preferred_element_type=f32),
                        lax.dot_general(gs, q, contract0, preferred_element_type=f32),
                        lax.dot_general(p.astype(bf), gc, contract0, preferred_element_type=f32),
                    )
                )
            hb[4, :, cols] = (jnp.where(low_half, outs[0][0], outs[1][0]) * scale).astype(bf)
            hb[6, :, cols] = (jnp.where(low_half, outs[0][1], outs[1][1]) * scale).astype(bf)
            hb[8, :, cols] = jnp.where(low_half, outs[0][2], outs[1][2]).astype(bf)
            return carry

        lax.fori_loop(low_pair, high_pair, head, 0)

    def event_inputs():
        order = [(m, i) for i in range(2) for m in (wq, wk, wv)]

        def weight_copy(n):
            m, i = order[n]
            return pltpu.make_async_copy(m.at[pl.ds(i * half, half)], wd.at[n % 2], w_sem.at[n % 2, 0])

        weight_copy(0).start()
        for n in range(6):
            weight_copy(n).wait()
            if n < 5:
                weight_copy(n + 1).start()
            value = lax.dot_general(hb[4 + 2 * (n % 3)], wd[n % 2], last_dims, preferred_element_type=f32)
            cols = slice((n // 3) * half, (n // 3 + 1) * half)
            if n % 3 == 0:
                accf[0:tokens, cols] = value
            else:
                accf[0:tokens, cols] += value
        for i in range(4):
            far_attn(2 + i, hb.at[4 + 2 * i]).start()
        gain_row = gain[...].astype(f32)

        def norms(i, carry):
            at = pl.ds(pl.multiple_of(i * part, part), part)
            total, value = norm_parts_of(hb[11, at].astype(f32), accf[at], gain_row)
            small_ref[2:3] += total
            midf[at] += value
            return carry

        lax.fori_loop(0, tokens // part, norms, 0)
        small_ref[6:7] = branch_sq[0:1]
        small_ref[7:9] = sub_sq[0:2]
        start0()

    def event_products():
        for i in range(6):
            far_attn(i, hb.at[0]).wait_recv()
        fetch(
            [(midf.at[pl.ds(0, tokens)], input_grad)]
            + [(attn_far.at[i], hb.at[2 * i + 1]) for i in range(6)]
        )
        step = 8 * per

        for w in range(4):
            lhs = 0 if w < 3 else 2
            rhs = 4 + 2 * w

            def form(m, carry):
                cols = pl.ds(pl.multiple_of(m * step, step), step)
                left_part = hb[pl.ds(lhs, 2), :, cols].reshape(rows, step)
                value = lax.dot_general(left_part, flat(rhs), contract0, preferred_element_type=f32)
                value = value.astype(bf).reshape(2, 2, 2 * per, feat)
                mine = jnp.where(core == 0, value[:, 0], value[:, 1])
                prod[w, m] = mine.reshape(2, 2, per, feat)
                return carry

            lax.fori_loop(0, zs, form, 0)
            if w > 0:
                attn_ep(w - 1).start()
        for i in range(6):
            far_attn(i, hb.at[0]).wait_send()
        attn_ep(3).start()

    def attn_ep(w):
        return push(prod.at[w, :, :, 1 - ep], ep_in.at[w], es.at[w], er.at[w], y_peer)

    def attn_x(w):
        return push(prod.at[w, z, 1 - x, ep], x_in.at[w], axs.at[w], axr.at[w], x_peer)

    def fold_ep(w):
        attn_ep(w).wait()

        def body(m, carry):
            for i in range(2):
                total = prod[w, m, i, ep].astype(f32) + ep_in[w, m, i].astype(f32)
                prod[w, m, i, ep] = total.astype(bf)
            return carry

        lax.fori_loop(0, zs, body, 0)

    def attn_z_copy(w, k):
        d = dest(k)
        to_right = d > z
        nxt = jnp.where(to_right, z + 1, z - 1)
        slot = jnp.where(d != nxt, d, jnp.where(to_right, d, zs))
        return push(prod.at[w, d, :, ep], z_in.at[w, slot], azs.at[w, k], azr.at[w, slot], device(nxt, x, core, ep))

    def attn_z_wait(w, slot):
        ref = z_in.at[w, slot]
        push(ref, ref, azs.at[w, 0], azr.at[w, slot], x_peer).wait_recv()

    def begin_z(w):
        def body(k, carry):
            @pl.when(begins(dest(k)))
            def _():
                attn_z_copy(w, k).start()

            return carry

        lax.fori_loop(0, zs - 1, body, 0)

    def forward_z(w):
        def body(k, carry):
            d = dest(k)

            @pl.when(jnp.logical_not(begins(d)))
            def _():
                attn_z_wait(w, d)
                for i in range(2):
                    prod[w, d, i, ep] = (prod[w, d, i, ep].astype(f32) + z_in[w, d, i].astype(f32)).astype(bf)
                attn_z_copy(w, k).start()

            return carry

        lax.fori_loop(0, zs - 1, body, 0)

    def own_z(w):
        first = jnp.where(z > 0, z, zs)
        attn_z_wait(w, first)
        for i in range(2):
            prod[w, z, i, ep] = (prod[w, z, i, ep].astype(f32) + z_in[w, first, i].astype(f32)).astype(bf)

        @pl.when((z > 0) & (z < zs - 1))
        def _():
            attn_z_wait(w, zs)
            for i in range(2):
                prod[w, z, i, ep] = (prod[w, z, i, ep].astype(f32) + z_in[w, zs, i].astype(f32)).astype(bf)

        attn_x(w).start()

    def last_x(w):
        attn_x(w).wait()
        out_a[w][...] = prod[w, z, x, ep].astype(f32) + x_in[w].astype(f32)
        for k in range(zs - 1):
            attn_z_copy(w, k).wait_send()

    def small_stage(stage, n, mine, peer_at, src):
        def copy(k):
            return push(src, small_in.at[stage, mine], ss.at[stage, k], sr.at[stage, k], peer_at(lax.rem(mine + k, n)))

        def start():
            for k in range(1, n):
                copy(k).start()

        def end():
            for k in range(1, n):
                copy(k).wait()
            small_in[stage, mine] = src[...]
            total = small_in[stage, 0]
            for i in range(1, n):
                total = total + small_in[stage, i]
            return total

        return start, end

    start0, end0 = small_stage(0, 2, core, lambda i: device(z, x, i, ep), small_ref)
    start1, end1 = small_stage(1, 2, x, lambda i: device(z, i, core, ep), small_in.at[3, 3])
    start2, end2 = small_stage(2, zs, z, lambda i: device(i, x, core, ep), small_in.at[3, 2])
    start3, end3 = small_stage(3, 2, ep, lambda i: device(z, x, core, i), small_grp)

    def event_x(w):
        def act():
            fold_ep(w)
            begin_z(w)

        return act

    def event_small1():
        small_in[3, 3] = end0()
        start1()

    def event_small2():
        small_in[3, 2] = end1()
        start2()

    def event_small3():
        small_grp[...] = end2()
        start3()

    def event_z(w):
        def act():
            forward_z(w)

        return act

    def event_own(w):
        def act():
            own_z(w)

        return act

    def event_last():
        for w in range(4):
            last_x(w)
        small_all[...] = end3()

    pairs = heads // 2
    steps_at = [
        (1, event_second_start),
        (2, event_second_end),
        (3, event_far_start),
        (4, event_far_end),
        (5, event_own_start),
        (6, event_own_end),
        (7, event_combine),
        (8, lambda: event_heads(0, pairs // 2)),
        (9, lambda: event_heads(pairs // 2, pairs)),
        (10, event_inputs),
        (11, event_products),
        (11, event_small1),
        (12, event_small2),
        (13, event_small3),
    ]
    steps_at += [(12 + w, event_x(w)) for w in range(4)]
    steps_at += [(14 + w, event_z(w)) for w in range(4)]
    steps_at += [(16 + w, event_own(w)) for w in range(4)]

    def pipeline(t, carry):
        @pl.when(t < blocks)
        def _():
            stage_one(t)

        @pl.when((t > 0) & (t <= blocks))
        def _():
            @pl.when(t - 1 >= RING)
            def _():
                pl.semaphore_wait(free_sem, 1)

            for s in range(X_SLICES):
                x_copy(t - 1, s).start()

        for at, action in steps_at:
            pl.when(t == at)(action)

        @pl.when(t == LEAD - 1)
        def _():
            load_tile(0, q_second(0), 2)

        @pl.when((t >= LEAD) & (t < blocks + LEAD))
        def _():
            stage_two(t - LEAD)

        late = t - LEAD - jnp.where((z == 0) | (z == zs - 1), LAG, LAG - 1)

        @pl.when((late >= 0) & (late < blocks))
        def _():
            stage_three(late)

        return carry

    lax.fori_loop(0, blocks + LEAD + LAG, pipeline, 0)
    event_last()

    def drain(b, carry):
        z_sent(b)
        return carry

    lax.fori_loop(blocks - RING, blocks, drain, 0)
    for w in range(4):
        far_narrow(w).wait_send()
        all_far(w).wait_send()
    far_delta().wait_send()
    far_rows().wait_send()


def backward_step(zs, heads, big, experts, little, prefix):
    x, hidden = big[0], experts[0].shape[1]
    tokens, feat = x.shape
    rows = 2 * tokens
    chunk = hidden // (4 * zs)
    per = feat // (8 * zs)
    f32, bf = jnp.float32, jnp.bfloat16
    shape = jax.ShapeDtypeStruct
    vm = pl.BlockSpec(memory_space=pltpu.VMEM)
    hbm = pl.BlockSpec(memory_space=pl.ANY)
    dma = pltpu.SemaphoreType.DMA
    outs = [shape((4, chunk, feat), f32)]
    outs += [shape((per, feat), f32)] * 4
    outs += [shape((16, feat), f32)] * 2
    outs += [shape((tokens, feat), bf), shape((tokens, feat), f32)]
    outs += [shape((rows, hidden), bf)] * 2 + [shape((2, tokens, feat), bf), shape((tokens, feat), bf)]
    outs += [shape((4, 2 * zs, rows, chunk), bf), shape((4, 2, tokens, feat), bf), shape((6, tokens, feat), bf)]
    outs += [shape((tokens, feat), bf)] * 2
    s = SLICES
    blocks = 4 * zs
    tile = 512
    vmem = pltpu.VMEM
    return pl.pallas_call(
        functools.partial(step_kernel, zs, heads),
        out_shape=outs,
        in_specs=[hbm] * 27 + [vm] * 9,
        out_specs=[hbm] + [vm] * 6 + [hbm] * 11,
        scratch_shapes=[
            vmem((RING, chunk, feat), bf),
            vmem((RING, chunk, feat), bf),
            vmem((4, zs + 1, chunk, feat), bf),
            vmem((LAG + 1, chunk, feat), f32),
            vmem((4, 2 * rows, chunk), bf),
            vmem((2, 4, tokens, feat), bf),
            vmem((4, zs, 2, 2, per, feat), bf),
            vmem((4, zs, 2, per, feat), bf),
            vmem((4, per, feat), bf),
            vmem((4, zs + 1, 2, per, feat), bf),
            vmem((4, max(zs, 4), 16, feat), f32),
            vmem((16, feat), f32),
            vmem((2, tile, feat), bf),
            vmem((2, feat, tile), bf),
            vmem((2, rows, tile), bf),
            vmem((2, rows, tile), bf),
            vmem((16, tokens, feat), bf),
            vmem((rows, feat), f32),
            vmem((rows, feat), f32),
            vmem((rows, feat), f32),
            vmem((tokens, rows), bf),
            dma((4,)), dma((4,)), dma((4,)), dma((4,)),
            dma((blocks, s)), dma((blocks, s)), dma((blocks, s)), dma((4, zs + 1, s)),
            dma((4,)), dma((4,)), dma((4,)), dma((4,)), dma((4, zs)), dma((4, zs + 1)),
            dma((4, zs)), dma((4, zs)), dma((4, 2)), dma((2,)),
            dma((6,)), dma((6,)), dma((2,)), dma((2,)), dma((2, 3)), dma((2,)), dma((16,)), dma, pltpu.SemaphoreType.REGULAR,
        ],
        compiler_params=pltpu.CompilerParams(collective_id=2, has_side_effects=True, vmem_limit_bytes=VMEM_CAP),
        name="backward_step",
    )(*big, *experts, *little, prefix)


def shards(
    inputs,
    attn_gain,
    w_query,
    w_key,
    w_value,
    w_output,
    centroids,
    norm1_gain,
    norm2_gain,
    up_first,
    down_first,
    up_second,
    down_second,
    routes,
    prefix,
    cotangent,
):
    gathered = (
        lax.all_gather(attn_gain, ("grp", "ep"), axis=0, tiled=True),
        lax.all_gather(w_query, ("grp", "ep"), axis=0, tiled=True),
        lax.all_gather(w_key, ("grp", "ep"), axis=0, tiled=True),
        lax.all_gather(w_value, ("grp", "ep"), axis=0, tiled=True),
        lax.all_gather(w_output, ("grp", "ep"), axis=0, tiled=True),
        lax.all_gather(centroids, ("grp", "ep"), axis=0, tiled=True),
    )
    gain_attn, query_mat, key_mat, value_mat, output_mat, centroid_mat = gathered
    token_count, feature_width = inputs.shape
    head_count = HEADS
    head_width = feature_width // head_count
    scale_factor = head_width ** (-0.5)
    block_rows = min(512, token_count)
    prefix_len = prefix[0]
    inputs_wide = inputs.astype(jnp.float32)
    normed_attn, inverse_attn = norm_parts(inputs_wide)
    gain_attn_wide = gain_attn.astype(jnp.float32)
    attn_in = (normed_attn * gain_attn_wide).astype(jnp.bfloat16)
    queries = (
        matmul(attn_in, query_mat).astype(jnp.bfloat16).reshape(token_count, head_count, head_width)
    )
    key_heads = (
        matmul(attn_in, key_mat).astype(jnp.bfloat16).reshape(token_count, head_count, head_width)
    )
    value_heads = (
        matmul(attn_in, value_mat).astype(jnp.bfloat16).reshape(token_count, head_count, head_width)
    )

    def block_scores(block_index):
        row_start = block_index * block_rows
        scores = (
            jnp.einsum("qhd,khd->hqk", queries, key_heads, preferred_element_type=jnp.float32)
            * scale_factor
        )
        visible = visible_mask(row_start, block_rows, token_count, prefix_len)
        return (queries, jnp.where(visible[None], scores, -1e30))

    block_index = 0
    query_block, scores = block_scores(block_index)
    row_max = jnp.max(scores, axis=-1, keepdims=True)
    expsum = jnp.sum(jnp.exp(scores - row_max), axis=-1, keepdims=True)
    log_total = row_max + jnp.log(expsum)
    probs_low = jnp.exp(scores - log_total).astype(jnp.bfloat16)
    context_parts = jnp.einsum(
        "hqk,khd->qhd", probs_low, value_heads, preferred_element_type=jnp.float32
    ).astype(jnp.bfloat16)
    lse_parts = [log_total]
    context = context_parts.reshape(token_count, feature_width)
    branch = matmul(context, output_mat)
    hidden = inputs_wide + branch
    hidden_low = hidden.astype(jnp.bfloat16)
    expert_total = lax.axis_size("ep")
    group_total = lax.axis_size("grp")
    capacity = 2 * token_count // expert_total
    route_ids = routes[:, 0]
    expert_ids = jnp.arange(expert_total, dtype=jnp.int32)
    route_hot = (route_ids[:, None] == expert_ids[None, :]).astype(jnp.int32)
    position = jnp.sum((jnp.cumsum(route_hot, axis=0) - 1) * route_hot, axis=1)
    target = route_ids * capacity + position
    route_weight = route_hot.astype(jnp.float32)
    all_scores = matmul(hidden_low, centroid_mat)
    gate_value = jax.nn.sigmoid(jnp.sum(all_scores * route_weight, axis=1))
    slot_rows = fill_slots(hidden_low, target, expert_total * capacity).reshape(
        expert_total, capacity, feature_width
    )
    received = lax.all_to_all(slot_rows, "ep", split_axis=0, concat_axis=0, tiled=True).reshape(
        expert_total * capacity, feature_width
    )
    gain_one = norm1_gain[0].astype(jnp.float32)
    gain_two = norm2_gain[0].astype(jnp.float32)
    up_one = up_first[0]
    down_one = down_first[0]
    up_two = up_second[0]
    down_two = down_second[0]
    rows_wide = received.astype(jnp.float32)
    normed_one, inverse_one = norm_parts(rows_wide)
    in_one = (normed_one * gain_one).astype(jnp.bfloat16)
    pre_one = matmul(in_one, up_one)
    act_one = jax.nn.gelu(pre_one, approximate=False).astype(jnp.bfloat16)
    sub_one = matmul(act_one, down_one)
    middle = rows_wide + sub_one
    normed_two, inverse_two = norm_parts(middle)
    in_two = (normed_two * gain_two).astype(jnp.bfloat16)
    pre_two = matmul(in_two, up_two)
    act_two = jax.nn.gelu(pre_two, approximate=False).astype(jnp.bfloat16)
    sub_two = matmul(act_two, down_two)
    delta = (sub_one + sub_two).astype(jnp.bfloat16).reshape(expert_total, capacity, feature_width)
    back_slots = lax.all_to_all(delta, "ep", split_axis=0, concat_axis=0, tiled=True).reshape(
        expert_total * capacity, feature_width
    )
    returned = back_slots[target].astype(jnp.float32)
    result = hidden + gate_value[:, None] * returned
    square_terms = jnp.stack(
        [
            jnp.sum(result * result),
            jnp.sum(branch * branch),
            jnp.sum(sub_one * sub_one),
            jnp.sum(sub_two * sub_two),
        ]
    )
    square_totals = lax.psum(square_terms, ("grp", "ep"))
    cell_count = float(token_count * feature_width * group_total * expert_total)
    rms_values = jnp.sqrt(square_totals / cell_count)
    grad_out = cotangent.astype(jnp.float32)
    grad_gate = jnp.sum(grad_out * returned, axis=1)
    grad_score = grad_gate * gate_value * (1.0 - gate_value)
    grad_delta_tok = (gate_value[:, None] * grad_out).astype(jnp.bfloat16)
    grad_slots = fill_slots(grad_delta_tok, target, expert_total * capacity).reshape(
        expert_total, capacity, feature_width
    )
    grad_sum = lax.all_to_all(grad_slots, "ep", split_axis=0, concat_axis=0, tiled=True).reshape(
        expert_total * capacity, feature_width
    )
    grad_pre_two = (dot_last(grad_sum, down_two) * gelu_slope(pre_two)).astype(jnp.bfloat16)
    grad_in_two = dot_last(grad_pre_two, up_two)
    grad_gain_two = jnp.sum(grad_in_two * normed_two, axis=0)
    grad_middle = norm_back(grad_in_two * gain_two, normed_two, inverse_two)
    grad_sub_one = (grad_sum.astype(jnp.float32) + grad_middle).astype(jnp.bfloat16)
    grad_pre_one = (dot_last(grad_sub_one, down_one) * gelu_slope(pre_one)).astype(jnp.bfloat16)
    grad_in_one = dot_last(grad_pre_one, up_one)
    grad_gain_one = jnp.sum(grad_in_one * normed_one, axis=0)
    grad_rows = (norm_back(grad_in_one * gain_one, normed_one, inverse_one) + grad_middle).astype(
        jnp.bfloat16
    )
    grad_back = lax.all_to_all(
        grad_rows.reshape(expert_total, capacity, feature_width),
        "ep",
        split_axis=0,
        concat_axis=0,
        tiled=True,
    ).reshape(expert_total * capacity, feature_width)
    grad_down_two = dot_first(act_two, grad_sum)
    grad_up_two = dot_first(in_two, grad_pre_two)
    grad_down_one = dot_first(act_one, grad_sub_one)
    grad_up_one = dot_first(in_one, grad_pre_one)
    expert_sums = (
        lax.psum_scatter(grad_up_one[None], "grp", scatter_dimension=2, tiled=True),
        lax.psum_scatter(grad_down_one[None], "grp", scatter_dimension=1, tiled=True),
        lax.psum_scatter(grad_up_two[None], "grp", scatter_dimension=2, tiled=True),
        lax.psum_scatter(grad_down_two[None], "grp", scatter_dimension=1, tiled=True),
        lax.psum_scatter(grad_gain_one[None], "grp", scatter_dimension=1, tiled=True),
        lax.psum_scatter(grad_gain_two[None], "grp", scatter_dimension=1, tiled=True),
    )
    up_one_sum, down_one_sum, up_two_sum, down_two_sum, gain_one_sum, gain_two_sum = expert_sums
    centroid_wide = centroid_mat.astype(jnp.float32)
    score_weight = route_weight * grad_score[:, None]
    grad_hidden = (
        grad_out
        + jnp.dot(score_weight, centroid_wide.T, precision=HIGH)
        + grad_back[target].astype(jnp.float32)
    )
    grad_centroid = lax.dot_general(
        hidden_low.astype(jnp.float32), score_weight, (((0,), (0,)), ((), ())), precision=HIGH
    )
    grad_branch = grad_hidden.astype(jnp.bfloat16)
    grad_output_mat = dot_first(context, grad_branch)
    grad_context = (
        dot_last(grad_branch, output_mat)
        .astype(jnp.bfloat16)
        .reshape(token_count, head_count, head_width)
    )
    block_index = 0
    query_block, scores = block_scores(block_index)
    probs_wide = jnp.exp(scores - lse_parts[block_index])
    probs_low = probs_wide.astype(jnp.bfloat16)
    row_start = block_index * block_rows
    grad_value_sum = jnp.einsum(
        "hqk,qhd->khd", probs_low, grad_context, preferred_element_type=jnp.float32
    )
    grad_probs = jnp.einsum(
        "qhd,khd->hqk", grad_context, value_heads, preferred_element_type=jnp.float32
    )
    row_dot = jnp.sum(grad_probs * probs_wide, axis=-1, keepdims=True)
    grad_scores = (probs_wide * (grad_probs - row_dot)).astype(jnp.bfloat16)
    grad_query_parts = (
        jnp.einsum("hqk,khd->qhd", grad_scores, key_heads, preferred_element_type=jnp.float32)
        * scale_factor
    ).astype(jnp.bfloat16)
    grad_key_sum = (
        jnp.einsum("hqk,qhd->khd", grad_scores, query_block, preferred_element_type=jnp.float32)
        * scale_factor
    )
    grad_queries = grad_query_parts.reshape(token_count, feature_width)
    grad_keys = grad_key_sum.astype(jnp.bfloat16).reshape(token_count, feature_width)
    grad_values = grad_value_sum.astype(jnp.bfloat16).reshape(token_count, feature_width)
    grad_query_mat = dot_first(attn_in, grad_queries)
    grad_key_mat = dot_first(attn_in, grad_keys)
    grad_value_mat = dot_first(attn_in, grad_values)
    grad_attn_in = (
        dot_last(grad_queries, query_mat)
        + dot_last(grad_keys, key_mat)
        + dot_last(grad_values, value_mat)
    )
    grad_gain_attn = jnp.sum(grad_attn_in * normed_attn, axis=0)
    input_grad = grad_hidden + norm_back(grad_attn_in * gain_attn_wide, normed_attn, inverse_attn)
    attn_terms = (
        grad_gain_attn,
        grad_query_mat,
        grad_key_mat,
        grad_value_mat,
        grad_output_mat,
        grad_centroid,
    )
    outer_sums = (
        lax.psum_scatter(attn_terms[0], "grp", scatter_dimension=0, tiled=True),
        lax.psum_scatter(attn_terms[1], "grp", scatter_dimension=0, tiled=True),
        lax.psum_scatter(attn_terms[2], "grp", scatter_dimension=0, tiled=True),
        lax.psum_scatter(attn_terms[3], "grp", scatter_dimension=0, tiled=True),
        lax.psum_scatter(attn_terms[4], "grp", scatter_dimension=0, tiled=True),
        lax.psum_scatter(attn_terms[5], "grp", scatter_dimension=0, tiled=True),
    )
    attn_sums = (
        lax.psum_scatter(outer_sums[0], "ep", scatter_dimension=0, tiled=True),
        lax.psum_scatter(outer_sums[1], "ep", scatter_dimension=0, tiled=True),
        lax.psum_scatter(outer_sums[2], "ep", scatter_dimension=0, tiled=True),
        lax.psum_scatter(outer_sums[3], "ep", scatter_dimension=0, tiled=True),
        lax.psum_scatter(outer_sums[4], "ep", scatter_dimension=0, tiled=True),
        lax.psum_scatter(outer_sums[5], "ep", scatter_dimension=0, tiled=True),
    )
    return (
        result.astype(jnp.bfloat16),
        input_grad,
        attn_sums[0],
        attn_sums[1],
        attn_sums[2],
        attn_sums[3],
        attn_sums[4],
        attn_sums[5],
        gain_one_sum,
        gain_two_sum,
        up_one_sum,
        down_one_sum,
        up_two_sum,
        down_two_sum,
        rms_values,
    )


def fast_shards(
    inputs,
    attn_gain,
    w_query,
    w_key,
    w_value,
    w_output,
    centroids,
    norm1_gain,
    norm2_gain,
    up_first,
    down_first,
    up_second,
    down_second,
    routes,
    prefix,
    cotangent,
):
    zs = lax.axis_size("grp") // 4
    group_total = lax.axis_size("grp")
    ep_size = lax.axis_size("ep")
    per = w_query.shape[0]
    tokens, width = inputs.shape
    extra = jnp.concatenate([attn_gain[None, :], centroids.T], axis=0)
    extra = jnp.pad(extra, ((0, 16 - extra.shape[0]), (0, 128 - per)))
    made = front(zs, HEADS, [w_query, w_key, w_value, w_output, extra], inputs, routes, cotangent, prefix)
    mats = [f.reshape(width, width) for f in made[:4]]
    attn_in, queries, keys, values, context, hidden, gate, pick, slot_rows, slot_grads, branch_sq, gain, cents = made[4:]
    gain1, gain2 = norm1_gain, norm2_gain
    weights = (up_first, down_first, up_second, down_second)
    in_one, in_two, act_one, slope_one, act_two, slope_two, middle, delta, sub_sq, rows, grads = expert_forward(
        slot_rows.reshape(2, tokens, width), slot_grads.reshape(2, tokens, width), gain1, gain2, *weights
    )
    pieces = lambda a: a.reshape(ep_size, tokens, width)
    reduced = backward_step(
        zs,
        HEADS,
        [inputs, attn_in, queries, keys, values, context, cotangent, hidden, pick, *mats],
        [act_one, act_two, slope_one, slope_two, pieces(in_one), pieces(in_two), grads, rows,
         pieces(delta), middle, *weights],
        [gain, cents, gain1, gain2, gate, routes, branch_sq, sub_sq],
        prefix.reshape(1, 1),
    )
    result, input_grad = reduced[7:9]
    down_two_sum, up_two_sum, down_one_sum, up_one_sum = (reduced[0][i] for i in range(4))
    query_sum, key_sum, value_sum, output_sum = reduced[1:5]
    grp_sum, all_sum = reduced[5], reduced[6]
    grp_at = lax.axis_index("grp") * (width // group_total)
    all_at = (lax.axis_index("grp") * ep_size + lax.axis_index("ep")) * per
    gains = lax.dynamic_slice(grp_sum, (0, grp_at), (2, width // group_total))
    outer = lax.dynamic_slice(all_sum, (0, all_at), (5, per))
    cell_count = float(tokens * width * group_total * ep_size)
    rms_values = jnp.sqrt(jnp.sum(all_sum[5:9], axis=1) / cell_count)
    return (
        result,
        input_grad,
        outer[2],
        query_sum,
        key_sum,
        value_sum,
        output_sum,
        outer[3:5].T,
        gains[0:1],
        gains[1:2],
        up_one_sum.T[None],
        down_one_sum[None],
        up_two_sum.T[None],
        down_two_sum[None],
        rms_values,
    )


def solution(mesh):
    fast = mesh.shape["ep"] == 2 and mesh.shape["grp"] == 16
    in_specs = (
        P(("grp", "ep"), None),
        P(("grp", "ep")),
        P(("grp", "ep"), None),
        P(("grp", "ep"), None),
        P(("grp", "ep"), None),
        P(("grp", "ep"), None),
        P(("grp", "ep"), None),
        P("ep", None),
        P("ep", None),
        P("ep", None, None),
        P("ep", None, None),
        P("ep", None, None),
        P("ep", None, None),
        P(("grp", "ep"), None),
        P(("grp", "ep")),
        P(("grp", "ep"), None),
    )
    out_specs = (
        P(("grp", "ep"), None),
        P(("grp", "ep"), None),
        P(("grp", "ep")),
        P(("grp", "ep"), None),
        P(("grp", "ep"), None),
        P(("grp", "ep"), None),
        P(("grp", "ep"), None),
        P(("grp", "ep"), None),
        P("ep", "grp"),
        P("ep", "grp"),
        P("ep", None, "grp"),
        P("ep", "grp", None),
        P("ep", None, "grp"),
        P("ep", "grp", None),
        P(),
    )
    return jax.shard_map(fast_shards if fast else shards, mesh=mesh, in_specs=in_specs, out_specs=out_specs, check_vma=False)
```

```python
import functools

import jax
import jax.numpy as jnp
from jax import lax
from jax.experimental import pallas as pl
from jax.experimental.pallas import tpu as pltpu
from jax.sharding import PartitionSpec as P

HEADS = 16


EPSILON = 1e-05
SQRT_HALF = 0.7071067811865476
INV_ROOT_TWO_PI = 0.3989422804014327
HIGH = lax.Precision.HIGHEST
HALF_LOG2E = -0.7213475204444817
ERF_P = 0.3275911 * SQRT_HALF
ERF_A1 = 0.5 * 0.254829592
ERF_A2 = 0.5 * -0.284496736
ERF_A3 = 0.5 * 1.421413741
ERF_A4 = 0.5 * -1.453152027
ERF_A5 = 0.5 * 1.061405429


def norm_parts(rows_in):
    center = rows_in - jnp.mean(rows_in, axis=-1, keepdims=True)
    inverse = lax.rsqrt(jnp.mean(center * center, axis=-1, keepdims=True) + EPSILON)
    return (center * inverse, inverse)


def norm_back(grad_normed, normed, inverse):
    mean_grad = jnp.mean(grad_normed, axis=-1, keepdims=True)
    mean_dot = jnp.mean(grad_normed * normed, axis=-1, keepdims=True)
    return inverse * (grad_normed - mean_grad - normed * mean_dot)


def gelu_slope(preact):
    return (
        0.5 * (1.0 + jax.scipy.special.erf(preact * SQRT_HALF))
        + preact * jnp.exp(-0.5 * preact * preact) * INV_ROOT_TWO_PI
    )


def matmul(left_side, right_side):
    return jnp.dot(left_side, right_side, preferred_element_type=jnp.float32)


def dot_first(left_side, right_side):
    return lax.dot_general(
        left_side, right_side, (((0,), (0,)), ((), ())), preferred_element_type=jnp.float32
    )


def dot_last(left_side, right_side):
    return lax.dot_general(
        left_side, right_side, (((1,), (1,)), ((), ())), preferred_element_type=jnp.float32
    )


def visible_mask(row_start, row_count, key_count, prefix_len):
    row_ids = row_start + jnp.arange(row_count, dtype=jnp.int32)[:, None]
    col_ids = jnp.arange(key_count, dtype=jnp.int32)[None, :]
    return (col_ids <= row_ids) | (col_ids < prefix_len)


def fill_slots(rows_in, target, slot_total):
    return jnp.zeros((slot_total, rows_in.shape[1]), rows_in.dtype).at[target].set(rows_in)


MESH = pl.DeviceIdType.MESH
VMEM_CAP = 66 * 1000 * 1000


def place(zs):
    grp = lax.axis_index("grp")
    ep = lax.axis_index("ep")
    core = lax.rem(grp, 2)
    x = lax.rem(lax.div(grp, 2), 2)
    z = lax.div(grp, 4)
    return z, x, core, ep


def device(z, x, core, ep):
    return ((z * 2 + x) * 2 + core, ep)


def greet(peers):
    barrier = pltpu.get_barrier_semaphore()
    for peer in peers:
        pl.semaphore_signal(barrier, inc=1, device_id=peer, device_id_type=MESH)
    pl.semaphore_wait(barrier, len(peers))


def push(src, dst, send_sem, recv_sem, peer):
    return pltpu.make_async_remote_copy(
        src_ref=src, dst_ref=dst, send_sem=send_sem, recv_sem=recv_sem, device_id=peer, device_id_type=MESH
    )


def layer_norm(v):
    center = v - jnp.mean(v, axis=-1, keepdims=True)
    inverse = lax.rsqrt(jnp.mean(center * center, axis=-1, keepdims=True) + EPSILON)
    return center * inverse, inverse


def gelu_pair(v):
    tail = jnp.exp2(v * v * HALF_LOG2E)
    t = 1.0 / (1.0 + ERF_P * jnp.abs(v))
    poly = ((((ERF_A5 * t + ERF_A4) * t + ERF_A3) * t + ERF_A2) * t + ERF_A1) * t
    upper = poly * tail
    phi = jnp.where(v >= 0.0, 1.0 - upper, upper)
    return v * phi, phi + v * (tail * INV_ROOT_TWO_PI)


def expert_forward_kernel(tiles, slots, slot_grads, gain1, gain2, up1, down1, up2, down2, in1, in2, act1, slope1, act2, slope2, middle, delta, sums, rows, grads, acc, sub, near, stage, send_sem, recv_sem, copy_sem):
    layer = pl.program_id(0)
    t = pl.program_id(1)
    bf, f32 = jnp.bfloat16, jnp.float32
    z, x, core, ep = place(0)
    y_peer = device(z, x, core, 1 - ep)
    count = near.shape[1]

    def far_rows():
        return push(slots.at[1], rows.at[1], send_sem.at[0], recv_sem.at[0], y_peer)

    def far_grads():
        return push(slot_grads.at[1], grads.at[1], send_sem.at[1], recv_sem.at[1], y_peer)

    def copy(src, dst, i):
        return pltpu.make_async_copy(src, dst, copy_sem.at[i])

    def norm_rows(half):
        normed, _ = layer_norm(near[half].astype(f32))
        in1[half * count : (half + 1) * count] = (normed * gain1[...].astype(f32)).astype(bf)

    @pl.when((layer == 0) & (t == 0))
    def _():
        greet([y_peer])
        far_rows().start()
        far_grads().start()
        copy(slots.at[0], near.at[0], 0).start()
        copy(slot_grads.at[0], stage, 1).start()
        copy(slots.at[0], near.at[0], 0).wait()
        copy(slot_grads.at[0], stage, 1).wait()
        copy(near.at[0], rows.at[0], 0).start()
        copy(stage, grads.at[0], 1).start()
        norm_rows(0)

    @pl.when((layer == 1) & (t == 0))
    def _():
        copy(near.at[0], rows.at[0], 0).wait()
        copy(stage, grads.at[0], 1).wait()
        far_rows().wait()
        copy(rows.at[1], near.at[1], 0).start()
        copy(rows.at[1], near.at[1], 0).wait()
        norm_rows(1)

    def step(source, span, up, down, act, slope):
        pre = jnp.dot(source[span], up[0], preferred_element_type=f32)
        a, s = gelu_pair(pre)
        low = a.astype(bf)
        act[...] = low
        slope[...] = s.astype(bf)
        prod = jnp.dot(low, down[0], preferred_element_type=f32)

        @pl.when(t == 0)
        def _():
            acc[span] = prod

        @pl.when(t > 0)
        def _():
            acc[span] += prod

    for half in range(2):
        @pl.when(layer == half)
        def _():
            span = slice(half * count, (half + 1) * count)
            step(in1, span, up1, down1, act1, slope1)

            @pl.when(t == tiles - 1)
            def _():
                value = acc[span]
                sub[span] = value
                square = jnp.sum(value * value, axis=0, keepdims=True)
                if half == 0:
                    sums[0:1] = square
                else:
                    sums[0:1] += square
                mid = near[half].astype(f32) + value
                middle[span] = mid
                normed, _ = layer_norm(mid)
                in2[span] = (normed * gain2[...].astype(f32)).astype(bf)

    @pl.when(layer == 2)
    def _():
        step(in2, slice(0, 2 * count), up2, down2, act2, slope2)

        @pl.when(t == tiles - 1)
        def _():
            value = acc[...]
            sums[1:2] = jnp.sum(value * value, axis=0, keepdims=True)
            sums[2:8] = jnp.zeros((6, value.shape[1]), f32)
            delta[...] = (sub[...] + value).astype(bf)
            far_grads().wait()


def expert_forward(slots, slot_grads, gain1, gain2, up1, down1, up2, down2):
    _, count, feat = slots.shape
    n = 2 * count
    hidden = up1.shape[2]
    tile = 1024
    tiles = hidden // tile
    last = tiles - 1
    bf, f32 = jnp.bfloat16, jnp.float32
    shape = jax.ShapeDtypeStruct
    hbm = pl.BlockSpec(memory_space=pl.ANY)
    whole = lambda s: pl.BlockSpec(s, lambda l, t: (0,) * len(s))
    first = lambda l, t: jnp.where(l < 2, t, last)
    second = lambda l, t: jnp.where(l < 2, 0, t)
    up = lambda f: pl.BlockSpec((1, feat, tile), lambda l, t: (0, 0, f(l, t)))
    down = lambda f: pl.BlockSpec((1, tile, feat), lambda l, t: (0, f(l, t), 0))
    halves = pl.BlockSpec((count, tile), lambda l, t: (jnp.minimum(l, 1), first(l, t)))
    wide = pl.BlockSpec((n, tile), lambda l, t: (0, second(l, t)))
    dma = pltpu.SemaphoreType.DMA
    return pl.pallas_call(
        functools.partial(expert_forward_kernel, tiles),
        grid=(3, tiles),
        in_specs=[hbm, hbm, whole((1, feat)), whole((1, feat)), up(first), down(first), up(second), down(second)],
        out_specs=[whole((n, feat))] * 2 + [halves] * 2 + [wide] * 2 + [whole((n, feat))] * 2 + [whole((8, feat)), hbm, hbm],
        out_shape=[shape((n, feat), bf)] * 2
        + [shape((n, hidden), bf)] * 4
        + [shape((n, feat), f32), shape((n, feat), bf), shape((8, feat), f32)]
        + [shape((2, count, feat), bf)] * 2,
        scratch_shapes=[
            pltpu.VMEM((n, feat), f32),
            pltpu.VMEM((n, feat), f32),
            pltpu.VMEM((2, count, feat), bf),
            pltpu.VMEM((count, feat), bf),
            dma((2,)),
            dma((2,)),
            dma((2,)),
        ],
        compiler_params=pltpu.CompilerParams(
            collective_id=3, has_side_effects=True, vmem_limit_bytes=VMEM_CAP, dimension_semantics=("arbitrary", "arbitrary")
        ),
        name="expert_forward",
    )(slots, slot_grads, gain1, gain2, up1, down1, up2, down2)


def front_kernel(zs, heads, *refs):
    shard = refs[0:5]
    x, routes, cotangent, prefix = refs[5:9]
    out_full = refs[9:13]
    attn_in, queries, keys, values, context, hidden, gate, pick, slot_rows, slot_grads, sums, gain, cents = refs[13:26]
    full = refs[26:31]
    ctx, own_sem, z_send, z_recv, p_send, p_recv, c_send, c_recv, out_sem = refs[31:]
    bf, f32 = jnp.bfloat16, jnp.float32
    tokens, feat = x.shape
    pair = 2 * feat // heads
    scale = (feat // heads) ** -0.5
    z, xx, core, ep = place(zs)
    right = device(jnp.minimum(z + 1, zs - 1), xx, core, ep)
    left = device(jnp.maximum(z - 1, 0), xx, core, ep)
    x_peer = device(z, 1 - xx, core, ep)
    y_peer = device(z, xx, core, 1 - ep)
    c_peer = device(z, xx, 1 - core, ep)
    others = [device(lax.rem(z + k, zs), xx, core, ep) for k in range(1, zs)]
    half = shard[0].shape[1] // 2
    per = shard[0].shape[0]
    items = []
    for w in range(4):
        items.append((w, slice(0, half), True))
        items.append((w, slice(half, 2 * half), False))
    items.append((4, slice(0, shard[4].shape[1]), True))
    count = len(items)

    def own(i):
        w, cols, _ = items[i]
        return pltpu.make_async_copy(shard[w].at[:, cols], full[w].at[z, xx, core, ep, :, cols], own_sem.at[i])

    def z_copy(i, src, slot, way, hop, peer):
        w, cols, _ = items[i]
        return push(src, full[w].at[slot, xx, core, ep, :, cols], z_send.at[i, way, hop], z_recv.at[i, way, hop], peer)

    def z_start(i):
        w, cols, _ = items[i]

        @pl.when(z < zs - 1)
        def _():
            z_copy(i, shard[w].at[:, cols], z, 0, 0, right).start()

        @pl.when(z > 0)
        def _():
            z_copy(i, shard[w].at[:, cols], z, 1, 0, left).start()

    def z_hop(i, hop):
        w, cols, _ = items[i]
        low = jnp.maximum(z - hop, 0)
        high = jnp.minimum(z + hop, zs - 1)
        from_left = full[w].at[low, xx, core, ep, :, cols]
        from_right = full[w].at[high, xx, core, ep, :, cols]

        @pl.when(z >= hop)
        def _():
            z_copy(i, from_left, low, 0, hop - 1, right).wait_recv()

        if hop < zs - 1:
            @pl.when((z >= hop) & (z < zs - 1))
            def _():
                z_copy(i, from_left, low, 0, hop, right).start()

        @pl.when(z + hop <= zs - 1)
        def _():
            z_copy(i, from_right, high, 1, hop - 1, left).wait_recv()

        if hop < zs - 1:
            @pl.when((z + hop <= zs - 1) & (z > 0))
            def _():
                z_copy(i, from_right, high, 1, hop, left).start()

    def z_drain(i):
        w, cols, _ = items[i]
        for hop in range(zs - 1):
            src = full[w].at[z, xx, core, ep, :, cols]

            @pl.when((z < zs - 1) & (z >= hop))
            def _():
                z_copy(i, src, z, 0, hop, right).wait_send()

            @pl.when((z > 0) & (z + hop <= zs - 1))
            def _():
                z_copy(i, src, z, 1, hop, left).wait_send()

    def second(i):
        w, cols, x_first = items[i]
        part = full[w].at[:, xx, core, ep, :, cols]
        return push(part, part, p_send.at[i, 0], p_recv.at[i, 0], x_peer if x_first else y_peer)

    def third(i):
        w, cols, x_first = items[i]
        part = full[w].at[:, :, core, ep, :, cols] if x_first else full[w].at[:, xx, core, :, :, cols]
        return push(part, part, p_send.at[i, 1], p_recv.at[i, 1], y_peer if x_first else x_peer)

    def fourth(i):
        w, cols, _ = items[i]
        part = full[w].at[:, :, core, :, :, cols]
        return push(part, part, c_send.at[i], c_recv.at[i], c_peer)

    def put_out(w):
        return pltpu.make_async_copy(full[w], out_full[w], out_sem.at[w])

    def matrix(w):
        return full[w][...].reshape(feat, feat)

    last_dims = (((1,), (1,)), ((), ()))
    first_dims = (((0,), (0,)), ((), ()))

    def spread_extras():
        table = full[4][...].reshape(feat // per, 16, 128)
        lane = lax.broadcasted_iota(jnp.int32, (128, feat), 1)
        source = lax.broadcasted_iota(jnp.int32, (128, feat), 0)
        choose = (lax.rem(lane, per) == source).astype(bf)
        dev = lax.broadcasted_iota(jnp.int32, (feat // per, feat), 0)
        home = lax.div(lax.broadcasted_iota(jnp.int32, (feat // per, feat), 1), per)
        for r in range(3):
            spread = jnp.dot(table[:, r, :], choose, preferred_element_type=f32)
            row = jnp.sum(jnp.where(dev == home, spread, 0.0), axis=0, keepdims=True).astype(bf)
            if r == 0:
                gain[...] = row
            else:
                cents[r - 1 : r] = row
        normed, _ = layer_norm(x[...].astype(f32))
        attn_in[...] = (normed * gain[...].astype(f32)).astype(bf)

    def project(w):
        out = (queries, keys, values)[w]
        out[...] = jnp.dot(attn_in[...], matrix(w), preferred_element_type=f32).astype(bf)

    row_ids = lax.broadcasted_iota(jnp.int32, (tokens, tokens), 0)
    col_ids = lax.broadcasted_iota(jnp.int32, (tokens, tokens), 1)

    def attention():
        low_half = lax.broadcasted_iota(jnp.int32, (tokens, pair), 1) < pair // 2

        def body(h, carry):
            visible = (col_ids <= row_ids) | (col_ids < prefix[0])
            cols = pl.ds(pl.multiple_of(h * pair, pair), pair)
            q, k, v = queries[:, cols], keys[:, cols], values[:, cols]
            outs = []
            for side in (low_half, jnp.logical_not(low_half)):
                mine = jnp.where(side, q, jnp.zeros_like(q))
                s = lax.dot_general(mine, k, last_dims, preferred_element_type=f32) * scale
                s = jnp.where(visible, s, -1e30)
                top = jnp.max(s, axis=-1, keepdims=True)
                total = top + jnp.log(jnp.sum(jnp.exp(s - top), axis=-1, keepdims=True))
                p = jnp.exp(s - total).astype(bf)
                outs.append(jnp.dot(p, v, preferred_element_type=f32))
            ctx[:, cols] = jnp.where(low_half, outs[0], outs[1]).astype(bf)
            return carry

        lax.fori_loop(0, heads // 2, body, 0)
        context[...] = ctx[...]

    def dispatch():
        branch = jnp.dot(ctx[...], matrix(3), preferred_element_type=f32)
        sums[...] = jnp.broadcast_to(jnp.sum(branch * branch, axis=0, keepdims=True), sums.shape)
        hid = x[...].astype(f32) + branch
        hidden[...] = hid
        low = hid.astype(bf)
        scores = lax.dot_general(low, cents[...], last_dims, preferred_element_type=f32)
        lane = lax.broadcasted_iota(jnp.int32, scores.shape, 1)
        hot = (lane == routes[...]).astype(f32)
        g = 1.0 / (1.0 + jnp.exp(-jnp.sum(scores * hot, axis=1, keepdims=True)))
        gate[...] = g
        tri = (col_ids <= row_ids).astype(bf)
        counted = jnp.dot(tri, hot.astype(bf), preferred_element_type=f32)
        position = jnp.sum(counted * hot, axis=1, keepdims=True) - 1.0
        away = (routes[...] != ep).astype(jnp.int32)
        target = away * tokens + position.astype(jnp.int32)
        slots = lax.broadcasted_iota(jnp.int32, (tokens, 2 * tokens), 1)
        chosen = (slots == target).astype(bf)
        pick[...] = chosen
        slot_rows[...] = lax.dot_general(chosen, low, first_dims, preferred_element_type=f32).astype(bf)
        grads = (g * cotangent[...].astype(f32)).astype(bf)
        slot_grads[...] = lax.dot_general(chosen, grads, first_dims, preferred_element_type=f32).astype(bf)

    greet(others + [x_peer, y_peer, c_peer])
    order = [[8, 0, 1], [2, 3], [4, 5], [6, 7]]
    for i in order[0] + order[1]:
        z_start(i)
    for i in range(count):
        own(i).start()
    for t in range(len(order) + 3):
        if t < len(order):
            for hop in range(1, zs):
                for i in order[t]:
                    z_hop(i, hop)
            for i in order[t]:
                own(i).wait()
                second(i).start()
            if t + 2 < len(order):
                for i in order[t + 2]:
                    z_start(i)
        if 1 <= t < len(order) + 1:
            for i in order[t - 1]:
                second(i).wait_recv()
                third(i).start()

        def pass_on():
            for i in order[t - 2]:
                third(i).wait_recv()
                fourth(i).start()

        if 2 <= t < len(order) + 1:
            pass_on()
        if t >= 3:
            w = t - 3
            for i in order[w]:
                fourth(i).wait_recv()
            put_out(w).start()
            if w == 0:
                spread_extras()
            if w < 3:
                project(w)
            if w == 2:
                attention()
        if t == len(order) + 1:
            pass_on()
    dispatch()
    for w in range(4):
        put_out(w).wait()
    for i in range(count):
        z_drain(i)
        second(i).wait_send()
        third(i).wait_send()
        fourth(i).wait_send()


def front(zs, heads, shards_in, x, routes, cotangent, prefix):
    tokens, feat = x.shape
    bf, f32 = jnp.bfloat16, jnp.float32
    shape = jax.ShapeDtypeStruct
    vm = pl.BlockSpec(memory_space=pltpu.VMEM)
    hbm = pl.BlockSpec(memory_space=pl.ANY)
    n = 2 * len(shards_in) - 1
    dma = pltpu.SemaphoreType.DMA
    wholes = [(zs, 2, 2, 2) + s.shape for s in shards_in]
    shapes = [shape(s, bf) for s in wholes[:4]]
    shapes += [shape((tokens, feat), bf)] * 5
    shapes += [shape((tokens, feat), f32), shape((tokens, 1), f32), shape((tokens, 2 * tokens), bf)]
    shapes += [shape((2 * tokens, feat), bf)] * 2 + [shape((8, feat), f32), shape((1, feat), bf), shape((2, feat), bf)]
    return pl.pallas_call(
        functools.partial(front_kernel, zs, heads),
        out_shape=shapes,
        in_specs=[vm] * 8 + [pl.BlockSpec(memory_space=pltpu.SMEM)],
        out_specs=[hbm] * 4 + [vm] * 13,
        scratch_shapes=[pltpu.VMEM(s, bf) for s in wholes]
        + [
            pltpu.VMEM((tokens, feat), bf),
            dma((n,)), dma((n, 2, zs)), dma((n, 2, zs)), dma((n, 2)), dma((n, 2)), dma((n,)), dma((n,)), dma((4,)),
        ],
        compiler_params=pltpu.CompilerParams(collective_id=1, has_side_effects=True, vmem_limit_bytes=VMEM_CAP),
        name="front",
    )(*shards_in, x, routes, cotangent, prefix)


SLICES = 2
X_SLICES = 1
LEAD = 2
LAG = 3
RING = 8


def step_kernel(zs, heads, *refs):
    (x_ref, attn_in_ref, q_ref, k_ref, v_ref, context_ref, cot_ref, hidden_ref, pick_ref, wq, wk, wv, wo) = refs[0:13]
    (act_one, act_two, slope_one, slope_two, in_one, in_two, grads, rows_ref, delta, middle, up1, down1, up2, down2) = refs[13:27]
    gain, cents, gain1, gain2, gate, routes, branch_sq, sub_sq, prefix = refs[27:36]
    out_w = refs[36]
    out_a = refs[37:41]
    small_grp, small_all, result, input_grad = refs[41:45]
    pre_two, pre_one, sub_grad, row_grad, wide_far, narrow_far, attn_far, back_far, grad_far = refs[45:54]
    (send, xrecv, zrecv, acc, tiles, sides, prod, ep_in, x_in, z_in, small_in, small_ref) = refs[54:66]
    (wd, wu, sl, ps, hb, accf, midf, loadf, picks) = refs[66:75]
    (wf_s, wf_r, nf_s, nf_r, xs, xr, zsem_s, zsem_r, es, er, axs, axr, azs, azr, ss, sr, tile_sem, side_sem) = refs[75:93]
    (af_s, af_r, y_s, y_r, w_sem, ps_sem, ld_sem, out_sem, free_sem) = refs[93:]
    wide = (act_two, pre_two, act_one, pre_one)
    narrow = (grads, in_two, sub_grad, in_one)
    bf, f32 = jnp.bfloat16, jnp.float32
    z, x, core, ep = place(zs)
    tokens, feat = x_ref.shape
    rows = 2 * tokens
    hidden = act_one.shape[1]
    chunk = out_w.shape[1]
    per = prod.shape[4]
    blocks = 4 * zs
    size = chunk // SLICES
    right = device(jnp.minimum(z + 1, zs - 1), x, core, ep)
    left = device(jnp.maximum(z - 1, 0), x, core, ep)
    x_peer = device(z, 1 - x, core, ep)
    y_peer = device(z, x, core, 1 - ep)
    c_peer = device(z, x, 1 - core, ep)
    others = [device(lax.rem(z + k, zs), x, core, ep) for k in range(1, zs)]
    contract0 = (((0,), (0,)), ((), ()))
    last_dims = (((1,), (1,)), ((), ()))

    def dest(k):
        to_right = zs - 1 - z
        lower = jnp.where(k < to_right, zs - 1 - k, k - to_right)
        upper = jnp.where(k < z, k, zs - 1 - (k - z))
        return jnp.where(k < zs - 1, jnp.where(z < zs // 2, lower, upper), z)

    def begins(d):
        return ((d > z) & (z == 0)) | ((d < z) & (z == zs - 1))

    def loads(pairs, at=0):
        return [pltpu.make_async_copy(src, dst, ld_sem.at[at + i]) for i, (src, dst) in enumerate(pairs)]

    def begin(copies):
        for c in copies:
            c.start()

    def end(copies):
        for c in copies:
            c.wait()

    def fetch(pairs):
        copies = loads(pairs)
        begin(copies)
        end(copies)

    def two(slot):
        return hb.at[pl.ds(slot, 2)]

    def flat(slot):
        return hb[pl.ds(slot, 2)].reshape(rows, feat)

    greet(others + [x_peer, y_peer, c_peer])

    def far_wide(w, q):
        j = q * 2 + (1 - core)
        return push(
            wide[w].at[:, pl.ds(pl.multiple_of(j * chunk, chunk), chunk)], wide_far.at[w, q], wf_s.at[w], wf_r.at[w], c_peer
        )

    def far_narrow(w):
        return push(narrow[w], narrow_far.at[w], nf_s.at[w], nf_r.at[w], c_peer)

    def all_far(w):
        return push(wide_far.at[w], wide_far.at[w], wf_s.at[w], wf_r.at[w], c_peer)

    def send_wide(w):
        def send_far(q, carry):
            far_wide(w, q).start()
            return carry

        lax.fori_loop(0, 2 * zs, send_far, 0)

    def far_attn(i, src):
        return push(src, attn_far.at[i], af_s.at[i], af_r.at[i], c_peer)

    def far_delta():
        return push(delta.at[1], back_far, y_s.at[0], y_r.at[0], y_peer)

    def far_rows():
        return push(row_grad, grad_far, y_s.at[1], y_r.at[1], y_peer)

    far_narrow(0).start()
    send_wide(0)
    far_delta().start()
    far_narrow(1).start()
    far_narrow(3).start()
    far_attn(0, attn_in_ref).start()
    far_attn(1, context_ref).start()

    def load_tile(w, q, slot):
        j = q * 2 + core
        for i in range(4):
            @pl.when(w == i)
            def _():
                pltpu.make_async_copy(
                    wide[i].at[:, pl.ds(pl.multiple_of(j * chunk, chunk), chunk)],
                    tiles.at[slot, pl.ds(0, rows), :],
                    tile_sem.at[slot, 0],
                ).start()

        pltpu.make_async_copy(wide_far.at[w, q], tiles.at[slot, pl.ds(rows, rows), :], tile_sem.at[slot, 1]).start()

    def wait_tile(slot):
        for i in range(2):
            part = tiles.at[slot, pl.ds(i * rows, rows), :]
            pltpu.make_async_copy(part, part, tile_sem.at[slot, i]).wait()

    def load_side(w):
        slot = lax.rem(w, 2)
        for i in range(4):
            @pl.when(w == i)
            def _():
                pltpu.make_async_copy(narrow[i], sides.at[slot, pl.ds(0, 2)], side_sem.at[0]).start()

        pltpu.make_async_copy(narrow_far.at[w], sides.at[slot, pl.ds(2, 2)], side_sem.at[1]).start()

    def wait_side(w):
        slot = lax.rem(w, 2)
        for i in range(2):
            part = sides.at[slot, pl.ds(2 * i, 2)]
            pltpu.make_async_copy(part, part, side_sem.at[i]).wait()

    def product(w, slot):
        side = sides[lax.rem(w, 2)].reshape(2 * rows, feat)
        return lax.dot_general(tiles[slot], side, contract0, preferred_element_type=f32)

    def span(s):
        return pl.ds(pl.multiple_of(s * size, size), size)

    def x_copy(b, s):
        wide_size = chunk // X_SLICES
        at = pl.ds(pl.multiple_of(s * wide_size, wide_size), wide_size)
        return push(send.at[lax.rem(b, RING), at, :], xrecv.at[lax.rem(b, RING), at, :], xs.at[b, s], xr.at[b, s], x_peer)

    def z_copy(b, s):
        w = lax.div(b, zs)
        d = dest(lax.rem(b, zs))
        to_right = d > z
        nxt = jnp.where(to_right, z + 1, z - 1)
        slot = jnp.where(d != nxt, d, jnp.where(to_right, d, zs))
        return push(
            send.at[lax.rem(b, RING), span(s), :], zrecv.at[w, slot, span(s), :], zsem_s.at[b, s],
            zsem_r.at[w, slot, s], device(nxt, x, core, ep),
        )

    def z_wait(w, slot, s):
        ref = zrecv.at[w, slot, span(s), :]
        push(ref, ref, zsem_s.at[0, s], zsem_r.at[w, slot, s], x_peer).wait_recv()
        return ref[...].astype(f32)

    def z_sent(b):
        @pl.when(lax.rem(b, zs) < zs - 1)
        def _():
            for s in range(SLICES):
                z_copy(b, s).wait_send()

    def q_first(b):
        return dest(lax.rem(b, zs)) * 2 + (1 - x)

    def q_second(b):
        return dest(lax.rem(b, zs)) * 2 + x

    def far_wait(w):
        for i in range(4):
            @pl.when(w == i)
            def _():
                far_narrow(i).wait_recv()
                all_far(i).wait_recv()

    def stage_one(b):
        w = lax.div(b, zs)
        slot = lax.rem(b, 2)

        @pl.when(lax.rem(b, zs) == 0)
        def _():
            far_wait(w)
            load_side(w)
            load_tile(w, q_first(b), slot)
            wait_side(w)

        wait_tile(slot)

        @pl.when(lax.rem(b, zs) < zs - 1)
        def _():
            load_tile(w, q_first(b + 1), 1 - slot)

        @pl.when(b >= RING)
        def _():
            z_sent(b - RING)

        send[lax.rem(b, RING)] = product(w, slot).astype(bf)

    def stage_two(b):
        w = lax.div(b, zs)
        d = dest(lax.rem(b, zs))
        slot = 2 + lax.rem(b, 2)
        mine = lax.rem(b, RING)
        wait_tile(slot)

        @pl.when(b + 1 < blocks)
        def _():
            load_tile(lax.div(b + 1, zs), q_second(b + 1), 5 - slot)

        keep = lax.rem(b, LAG + 1)
        acc[keep] = product(w, slot)

        def piece(s, carry):
            sp = span(s)
            per_x = SLICES // X_SLICES

            @pl.when(lax.rem(s, per_x) == 0)
            def _():
                x_copy(b, lax.div(s, per_x)).wait()

            total = acc[keep, sp, :] + xrecv[mine, sp, :].astype(f32)
            acc[keep, sp, :] = total

            @pl.when(begins(d))
            def _():
                send[mine, sp, :] = total.astype(bf)

            return carry

        lax.fori_loop(0, SLICES, piece, 0)

        @pl.when(b < blocks - RING)
        def _():
            pl.semaphore_signal(free_sem, inc=1, device_id=x_peer, device_id_type=MESH)

        @pl.when(begins(d))
        def _():
            for s in range(SLICES):
                z_copy(b, s).start()

    def stage_three(b):
        w = lax.div(b, zs)
        d = dest(lax.rem(b, zs))
        mine = lax.rem(b, RING)
        keep = lax.rem(b, LAG + 1)

        @pl.when((d != z) & jnp.logical_not(begins(d)))
        def _():
            def piece(s, carry):
                sp = span(s)
                send[mine, sp, :] = (acc[keep, sp, :] + z_wait(w, d, s)).astype(bf)

                @pl.when(s > 0)
                def _():
                    z_copy(b, s - 1).start()

                return carry

            lax.fori_loop(0, SLICES, piece, 0)
            z_copy(b, SLICES - 1).start()

        @pl.when(d == z)
        def _():
            def piece(s, carry):
                sp = span(s)
                acc[keep, sp, :] += z_wait(w, jnp.where(z > 0, z, zs), s)

                @pl.when((z > 0) & (z < zs - 1))
                def _():
                    acc[keep, sp, :] += z_wait(w, zs, s)

                return carry

            lax.fori_loop(0, SLICES, piece, 0)
            copy = pltpu.make_async_copy(acc.at[keep], out_w.at[w], out_sem)
            copy.start()
            copy.wait()

    tile = wd.shape[1]

    def stream(source, start, count, up, down, slope, pre, low_step, high_step):
        def copies(t, slot):
            cols = pl.ds(pl.multiple_of(t * tile, tile), tile)
            return (
                pltpu.make_async_copy(down.at[0, cols, :], wd.at[slot], w_sem.at[slot, 0]),
                pltpu.make_async_copy(up.at[0, :, cols], wu.at[slot], w_sem.at[slot, 1]),
                pltpu.make_async_copy(slope.at[pl.ds(start, count), cols], sl.at[slot, pl.ds(0, count), :], w_sem.at[slot, 2]),
            )

        def out(t, slot):
            cols = pl.ds(pl.multiple_of(t * tile, tile), tile)
            return pltpu.make_async_copy(ps.at[slot, pl.ds(0, count), :], pre.at[pl.ds(start, count), cols], ps_sem.at[slot])

        for c in copies(low_step, low_step % 2):
            c.start()

        def body(t, carry):
            slot = lax.rem(t, 2)
            for c in copies(t, slot):
                c.wait()

            @pl.when(t + 1 < high_step)
            def _():
                for c in copies(t + 1, 1 - slot):
                    c.start()

            g = lax.dot_general(source(), wd[slot], last_dims, preferred_element_type=f32)
            low = (g * sl[slot, 0:count].astype(f32)).astype(bf)

            @pl.when(t >= low_step + 2)
            def _():
                out(t - 2, slot).wait()

            ps[slot, 0:count] = low
            out(t, slot).start()
            value = lax.dot_general(low, wu[slot], last_dims, preferred_element_type=f32)

            @pl.when(t == 0)
            def _():
                accf[0:count] = value

            @pl.when(t > 0)
            def _():
                accf[0:count] += value

            return carry

        lax.fori_loop(low_step, high_step, body, 0)
        for t in range(high_step - 2, high_step):
            out(t, t % 2).wait()

    part = 64

    def norm_parts_of(value, g, gain_row):
        normed, inverse = layer_norm(value)
        total = jnp.sum(g * normed, axis=0, keepdims=True)
        q = g * gain_row
        mean_q = jnp.mean(q, axis=-1, keepdims=True)
        mean_dot = jnp.mean(q * normed, axis=-1, keepdims=True)
        return total, inverse * (q - mean_q - normed * mean_dot)

    steps = hidden // tile
    part_loads = loads(
        [
            (cot_ref, hb.at[1]),
            (attn_in_ref, hb.at[0]),
            (q_ref, hb.at[12]),
            (k_ref, hb.at[13]),
            (v_ref, hb.at[14]),
            (x_ref, hb.at[11]),
            (hidden_ref, loadf.at[pl.ds(0, tokens)]),
            (pick_ref, picks),
        ]
    )
    late_loads = loads(
        [
            (delta.at[0], hb.at[3]),
            (context_ref, hb.at[2]),
            (wo.at[pl.ds(0, feat // 2)], wd.at[0]),
            (wo.at[pl.ds(feat // 2, feat // 2)], wd.at[1]),
            (back_far, hb.at[5]),
        ],
        8,
    )
    expert_loads = loads([(middle, loadf), (rows_ref, two(2))], 14)

    def event_second_start():
        fetch([(grads, two(0))])
        begin(expert_loads)
        stream(lambda: flat(0), 0, rows, up2, down2, slope_two, pre_two, 0, steps // 2)

    def event_second_end():
        stream(lambda: flat(0), 0, rows, up2, down2, slope_two, pre_two, steps // 2, steps)
        send_wide(1)
        end(expert_loads)
        small_ref[...] = jnp.zeros_like(small_ref)
        gain_row = gain2[...].astype(f32)
        per_block = tokens // part

        def body(i, carry):
            at = pl.ds(pl.multiple_of(i * part, part), part)
            total, value = norm_parts_of(loadf[at], accf[at], gain_row)
            small_ref[1:2] += total
            midf[at] = value
            blk = lax.div(i, per_block)
            sub = pl.ds(pl.multiple_of(lax.rem(i, per_block) * part, part), part)
            hb[4 + blk, sub] = (hb[blk, sub].astype(f32) + value).astype(bf)
            return carry

        lax.fori_loop(0, rows // part, body, 0)
        fetch([(two(4), sub_grad)])
        far_narrow(2).start()
        send_wide(2)
        begin(part_loads)

    def first_stream(blk, low_step, high_step):
        start = blk * tokens
        stream(lambda: hb[4 + blk], start, tokens, up1, down1, slope_one, pre_one, low_step, high_step)

    def first_norm(blk):
        gain_row = gain1[...].astype(f32)

        def body(i, carry):
            at = pl.ds(pl.multiple_of(i * part, part), part)
            value = hb[2 + blk, at].astype(f32)
            total, back = norm_parts_of(value, accf[at], gain_row)
            small_ref[0:1] += total
            mid = midf[pl.ds(pl.multiple_of(blk * tokens + i * part, part), part)]
            hb[6 + blk, at] = (back + mid).astype(bf)
            return carry

        lax.fori_loop(0, tokens // part, body, 0)

    def event_far_start():
        first_stream(1, 0, steps // 2)

    def event_far_end():
        first_stream(1, steps // 2, steps)
        first_norm(1)
        fetch_out = pltpu.make_async_copy(hb.at[7], row_grad, out_sem)
        fetch_out.start()
        fetch_out.wait()
        far_rows().start()

    def event_own_start():
        first_stream(0, 0, steps // 2)

    def event_own_end():
        first_stream(0, steps // 2, steps)
        first_norm(0)
        send_wide(3)
        far_delta().wait_recv()
        begin(late_loads)

    half = feat // 2

    def event_combine():
        far_rows().wait_recv()
        row_load = pltpu.make_async_copy(grad_far, hb.at[9], out_sem)
        row_load.start()
        end(part_loads)
        end(late_loads)
        row_load.wait()
        c = cents[...].astype(f32)

        def combine(i, carry):
            at = pl.ds(pl.multiple_of(i * part, part), part)
            own = picks[at, 0:tokens]
            far = picks[at, tokens : 2 * tokens]
            returned = jnp.dot(own, hb[3], preferred_element_type=f32) + jnp.dot(far, hb[5], preferred_element_type=f32)
            back = jnp.dot(own, hb[6], preferred_element_type=f32) + jnp.dot(far, hb[9], preferred_element_type=f32)
            g = gate[at]
            hid = loadf[at]
            res = hid + g * returned
            hb[15, at] = res.astype(bf)
            small_ref[5:6] += jnp.sum(res * res, axis=0, keepdims=True)
            grad_out = hb[1, at].astype(f32)
            grad_score = jnp.sum(grad_out * returned, axis=1, keepdims=True) * g * (1.0 - g)
            is_first = routes[at] == 0
            weighted = grad_score * hid.astype(bf).astype(f32)
            zero = jnp.zeros_like(weighted)
            small_ref[3:4] += jnp.sum(jnp.where(is_first, weighted, zero), axis=0, keepdims=True)
            small_ref[4:5] += jnp.sum(jnp.where(is_first, zero, weighted), axis=0, keepdims=True)
            grad_hidden = grad_out + grad_score * jnp.where(is_first, c[0:1], c[1:2]) + back
            midf[at] = grad_hidden
            hb[10, at] = grad_hidden.astype(bf)
            return carry

        lax.fori_loop(0, tokens // part, combine, 0)
        fetch([(hb.at[15], result)])
        for i in range(2):
            hb[15, :, i * half : (i + 1) * half] = lax.dot_general(
                hb[10], wd[i], last_dims, preferred_element_type=f32
            ).astype(bf)

    def event_heads(low_pair, high_pair):
        row_ids = lax.broadcasted_iota(jnp.int32, (tokens, tokens), 0)
        col_ids = lax.broadcasted_iota(jnp.int32, (tokens, tokens), 1)
        pair = 2 * feat // heads
        scale = (feat // heads) ** -0.5
        limit = prefix[...]

        def head(h, carry):
            visible = (col_ids <= row_ids) | (col_ids < limit)
            low_half = lax.broadcasted_iota(jnp.int32, (tokens, pair), 1) < pair // 2
            cols = pl.ds(pl.multiple_of(h * pair, pair), pair)
            q, k, v, gc = hb[12, :, cols], hb[13, :, cols], hb[14, :, cols], hb[15, :, cols]
            outs = []
            for side in (low_half, jnp.logical_not(low_half)):
                s = lax.dot_general(jnp.where(side, q, jnp.zeros_like(q)), k, last_dims, preferred_element_type=f32) * scale
                s = jnp.where(visible, s, -1e30)
                top = jnp.max(s, axis=-1, keepdims=True)
                total = top + jnp.log(jnp.sum(jnp.exp(s - top), axis=-1, keepdims=True))
                p = jnp.exp(s - total)
                gp = lax.dot_general(jnp.where(side, gc, jnp.zeros_like(gc)), v, last_dims, preferred_element_type=f32)
                dot = jnp.sum(gp * p, axis=-1, keepdims=True)
                gs = (p * (gp - dot)).astype(bf)
                outs.append(
                    (
                        jnp.dot(gs, k, preferred_element_type=f32),
                        lax.dot_general(gs, q, contract0, preferred_element_type=f32),
                        lax.dot_general(p.astype(bf), gc, contract0, preferred_element_type=f32),
                    )
                )
            hb[4, :, cols] = (jnp.where(low_half, outs[0][0], outs[1][0]) * scale).astype(bf)
            hb[6, :, cols] = (jnp.where(low_half, outs[0][1], outs[1][1]) * scale).astype(bf)
            hb[8, :, cols] = jnp.where(low_half, outs[0][2], outs[1][2]).astype(bf)
            return carry

        lax.fori_loop(low_pair, high_pair, head, 0)

    def event_inputs():
        order = [(m, i) for i in range(2) for m in (wq, wk, wv)]

        def weight_copy(n):
            m, i = order[n]
            return pltpu.make_async_copy(m.at[pl.ds(i * half, half)], wd.at[n % 2], w_sem.at[n % 2, 0])

        weight_copy(0).start()
        for n in range(6):
            weight_copy(n).wait()
            if n < 5:
                weight_copy(n + 1).start()
            value = lax.dot_general(hb[4 + 2 * (n % 3)], wd[n % 2], last_dims, preferred_element_type=f32)
            cols = slice((n // 3) * half, (n // 3 + 1) * half)
            if n % 3 == 0:
                accf[0:tokens, cols] = value
            else:
                accf[0:tokens, cols] += value
        for i in range(4):
            far_attn(2 + i, hb.at[4 + 2 * i]).start()
        gain_row = gain[...].astype(f32)

        def norms(i, carry):
            at = pl.ds(pl.multiple_of(i * part, part), part)
            total, value = norm_parts_of(hb[11, at].astype(f32), accf[at], gain_row)
            small_ref[2:3] += total
            midf[at] += value
            return carry

        lax.fori_loop(0, tokens // part, norms, 0)
        small_ref[6:7] = branch_sq[0:1]
        small_ref[7:9] = sub_sq[0:2]
        start0()

    def event_products():
        for i in range(6):
            far_attn(i, hb.at[0]).wait_recv()
        fetch(
            [(midf.at[pl.ds(0, tokens)], input_grad)]
            + [(attn_far.at[i], hb.at[2 * i + 1]) for i in range(6)]
        )
        step = 8 * per

        for w in range(4):
            lhs = 0 if w < 3 else 2
            rhs = 4 + 2 * w

            def form(m, carry):
                cols = pl.ds(pl.multiple_of(m * step, step), step)
                left_part = hb[pl.ds(lhs, 2), :, cols].reshape(rows, step)
                value = lax.dot_general(left_part, flat(rhs), contract0, preferred_element_type=f32)
                value = value.astype(bf).reshape(2, 2, 2 * per, feat)
                mine = jnp.where(core == 0, value[:, 0], value[:, 1])
                prod[w, m] = mine.reshape(2, 2, per, feat)
                return carry

            lax.fori_loop(0, zs, form, 0)
            if w > 0:
                attn_ep(w - 1).start()
        for i in range(6):
            far_attn(i, hb.at[0]).wait_send()
        attn_ep(3).start()

    def attn_ep(w):
        return push(prod.at[w, :, :, 1 - ep], ep_in.at[w], es.at[w], er.at[w], y_peer)

    def attn_x(w):
        return push(prod.at[w, z, 1 - x, ep], x_in.at[w], axs.at[w], axr.at[w], x_peer)

    def fold_ep(w):
        attn_ep(w).wait()

        def body(m, carry):
            for i in range(2):
                total = prod[w, m, i, ep].astype(f32) + ep_in[w, m, i].astype(f32)
                prod[w, m, i, ep] = total.astype(bf)
            return carry

        lax.fori_loop(0, zs, body, 0)

    def attn_z_copy(w, k):
        d = dest(k)
        to_right = d > z
        nxt = jnp.where(to_right, z + 1, z - 1)
        slot = jnp.where(d != nxt, d, jnp.where(to_right, d, zs))
        return push(prod.at[w, d, :, ep], z_in.at[w, slot], azs.at[w, k], azr.at[w, slot], device(nxt, x, core, ep))

    def attn_z_wait(w, slot):
        ref = z_in.at[w, slot]
        push(ref, ref, azs.at[w, 0], azr.at[w, slot], x_peer).wait_recv()

    def begin_z(w):
        def body(k, carry):
            @pl.when(begins(dest(k)))
            def _():
                attn_z_copy(w, k).start()

            return carry

        lax.fori_loop(0, zs - 1, body, 0)

    def forward_z(w):
        def body(k, carry):
            d = dest(k)

            @pl.when(jnp.logical_not(begins(d)))
            def _():
                attn_z_wait(w, d)
                for i in range(2):
                    prod[w, d, i, ep] = (prod[w, d, i, ep].astype(f32) + z_in[w, d, i].astype(f32)).astype(bf)
                attn_z_copy(w, k).start()

            return carry

        lax.fori_loop(0, zs - 1, body, 0)

    def own_z(w):
        first = jnp.where(z > 0, z, zs)
        attn_z_wait(w, first)
        for i in range(2):
            prod[w, z, i, ep] = (prod[w, z, i, ep].astype(f32) + z_in[w, first, i].astype(f32)).astype(bf)

        @pl.when((z > 0) & (z < zs - 1))
        def _():
            attn_z_wait(w, zs)
            for i in range(2):
                prod[w, z, i, ep] = (prod[w, z, i, ep].astype(f32) + z_in[w, zs, i].astype(f32)).astype(bf)

        attn_x(w).start()

    def last_x(w):
        attn_x(w).wait()
        out_a[w][...] = prod[w, z, x, ep].astype(f32) + x_in[w].astype(f32)
        for k in range(zs - 1):
            attn_z_copy(w, k).wait_send()

    def small_stage(stage, n, mine, peer_at, src):
        def copy(k):
            return push(src, small_in.at[stage, mine], ss.at[stage, k], sr.at[stage, k], peer_at(lax.rem(mine + k, n)))

        def start():
            for k in range(1, n):
                copy(k).start()

        def end():
            for k in range(1, n):
                copy(k).wait()
            small_in[stage, mine] = src[...]
            total = small_in[stage, 0]
            for i in range(1, n):
                total = total + small_in[stage, i]
            return total

        return start, end

    start0, end0 = small_stage(0, 2, core, lambda i: device(z, x, i, ep), small_ref)
    start1, end1 = small_stage(1, 2, x, lambda i: device(z, i, core, ep), small_in.at[3, 3])
    start2, end2 = small_stage(2, zs, z, lambda i: device(i, x, core, ep), small_in.at[3, 2])
    start3, end3 = small_stage(3, 2, ep, lambda i: device(z, x, core, i), small_grp)

    def event_x(w):
        def act():
            fold_ep(w)
            begin_z(w)

        return act

    def event_small1():
        small_in[3, 3] = end0()
        start1()

    def event_small2():
        small_in[3, 2] = end1()
        start2()

    def event_small3():
        small_grp[...] = end2()
        start3()

    def event_z(w):
        def act():
            forward_z(w)

        return act

    def event_own(w):
        def act():
            own_z(w)

        return act

    def event_last():
        for w in range(4):
            last_x(w)
        small_all[...] = end3()

    pairs = heads // 2
    steps_at = [
        (1, event_second_start),
        (2, event_second_end),
        (3, event_far_start),
        (4, event_far_end),
        (5, event_own_start),
        (6, event_own_end),
        (7, event_combine),
        (8, lambda: event_heads(0, pairs // 2)),
        (9, lambda: event_heads(pairs // 2, pairs)),
        (10, event_inputs),
        (11, event_products),
        (11, event_small1),
        (12, event_small2),
        (13, event_small3),
    ]
    steps_at += [(12 + w, event_x(w)) for w in range(4)]
    steps_at += [(13 + w, event_z(w)) for w in range(4)]
    steps_at += [(15 + w, event_own(w)) for w in range(4)]

    def pipeline(t, carry):
        @pl.when(t < blocks)
        def _():
            stage_one(t)

        @pl.when((t > 0) & (t <= blocks))
        def _():
            @pl.when(t - 1 >= RING)
            def _():
                pl.semaphore_wait(free_sem, 1)

            for s in range(X_SLICES):
                x_copy(t - 1, s).start()

        for at, action in steps_at:
            pl.when(t == at)(action)

        @pl.when(t == LEAD - 1)
        def _():
            load_tile(0, q_second(0), 2)

        @pl.when((t >= LEAD) & (t < blocks + LEAD))
        def _():
            stage_two(t - LEAD)

        late = t - LEAD - jnp.where((z == 0) | (z == zs - 1), LAG, LAG - 1)

        @pl.when((late >= 0) & (late < blocks))
        def _():
            stage_three(late)

        return carry

    lax.fori_loop(0, blocks + LEAD + LAG, pipeline, 0)
    event_last()

    def drain(b, carry):
        z_sent(b)
        return carry

    lax.fori_loop(blocks - RING, blocks, drain, 0)
    for w in range(4):
        far_narrow(w).wait_send()
        all_far(w).wait_send()
    far_delta().wait_send()
    far_rows().wait_send()


def backward_step(zs, heads, big, experts, little, prefix):
    x, hidden = big[0], experts[0].shape[1]
    tokens, feat = x.shape
    rows = 2 * tokens
    chunk = hidden // (4 * zs)
    per = feat // (8 * zs)
    f32, bf = jnp.float32, jnp.bfloat16
    shape = jax.ShapeDtypeStruct
    vm = pl.BlockSpec(memory_space=pltpu.VMEM)
    hbm = pl.BlockSpec(memory_space=pl.ANY)
    dma = pltpu.SemaphoreType.DMA
    outs = [shape((4, chunk, feat), f32)]
    outs += [shape((per, feat), f32)] * 4
    outs += [shape((16, feat), f32)] * 2
    outs += [shape((tokens, feat), bf), shape((tokens, feat), f32)]
    outs += [shape((rows, hidden), bf)] * 2 + [shape((2, tokens, feat), bf), shape((tokens, feat), bf)]
    outs += [shape((4, 2 * zs, rows, chunk), bf), shape((4, 2, tokens, feat), bf), shape((6, tokens, feat), bf)]
    outs += [shape((tokens, feat), bf)] * 2
    s = SLICES
    blocks = 4 * zs
    tile = 512
    vmem = pltpu.VMEM
    return pl.pallas_call(
        functools.partial(step_kernel, zs, heads),
        out_shape=outs,
        in_specs=[hbm] * 27 + [vm] * 9,
        out_specs=[hbm] + [vm] * 6 + [hbm] * 11,
        scratch_shapes=[
            vmem((RING, chunk, feat), bf),
            vmem((RING, chunk, feat), bf),
            vmem((4, zs + 1, chunk, feat), bf),
            vmem((LAG + 1, chunk, feat), f32),
            vmem((4, 2 * rows, chunk), bf),
            vmem((2, 4, tokens, feat), bf),
            vmem((4, zs, 2, 2, per, feat), bf),
            vmem((4, zs, 2, per, feat), bf),
            vmem((4, per, feat), bf),
            vmem((4, zs + 1, 2, per, feat), bf),
            vmem((4, max(zs, 4), 16, feat), f32),
            vmem((16, feat), f32),
            vmem((2, tile, feat), bf),
            vmem((2, feat, tile), bf),
            vmem((2, rows, tile), bf),
            vmem((2, rows, tile), bf),
            vmem((16, tokens, feat), bf),
            vmem((rows, feat), f32),
            vmem((rows, feat), f32),
            vmem((rows, feat), f32),
            vmem((tokens, rows), bf),
            dma((4,)), dma((4,)), dma((4,)), dma((4,)),
            dma((blocks, s)), dma((blocks, s)), dma((blocks, s)), dma((4, zs + 1, s)),
            dma((4,)), dma((4,)), dma((4,)), dma((4,)), dma((4, zs)), dma((4, zs + 1)),
            dma((4, zs)), dma((4, zs)), dma((4, 2)), dma((2,)),
            dma((6,)), dma((6,)), dma((2,)), dma((2,)), dma((2, 3)), dma((2,)), dma((16,)), dma, pltpu.SemaphoreType.REGULAR,
        ],
        compiler_params=pltpu.CompilerParams(collective_id=2, has_side_effects=True, vmem_limit_bytes=VMEM_CAP),
        name="backward_step",
    )(*big, *experts, *little, prefix)


def shards(
    inputs,
    attn_gain,
    w_query,
    w_key,
    w_value,
    w_output,
    centroids,
    norm1_gain,
    norm2_gain,
    up_first,
    down_first,
    up_second,
    down_second,
    routes,
    prefix,
    cotangent,
):
    gathered = (
        lax.all_gather(attn_gain, ("grp", "ep"), axis=0, tiled=True),
        lax.all_gather(w_query, ("grp", "ep"), axis=0, tiled=True),
        lax.all_gather(w_key, ("grp", "ep"), axis=0, tiled=True),
        lax.all_gather(w_value, ("grp", "ep"), axis=0, tiled=True),
        lax.all_gather(w_output, ("grp", "ep"), axis=0, tiled=True),
        lax.all_gather(centroids, ("grp", "ep"), axis=0, tiled=True),
    )
    gain_attn, query_mat, key_mat, value_mat, output_mat, centroid_mat = gathered
    token_count, feature_width = inputs.shape
    head_count = HEADS
    head_width = feature_width // head_count
    scale_factor = head_width ** (-0.5)
    block_rows = min(512, token_count)
    prefix_len = prefix[0]
    inputs_wide = inputs.astype(jnp.float32)
    normed_attn, inverse_attn = norm_parts(inputs_wide)
    gain_attn_wide = gain_attn.astype(jnp.float32)
    attn_in = (normed_attn * gain_attn_wide).astype(jnp.bfloat16)
    queries = (
        matmul(attn_in, query_mat).astype(jnp.bfloat16).reshape(token_count, head_count, head_width)
    )
    key_heads = (
        matmul(attn_in, key_mat).astype(jnp.bfloat16).reshape(token_count, head_count, head_width)
    )
    value_heads = (
        matmul(attn_in, value_mat).astype(jnp.bfloat16).reshape(token_count, head_count, head_width)
    )

    def block_scores(block_index):
        row_start = block_index * block_rows
        scores = (
            jnp.einsum("qhd,khd->hqk", queries, key_heads, preferred_element_type=jnp.float32)
            * scale_factor
        )
        visible = visible_mask(row_start, block_rows, token_count, prefix_len)
        return (queries, jnp.where(visible[None], scores, -1e30))

    block_index = 0
    query_block, scores = block_scores(block_index)
    row_max = jnp.max(scores, axis=-1, keepdims=True)
    expsum = jnp.sum(jnp.exp(scores - row_max), axis=-1, keepdims=True)
    log_total = row_max + jnp.log(expsum)
    probs_low = jnp.exp(scores - log_total).astype(jnp.bfloat16)
    context_parts = jnp.einsum(
        "hqk,khd->qhd", probs_low, value_heads, preferred_element_type=jnp.float32
    ).astype(jnp.bfloat16)
    lse_parts = [log_total]
    context = context_parts.reshape(token_count, feature_width)
    branch = matmul(context, output_mat)
    hidden = inputs_wide + branch
    hidden_low = hidden.astype(jnp.bfloat16)
    expert_total = lax.axis_size("ep")
    group_total = lax.axis_size("grp")
    capacity = 2 * token_count // expert_total
    route_ids = routes[:, 0]
    expert_ids = jnp.arange(expert_total, dtype=jnp.int32)
    route_hot = (route_ids[:, None] == expert_ids[None, :]).astype(jnp.int32)
    position = jnp.sum((jnp.cumsum(route_hot, axis=0) - 1) * route_hot, axis=1)
    target = route_ids * capacity + position
    route_weight = route_hot.astype(jnp.float32)
    all_scores = matmul(hidden_low, centroid_mat)
    gate_value = jax.nn.sigmoid(jnp.sum(all_scores * route_weight, axis=1))
    slot_rows = fill_slots(hidden_low, target, expert_total * capacity).reshape(
        expert_total, capacity, feature_width
    )
    received = lax.all_to_all(slot_rows, "ep", split_axis=0, concat_axis=0, tiled=True).reshape(
        expert_total * capacity, feature_width
    )
    gain_one = norm1_gain[0].astype(jnp.float32)
    gain_two = norm2_gain[0].astype(jnp.float32)
    up_one = up_first[0]
    down_one = down_first[0]
    up_two = up_second[0]
    down_two = down_second[0]
    rows_wide = received.astype(jnp.float32)
    normed_one, inverse_one = norm_parts(rows_wide)
    in_one = (normed_one * gain_one).astype(jnp.bfloat16)
    pre_one = matmul(in_one, up_one)
    act_one = jax.nn.gelu(pre_one, approximate=False).astype(jnp.bfloat16)
    sub_one = matmul(act_one, down_one)
    middle = rows_wide + sub_one
    normed_two, inverse_two = norm_parts(middle)
    in_two = (normed_two * gain_two).astype(jnp.bfloat16)
    pre_two = matmul(in_two, up_two)
    act_two = jax.nn.gelu(pre_two, approximate=False).astype(jnp.bfloat16)
    sub_two = matmul(act_two, down_two)
    delta = (sub_one + sub_two).astype(jnp.bfloat16).reshape(expert_total, capacity, feature_width)
    back_slots = lax.all_to_all(delta, "ep", split_axis=0, concat_axis=0, tiled=True).reshape(
        expert_total * capacity, feature_width
    )
    returned = back_slots[target].astype(jnp.float32)
    result = hidden + gate_value[:, None] * returned
    square_terms = jnp.stack(
        [
            jnp.sum(result * result),
            jnp.sum(branch * branch),
            jnp.sum(sub_one * sub_one),
            jnp.sum(sub_two * sub_two),
        ]
    )
    square_totals = lax.psum(square_terms, ("grp", "ep"))
    cell_count = float(token_count * feature_width * group_total * expert_total)
    rms_values = jnp.sqrt(square_totals / cell_count)
    grad_out = cotangent.astype(jnp.float32)
    grad_gate = jnp.sum(grad_out * returned, axis=1)
    grad_score = grad_gate * gate_value * (1.0 - gate_value)
    grad_delta_tok = (gate_value[:, None] * grad_out).astype(jnp.bfloat16)
    grad_slots = fill_slots(grad_delta_tok, target, expert_total * capacity).reshape(
        expert_total, capacity, feature_width
    )
    grad_sum = lax.all_to_all(grad_slots, "ep", split_axis=0, concat_axis=0, tiled=True).reshape(
        expert_total * capacity, feature_width
    )
    grad_pre_two = (dot_last(grad_sum, down_two) * gelu_slope(pre_two)).astype(jnp.bfloat16)
    grad_in_two = dot_last(grad_pre_two, up_two)
    grad_gain_two = jnp.sum(grad_in_two * normed_two, axis=0)
    grad_middle = norm_back(grad_in_two * gain_two, normed_two, inverse_two)
    grad_sub_one = (grad_sum.astype(jnp.float32) + grad_middle).astype(jnp.bfloat16)
    grad_pre_one = (dot_last(grad_sub_one, down_one) * gelu_slope(pre_one)).astype(jnp.bfloat16)
    grad_in_one = dot_last(grad_pre_one, up_one)
    grad_gain_one = jnp.sum(grad_in_one * normed_one, axis=0)
    grad_rows = (norm_back(grad_in_one * gain_one, normed_one, inverse_one) + grad_middle).astype(
        jnp.bfloat16
    )
    grad_back = lax.all_to_all(
        grad_rows.reshape(expert_total, capacity, feature_width),
        "ep",
        split_axis=0,
        concat_axis=0,
        tiled=True,
    ).reshape(expert_total * capacity, feature_width)
    grad_down_two = dot_first(act_two, grad_sum)
    grad_up_two = dot_first(in_two, grad_pre_two)
    grad_down_one = dot_first(act_one, grad_sub_one)
    grad_up_one = dot_first(in_one, grad_pre_one)
    expert_sums = (
        lax.psum_scatter(grad_up_one[None], "grp", scatter_dimension=2, tiled=True),
        lax.psum_scatter(grad_down_one[None], "grp", scatter_dimension=1, tiled=True),
        lax.psum_scatter(grad_up_two[None], "grp", scatter_dimension=2, tiled=True),
        lax.psum_scatter(grad_down_two[None], "grp", scatter_dimension=1, tiled=True),
        lax.psum_scatter(grad_gain_one[None], "grp", scatter_dimension=1, tiled=True),
        lax.psum_scatter(grad_gain_two[None], "grp", scatter_dimension=1, tiled=True),
    )
    up_one_sum, down_one_sum, up_two_sum, down_two_sum, gain_one_sum, gain_two_sum = expert_sums
    centroid_wide = centroid_mat.astype(jnp.float32)
    score_weight = route_weight * grad_score[:, None]
    grad_hidden = (
        grad_out
        + jnp.dot(score_weight, centroid_wide.T, precision=HIGH)
        + grad_back[target].astype(jnp.float32)
    )
    grad_centroid = lax.dot_general(
        hidden_low.astype(jnp.float32), score_weight, (((0,), (0,)), ((), ())), precision=HIGH
    )
    grad_branch = grad_hidden.astype(jnp.bfloat16)
    grad_output_mat = dot_first(context, grad_branch)
    grad_context = (
        dot_last(grad_branch, output_mat)
        .astype(jnp.bfloat16)
        .reshape(token_count, head_count, head_width)
    )
    block_index = 0
    query_block, scores = block_scores(block_index)
    probs_wide = jnp.exp(scores - lse_parts[block_index])
    probs_low = probs_wide.astype(jnp.bfloat16)
    row_start = block_index * block_rows
    grad_value_sum = jnp.einsum(
        "hqk,qhd->khd", probs_low, grad_context, preferred_element_type=jnp.float32
    )
    grad_probs = jnp.einsum(
        "qhd,khd->hqk", grad_context, value_heads, preferred_element_type=jnp.float32
    )
    row_dot = jnp.sum(grad_probs * probs_wide, axis=-1, keepdims=True)
    grad_scores = (probs_wide * (grad_probs - row_dot)).astype(jnp.bfloat16)
    grad_query_parts = (
        jnp.einsum("hqk,khd->qhd", grad_scores, key_heads, preferred_element_type=jnp.float32)
        * scale_factor
    ).astype(jnp.bfloat16)
    grad_key_sum = (
        jnp.einsum("hqk,qhd->khd", grad_scores, query_block, preferred_element_type=jnp.float32)
        * scale_factor
    )
    grad_queries = grad_query_parts.reshape(token_count, feature_width)
    grad_keys = grad_key_sum.astype(jnp.bfloat16).reshape(token_count, feature_width)
    grad_values = grad_value_sum.astype(jnp.bfloat16).reshape(token_count, feature_width)
    grad_query_mat = dot_first(attn_in, grad_queries)
    grad_key_mat = dot_first(attn_in, grad_keys)
    grad_value_mat = dot_first(attn_in, grad_values)
    grad_attn_in = (
        dot_last(grad_queries, query_mat)
        + dot_last(grad_keys, key_mat)
        + dot_last(grad_values, value_mat)
    )
    grad_gain_attn = jnp.sum(grad_attn_in * normed_attn, axis=0)
    input_grad = grad_hidden + norm_back(grad_attn_in * gain_attn_wide, normed_attn, inverse_attn)
    attn_terms = (
        grad_gain_attn,
        grad_query_mat,
        grad_key_mat,
        grad_value_mat,
        grad_output_mat,
        grad_centroid,
    )
    outer_sums = (
        lax.psum_scatter(attn_terms[0], "grp", scatter_dimension=0, tiled=True),
        lax.psum_scatter(attn_terms[1], "grp", scatter_dimension=0, tiled=True),
        lax.psum_scatter(attn_terms[2], "grp", scatter_dimension=0, tiled=True),
        lax.psum_scatter(attn_terms[3], "grp", scatter_dimension=0, tiled=True),
        lax.psum_scatter(attn_terms[4], "grp", scatter_dimension=0, tiled=True),
        lax.psum_scatter(attn_terms[5], "grp", scatter_dimension=0, tiled=True),
    )
    attn_sums = (
        lax.psum_scatter(outer_sums[0], "ep", scatter_dimension=0, tiled=True),
        lax.psum_scatter(outer_sums[1], "ep", scatter_dimension=0, tiled=True),
        lax.psum_scatter(outer_sums[2], "ep", scatter_dimension=0, tiled=True),
        lax.psum_scatter(outer_sums[3], "ep", scatter_dimension=0, tiled=True),
        lax.psum_scatter(outer_sums[4], "ep", scatter_dimension=0, tiled=True),
        lax.psum_scatter(outer_sums[5], "ep", scatter_dimension=0, tiled=True),
    )
    return (
        result.astype(jnp.bfloat16),
        input_grad,
        attn_sums[0],
        attn_sums[1],
        attn_sums[2],
        attn_sums[3],
        attn_sums[4],
        attn_sums[5],
        gain_one_sum,
        gain_two_sum,
        up_one_sum,
        down_one_sum,
        up_two_sum,
        down_two_sum,
        rms_values,
    )


def fast_shards(
    inputs,
    attn_gain,
    w_query,
    w_key,
    w_value,
    w_output,
    centroids,
    norm1_gain,
    norm2_gain,
    up_first,
    down_first,
    up_second,
    down_second,
    routes,
    prefix,
    cotangent,
):
    zs = lax.axis_size("grp") // 4
    group_total = lax.axis_size("grp")
    ep_size = lax.axis_size("ep")
    per = w_query.shape[0]
    tokens, width = inputs.shape
    extra = jnp.concatenate([attn_gain[None, :], centroids.T], axis=0)
    extra = jnp.pad(extra, ((0, 16 - extra.shape[0]), (0, 128 - per)))
    made = front(zs, HEADS, [w_query, w_key, w_value, w_output, extra], inputs, routes, cotangent, prefix)
    mats = [f.reshape(width, width) for f in made[:4]]
    attn_in, queries, keys, values, context, hidden, gate, pick, slot_rows, slot_grads, branch_sq, gain, cents = made[4:]
    gain1, gain2 = norm1_gain, norm2_gain
    weights = (up_first, down_first, up_second, down_second)
    in_one, in_two, act_one, slope_one, act_two, slope_two, middle, delta, sub_sq, rows, grads = expert_forward(
        slot_rows.reshape(2, tokens, width), slot_grads.reshape(2, tokens, width), gain1, gain2, *weights
    )
    pieces = lambda a: a.reshape(ep_size, tokens, width)
    reduced = backward_step(
        zs,
        HEADS,
        [inputs, attn_in, queries, keys, values, context, cotangent, hidden, pick, *mats],
        [act_one, act_two, slope_one, slope_two, pieces(in_one), pieces(in_two), grads, rows,
         pieces(delta), middle, *weights],
        [gain, cents, gain1, gain2, gate, routes, branch_sq, sub_sq],
        prefix.reshape(1, 1),
    )
    result, input_grad = reduced[7:9]
    down_two_sum, up_two_sum, down_one_sum, up_one_sum = (reduced[0][i] for i in range(4))
    query_sum, key_sum, value_sum, output_sum = reduced[1:5]
    grp_sum, all_sum = reduced[5], reduced[6]
    grp_at = lax.axis_index("grp") * (width // group_total)
    all_at = (lax.axis_index("grp") * ep_size + lax.axis_index("ep")) * per
    gains = lax.dynamic_slice(grp_sum, (0, grp_at), (2, width // group_total))
    outer = lax.dynamic_slice(all_sum, (0, all_at), (5, per))
    cell_count = float(tokens * width * group_total * ep_size)
    rms_values = jnp.sqrt(jnp.sum(all_sum[5:9], axis=1) / cell_count)
    return (
        result,
        input_grad,
        outer[2],
        query_sum,
        key_sum,
        value_sum,
        output_sum,
        outer[3:5].T,
        gains[0:1],
        gains[1:2],
        up_one_sum.T[None],
        down_one_sum[None],
        up_two_sum.T[None],
        down_two_sum[None],
        rms_values,
    )


def solution(mesh):
    fast = mesh.shape["ep"] == 2 and mesh.shape["grp"] == 16
    in_specs = (
        P(("grp", "ep"), None),
        P(("grp", "ep")),
        P(("grp", "ep"), None),
        P(("grp", "ep"), None),
        P(("grp", "ep"), None),
        P(("grp", "ep"), None),
        P(("grp", "ep"), None),
        P("ep", None),
        P("ep", None),
        P("ep", None, None),
        P("ep", None, None),
        P("ep", None, None),
        P("ep", None, None),
        P(("grp", "ep"), None),
        P(("grp", "ep")),
        P(("grp", "ep"), None),
    )
    out_specs = (
        P(("grp", "ep"), None),
        P(("grp", "ep"), None),
        P(("grp", "ep")),
        P(("grp", "ep"), None),
        P(("grp", "ep"), None),
        P(("grp", "ep"), None),
        P(("grp", "ep"), None),
        P(("grp", "ep"), None),
        P("ep", "grp"),
        P("ep", "grp"),
        P("ep", None, "grp"),
        P("ep", "grp", None),
        P("ep", None, "grp"),
        P("ep", "grp", None),
        P(),
    )
    return jax.shard_map(fast_shards if fast else shards, mesh=mesh, in_specs=in_specs, out_specs=out_specs, check_vma=False)
```
